512 devices in a mesh: tile: 32 (over z_lo, x), ens: 16 (over z_hi, y, core).
Axes of the slice: x: 4, y: 4, z: 16 (z_hi: 2, z_lo: 8; z = z_hi * 8 + z_lo), core: 2. Of those that a mesh axis runs over, the one named last changes fastest.
Arguments:
- features: bfloat16 [16, 32, 16, 16, 256], P('ens', 'tile'), may hold values from -6 to 6
- cotangent: bfloat16 [16, 32, 16, 16, 256], P('ens', 'tile'), may hold values from -6 to 6
- kernel: float32 [49, 256], replicated, may hold values from -0.875 to 0.875
- weight_in: bfloat16 [256, 1024], replicated, may hold values from -0.375 to 0.375
- weight_out: bfloat16 [1024, 256], replicated, may hold values from -0.1875 to 0.1875
- tile_neighbour: int32 [32, 4], P('tile'), may hold values from 0 to 31, as said below
- edge_code: int32 [32, 4], P('tile'), may hold values from 0 to 7, as said below
Outputs:
- grad_features: bfloat16 [16, 32, 16, 16, 256], P('ens', 'tile')
- grad_kernel: float32 [49, 256], replicated
- grad_weight_in: float32 [256, 1024], replicated
- grad_weight_out: float32 [1024, 256], replicated
The draws below stay inside these ranges and needn't reach their ends.
Inputs may be any that keep to these rules, and one draw needn't show every extreme that they name: `tile_neighbour`: tile t is held by index t // 1 of tile; every neighbour of tile t is held by that same index, the one before it or the one after it, cyclically. edge_code % 4 names the neighbour's edge (0 top, 1 bottom, 2 left, 3 right); 4 or more means reversed along the edge.
All inputs are finite; a program needn't handle non-finite values.
Results may differ from the reference program's by a relative error of at most 0.015.
Values may be sent and summed in bfloat16 or wider, within the bound.
A program may use at most 64 MiB of HBM per device.

```python
import math
import jax
import jax.numpy as jnp
from jax import lax

C = 256
HID = 1024
KERNEL_TAPS = 7
DILATION_STEP = 2
HALO = 6
TILE = 16
TPD = 1
MEMBERS = 16
TILES = 32


def draw_tile_neighbour(key, part):
    first_key, second_key = jax.random.split(jax.random.fold_in(key, 11))
    owners = TILES // TPD
    tile_ids = jnp.arange(TILES, dtype=jnp.int32)
    holder = tile_ids // TPD
    offset = jax.random.randint(first_key, (TILES, 4), -1, 2, dtype=jnp.int32)
    within = jax.random.randint(second_key, (TILES, 4), 0, TPD, dtype=jnp.int32)
    chosen = (holder[:, None] + offset) % owners * TPD + within
    chosen = chosen.at[0, 0].set(TILES - 1)
    chosen = chosen.at[0, 1].set(0)
    return chosen.astype(jnp.int32)


def draw_edge_code(key, part):
    codes = jax.random.randint(jax.random.fold_in(key, 23), (TILES, 4), 0, 8, dtype=jnp.int32)
    codes = codes.at[0, 2].set(7)
    codes = codes.at[0, 3].set(0)
    return codes.astype(jnp.int32)


def shard_levels(own_key, extent, pieces, least, top_value):
    level, own = 1.0, jax.random.fold_in(own_key, 6)
    for dim, shards_of in pieces:
        steps = jnp.exp(jax.random.uniform(jax.random.fold_in(own, dim), (shards_of,), jnp.float32, least / len(pieces), top_value / len(pieces)))
        level = level * jnp.repeat(steps, extent[dim] // shards_of).reshape([-1 if axis == dim else 1 for axis in range(len(extent))])
    return level


def gaussian(key, dims, spread, reach, pieces=(), kind=jnp.bfloat16):
    array = jax.random.normal(key, dims, jnp.float32) * spread
    if len(pieces) > 0:
        array = shard_levels(key, dims, pieces, -0.22, 0.18) * array
    return jnp.clip(array, min=-reach, max=reach).astype(kind)


def setup_inputs(seed: int = 0) -> dict:
    splits = jax.random.split(jax.random.key(seed), 8)
    features = gaussian(splits[0], (MEMBERS, TILES, TILE, TILE, C), 1.0, 6.0, ((0, 16), (1, 32)))
    cotangent = gaussian(splits[1], (MEMBERS, TILES, TILE, TILE, C), 1.0, 6.0, ((0, 16), (1, 32)))
    kernel = gaussian(splits[2], (KERNEL_TAPS * KERNEL_TAPS, C), (KERNEL_TAPS * KERNEL_TAPS) ** -0.5, 0.875, (), jnp.float32)
    weight_in = gaussian(splits[3], (C, HID), C ** -0.5, 0.375)
    weight_out = gaussian(splits[4], (HID, C), HID ** -0.5, 0.1875)
    tile_neighbour = draw_tile_neighbour(jax.random.fold_in(splits[7], 71), 0)
    edge_code = draw_edge_code(jax.random.fold_in(splits[7], 71), 0)
    return dict(features=features, cotangent=cotangent, kernel=kernel, weight_in=weight_in, weight_out=weight_out, tile_neighbour=tile_neighbour, edge_code=edge_code)


def pad_axis(values, from_end, before, later):
    widths = [(0, 0)] * values.ndim
    widths[values.ndim - from_end] = (before, later)
    return jnp.pad(values, widths)

def edge_strips(field_in, depth_rows):
    top_side = field_in[..., :depth_rows, :, :]
    bottom_side = jnp.flip(field_in[..., -depth_rows:, :, :], -3)
    left_side = jnp.swapaxes(field_in[..., :, :depth_rows, :], -3, -2)
    right_side = jnp.swapaxes(jnp.flip(field_in[..., :, -depth_rows:, :], -2), -3, -2)
    return jnp.stack([top_side, bottom_side, left_side, right_side], -4)

def place_edges(strips, edge_length):
    depth_rows = strips.shape[-3]
    extra = edge_length - depth_rows
    top_side = pad_axis(strips[..., 0, :, :, :], 3, 0, extra)
    bottom_side = pad_axis(jnp.flip(strips[..., 1, :, :, :], -3), 3, extra, 0)
    left_side = pad_axis(jnp.swapaxes(strips[..., 2, :, :, :], -3, -2), 2, 0, extra)
    right_side = pad_axis(jnp.flip(jnp.swapaxes(strips[..., 3, :, :, :], -3, -2), -2), 2, extra, 0)
    return top_side + bottom_side + left_side + right_side

def assemble(field_in, side_cells):
    top_block = jnp.flip(side_cells[..., 0, :, :, :], -3)
    bottom_block = side_cells[..., 1, :, :, :]
    left_block = jnp.flip(jnp.swapaxes(side_cells[..., 2, :, :, :], -3, -2), -2)
    right_block = jnp.swapaxes(side_cells[..., 3, :, :, :], -3, -2)
    middle = jnp.concatenate([left_block, field_in, right_block], -2)
    top_full = pad_axis(top_block, 2, HALO, HALO)
    bottom_full = pad_axis(bottom_block, 2, HALO, HALO)
    return jnp.concatenate([top_full, middle, bottom_full], -3)

def rim_cells(grad_padded_tile):
    edge_length = grad_padded_tile.shape[-2] - 2 * HALO
    inner = grad_padded_tile[..., HALO:HALO + edge_length, HALO:HALO + edge_length, :]
    top_side = jnp.flip(grad_padded_tile[..., :HALO, HALO:HALO + edge_length, :], -3)
    bottom_side = grad_padded_tile[..., HALO + edge_length:, HALO:HALO + edge_length, :]
    left_side = jnp.swapaxes(jnp.flip(grad_padded_tile[..., HALO:HALO + edge_length, :HALO, :], -2), -3, -2)
    right_side = jnp.swapaxes(grad_padded_tile[..., HALO:HALO + edge_length, HALO + edge_length:, :], -3, -2)
    return (inner, jnp.stack([top_side, bottom_side, left_side, right_side], -4))

def depthwise(padded_tile, kernel):
    edge_length = padded_tile.shape[-2] - 2 * HALO
    summed = jnp.zeros(padded_tile.shape[:-3] + (edge_length, edge_length, padded_tile.shape[-1]), jnp.float32)
    for first_operand in range(KERNEL_TAPS):
        for second_operand in range(KERNEL_TAPS):
            tap_window = padded_tile[..., DILATION_STEP * first_operand:DILATION_STEP * first_operand + edge_length, DILATION_STEP * second_operand:DILATION_STEP * second_operand + edge_length, :].astype(jnp.float32)
            summed = summed + tap_window * kernel[first_operand * KERNEL_TAPS + second_operand]
    return summed

def depthwise_back(grad_convolved, kernel):
    edge_length = grad_convolved.shape[-2]
    full_len = edge_length + 2 * HALO
    grad_padded_tile = jnp.zeros(grad_convolved.shape[:-3] + (full_len, full_len, grad_convolved.shape[-1]), jnp.float32)
    for first_operand in range(KERNEL_TAPS):
        for second_operand in range(KERNEL_TAPS):
            grad_padded_tile = grad_padded_tile.at[..., DILATION_STEP * first_operand:DILATION_STEP * first_operand + edge_length, DILATION_STEP * second_operand:DILATION_STEP * second_operand + edge_length, :].add(grad_convolved * kernel[first_operand * KERNEL_TAPS + second_operand])
    return grad_padded_tile

def tap_sums(padded_tile, grad_convolved):
    edge_length = grad_convolved.shape[-2]
    channels = grad_convolved.shape[-1]
    tap_rows = []
    for first_operand in range(KERNEL_TAPS):
        for second_operand in range(KERNEL_TAPS):
            tap_window = padded_tile[..., DILATION_STEP * first_operand:DILATION_STEP * first_operand + edge_length, DILATION_STEP * second_operand:DILATION_STEP * second_operand + edge_length, :].astype(jnp.float32)
            tap_rows.append(lax.optimization_barrier(jnp.sum((tap_window * grad_convolved).reshape(-1, channels), 0)))
    return jnp.stack(tap_rows)

def normalize(conv):
    mean_value = lax.optimization_barrier(jnp.mean(conv, -1, keepdims=True))
    centred = conv - mean_value
    inv_std = lax.rsqrt(lax.optimization_barrier(jnp.mean(centred * centred, -1, keepdims=True)) + 1e-06)
    return (centred * inv_std, inv_std)

def reference(features, cotangent, kernel, weight_in, weight_out, tile_neighbour, edge_code):
    source = (tile_neighbour * 4 + edge_code % 4).reshape(-1).astype(jnp.int32)
    flipped_mask = (edge_code >= 4)[:, :, None, None, None]
    norm_factor = 1.0 / math.sqrt(MEMBERS * TILES * TILE * TILE)

    def member_step(totals, inputs):
        field_in, grad_out = inputs
        strips = edge_strips(field_in, HALO).reshape(TILES * 4, HALO, TILE, C)
        side_cells = jnp.take(strips, source, axis=0).reshape(TILES, 4, HALO, TILE, C)
        side_cells = jnp.where(flipped_mask, jnp.flip(side_cells, -2), side_cells)
        padded_tile = assemble(field_in, side_cells)
        conv = depthwise(padded_tile, kernel)
        normed_f, inv_std = normalize(conv)
        normed = normed_f.astype(jnp.bfloat16).reshape(-1, C)
        preact = jnp.dot(normed, weight_in, preferred_element_type=jnp.float32)
        hidden = jax.nn.gelu(preact).astype(jnp.bfloat16)
        grad_rows = grad_out.reshape(-1, C)
        part_out = jnp.dot(hidden.T, grad_rows, preferred_element_type=jnp.float32)
        d_hidden = jnp.dot(grad_rows, weight_out.T, preferred_element_type=jnp.float32)
        _, pull_back = jax.vjp(jax.nn.gelu, preact)
        d_preact = pull_back(d_hidden)[0].astype(jnp.bfloat16)
        part_in = jnp.dot(normed.T, d_preact, preferred_element_type=jnp.float32)
        d_normed = jnp.dot(d_preact, weight_in.T, preferred_element_type=jnp.float32).reshape(conv.shape)
        grad_convolved = inv_std * (d_normed - lax.optimization_barrier(jnp.mean(d_normed, -1, keepdims=True)) - normed_f * lax.optimization_barrier(jnp.mean(d_normed * normed_f, -1, keepdims=True)))
        part_kernel = tap_sums(padded_tile, grad_convolved)
        grad_padded_tile = depthwise_back(grad_convolved, kernel)
        inner, side_grads = rim_cells(grad_padded_tile)
        side_grads = jnp.where(flipped_mask, jnp.flip(side_grads, -2), side_grads)
        edge_back = jax.ops.segment_sum(side_grads.reshape(TILES * 4, HALO, TILE, C), source, num_segments=TILES * 4)
        edge_back = edge_back.reshape(TILES, 4, HALO, TILE, C)
        grad_field = (grad_out.astype(jnp.float32) + inner + place_edges(edge_back, TILE)).astype(jnp.bfloat16)
        new_totals = (totals[0] + part_kernel, totals[1] + part_in, totals[2] + part_out)
        return (new_totals, grad_field)
    start = (jnp.zeros((KERNEL_TAPS * KERNEL_TAPS, C), jnp.float32), jnp.zeros((C, HID), jnp.float32), jnp.zeros((HID, C), jnp.float32))
    totals, grad_features = lax.scan(member_step, start, (features, cotangent))
    return (grad_features, totals[0] * norm_factor, totals[1] * norm_factor, totals[2] * norm_factor)
```

```python
import functools
import math

import jax
import jax.numpy as jnp
from jax import lax
from jax.experimental import pallas as pl
from jax.experimental.pallas import tpu as pltpu
from jax.sharding import PartitionSpec as P

C = 256
HID = 1024
TAPS = 7
HALO = 6
TILE = 16
PIX = TILE * TILE
LANES = 128
HALVES = C // LANES
BLOCK = 16 * 16
GRID = 4 * BLOCK
OUT_ROWS = 8
DC_PITCH = 24
CHUNK = 256
CHUNKS = HID // CHUNK
HALF_ROWS = C * HID // LANES
KROWS = 128
F32 = jnp.float32
BF16 = jnp.bfloat16
FACTORS = {(32, 16): (4, 8, 2, 4), (4, 4): (2, 2, 1, 2)}


def source_pixels(index, offset, step_k, step_m):
    r = 2 * ((index >> 4) & 15) + (index >> 9) - HALO
    c = 2 * (index & 15) + ((index >> 8) & 1) - HALO
    r_in = (r >= 0) & (r < TILE)
    c_in = (c >= 0) & (c < TILE)
    found = jnp.where(r_in & c_in, PIX + TILE * r + c, -1)
    sides = (
        (c_in & (r < 0), -1 - r, c),
        (c_in & (r >= TILE) & (r < TILE + HALO), r - TILE, c),
        (r_in & (c < 0), -1 - c, r),
        (r_in & (c >= TILE) & (c < TILE + HALO), c - TILE, r),
    )
    for s, (mask, depth, along) in enumerate(sides):
        found = jnp.where(mask, offset[s] + step_k[s] * depth + step_m[s] * along, found)
    return found


def dot(a, b, contract=((1,), (0,))):
    return lax.dot_general(a, b, (contract, ((), ())), preferred_element_type=F32)


def kernel_body(
    sizes,
    near_ref,
    code_ref,
    x_ref,
    cot_ref,
    taps_ref,
    w_in_ref,
    w_out_ref,
    gf_ref,
    gk_ref,
    gwi_ref,
    gwo_ref,
    tiles,
    gather,
    spread,
    padded,
    taps_b,
    conv,
    normed_f,
    normed_b,
    cot_p,
    d_hidden,
    d_conv,
    d_pad_hi,
    d_pad_lo,
    rim_send,
    rim_recv,
    tap_acc,
    part,
    part_b,
    r0,
    half,
    s1,
    r1,
    t1,
    s2,
    r2,
    zb,
    r3,
    zg,
    full,
    kb,
    kr_z,
    k_core,
    k_x,
    k_y,
    k_z,
    send_sem,
    recv_sem,
):
    nx, nzlo, nzhi, ny = sizes
    nz = nzlo * nzhi
    tiles_n = nzlo * nx
    me_t = lax.axis_index("tile")
    me_e = lax.axis_index("ens")
    x = lax.rem(me_t, nx)
    zlo = lax.div(me_t, nx)
    core = lax.rem(me_e, 2)
    y = lax.rem(lax.div(me_e, 2), ny)
    zhi = lax.div(me_e, 2 * ny)
    z = zhi * nzlo + zlo

    def at(tile, ens):
        return {"tile": tile, "ens": ens}

    before = at(lax.rem(me_t + tiles_n - 1, tiles_n), me_e)
    ahead = at(lax.rem(me_t + 1, tiles_n), me_e)
    sibling = at(me_t, me_e + 1 - 2 * core)
    xs = [lax.rem(x + d, nx) for d in range(1, nx)]
    ys = [lax.rem(y + d, ny) for d in range(1, ny)]
    zs = [lax.rem(z + d, nz) for d in range(1, nz)]
    x_peers = [at(zlo * nx + v, me_e) for v in xs]
    y_peers = [at(me_t, (zhi * ny + v) * 2 + core) for v in ys]
    z_peers = [
        at(lax.rem(v, nzlo) * nx + x, (lax.div(v, nzlo) * ny + y) * 2 + core) for v in zs
    ]
    peers = [before, ahead, sibling, *x_peers, *y_peers, *z_peers]

    barrier = pltpu.get_barrier_semaphore()
    for peer in peers:
        pl.semaphore_signal(
            barrier, inc=1, device_id=peer, device_id_type=pl.DeviceIdType.MESH
        )
    pl.semaphore_wait(barrier, len(peers))

    started = []

    def send(src, dst, peer):
        n = len(started)
        copy = pltpu.make_async_remote_copy(
            src_ref=src,
            dst_ref=dst,
            send_sem=send_sem.at[n],
            recv_sem=recv_sem.at[n],
            device_id=peer,
            device_id_type=pl.DeviceIdType.MESH,
        )
        copy.start()
        started.append(copy)
        return copy

    def rows(start, size):
        return pl.ds(pl.multiple_of(start, size), size)

    halo = [
        send(x_ref, tiles.at[pl.ds(2 * PIX, PIX)], before),
        send(x_ref, tiles.at[pl.ds(0, PIX)], ahead),
    ]

    tiles[pl.ds(PIX, PIX), :] = x_ref[...]
    offset, step_k, step_m = [], [], []
    for s in range(4):
        code = code_ref[0, s]
        slot = lax.rem(near_ref[0, s] - me_t + (tiles_n + 1), tiles_n)
        edge = lax.rem(code, 4)
        flip = lax.div(code, 4)
        along_rows = lax.div(edge, 2)
        far = lax.rem(edge, 2)
        mult_k = TILE - (TILE - 1) * along_rows
        mult_m = 1 + (TILE - 1) * along_rows
        offset.append(slot * PIX + (TILE - 1) * (mult_k * far + mult_m * flip))
        step_k.append(mult_k * (1 - 2 * far))
        step_m.append(mult_m * (1 - 2 * flip))

    def one_hot(mask):
        return jnp.where(mask, 1.0, 0.0).astype(BF16)

    def fill_gather(i, _):
        cells = i * LANES + lax.broadcasted_iota(jnp.int32, (LANES, 1), 0)
        found = source_pixels(cells, offset, step_k, step_m)
        pixel = lax.broadcasted_iota(jnp.int32, (LANES, 3 * PIX), 1)
        gather[rows(i * LANES, LANES), :] = one_hot(found == pixel)
        return 0

    lax.fori_loop(0, GRID // LANES, fill_gather, 0)
    cells_row = lax.broadcasted_iota(jnp.int32, (1, GRID), 1)
    found_row = source_pixels(cells_row, offset, step_k, step_m)

    def fill_spread(i, _):
        pixel = i * 64 + lax.broadcasted_iota(jnp.int32, (64, GRID), 0)
        spread[rows(i * 64, 64), :] = one_hot(pixel == found_row)
        return 0

    lax.fori_loop(0, 3 * PIX // 64, fill_spread, 0)

    order = lax.broadcasted_iota(jnp.int32, (PIX, 1), 0)
    natural = (2 * ((order >> 3) & 7) + (order >> 7)) * TILE + 2 * (order & 7) + (
        (order >> 6) & 1
    )
    reorder = one_hot(natural == lax.broadcasted_iota(jnp.int32, (PIX, PIX), 1))
    cot_p[...] = dot(reorder, cot_ref[...]).astype(BF16)
    for n in range(CHUNKS):
        cols = pl.ds(n * CHUNK, CHUNK)
        d_hidden[:, cols] = dot(cot_p[...], w_out_ref[cols, :], ((1,), (1,)))
    for h in range(HALVES):
        lanes = pl.ds(h * LANES, LANES)
        for tap in range(TAPS * TAPS):
            taps_b[h, pl.ds(tap * 8, 8), :] = jnp.broadcast_to(
                taps_ref[pl.ds(tap, 1), lanes], (8, LANES)
            )
    d_conv[...] = jnp.zeros_like(d_conv)
    d_pad_hi[...] = jnp.zeros_like(d_pad_hi)
    d_pad_lo[...] = jnp.zeros_like(d_pad_lo)
    tap_acc[...] = jnp.zeros_like(tap_acc)
    kb[...] = jnp.zeros_like(kb)

    for copy in halo:
        copy.wait_recv()

    def assemble(i, _):
        got = dot(gather[rows(i * BLOCK, BLOCK), :], tiles[...])
        for h in range(HALVES):
            padded[h, rows(i * BLOCK, BLOCK), :] = got[:, h * LANES : (h + 1) * LANES]
        return 0

    lax.fori_loop(0, 4, assemble, 0)

    def conv_block(i, _):
        h, blk = lax.div(i, 4), lax.rem(i, 4)
        base = pl.multiple_of(blk * BLOCK, BLOCK)
        acc = [jnp.zeros((8, LANES), F32) for _ in range(OUT_ROWS)]
        for b in range(TAPS):
            weight = [taps_b[h, pl.ds((a * TAPS + b) * 8, 8), :] for a in range(TAPS)]
            for rr in range(OUT_ROWS + TAPS - 1):
                cell = padded[h, pl.ds(base + (rr * 16 + b), 8), :]
                for a in range(TAPS):
                    if 0 <= rr - a < OUT_ROWS:
                        acc[rr - a] += cell * weight[a]
        out = pl.multiple_of(blk * 64, 64)
        for ii in range(OUT_ROWS):
            conv[h, pl.ds(out + ii * 8, 8), :] = acc[ii]
        return 0

    lax.fori_loop(0, 4 * HALVES, conv_block, 0)

    c0, c1 = conv[0], conv[1]
    mean = jnp.sum(c0 + c1, axis=-1, keepdims=True) * (1.0 / C)
    c0, c1 = c0 - mean, c1 - mean
    var = jnp.sum(c0 * c0 + c1 * c1, axis=-1, keepdims=True) * (1.0 / C)
    inv_std = lax.rsqrt(var + 1e-06)
    for h, centred in enumerate((c0, c1)):
        scaled = centred * inv_std
        normed_f[h] = scaled
        normed_b[:, pl.ds(h * LANES, LANES)] = scaled.astype(BF16)

    root = math.sqrt(2.0 / math.pi)
    first = []
    d_normed = jnp.zeros((PIX, C), F32)
    for n in range(CHUNKS):
        cols = pl.ds(n * CHUNK, CHUNK)
        pre = dot(normed_b[...], w_in_ref[:, cols])
        square = pre * pre
        bent = jnp.tanh(root * pre * (1.0 + 0.044715 * square))
        up = 0.5 * (1.0 + bent)
        hidden = (pre * up).astype(BF16)
        slope = up + 0.5 * pre * (1.0 - bent * bent) * (
            root * (1.0 + 3 * 0.044715 * square)
        )
        d_pre = (d_hidden[:, cols] * slope).astype(BF16)
        got_in = dot(normed_b[...], d_pre, ((0,), (0,)))
        got_out = dot(hidden, cot_p[...], ((0,), (0,)))
        for side, got in enumerate((got_in, got_out)):
            for h in range(HALVES):
                piece = got[:, h * LANES : (h + 1) * LANES]
                place = pl.ds((HALVES * n + h) * CHUNK, CHUNK)
                part[side, place, :] = piece
                part_b[side, place, :] = piece.astype(BF16)
        place = pl.ds(HALVES * n * CHUNK, HALVES * CHUNK)
        first.append(send(part_b.at[1 - core, place], r0.at[place], sibling))
        d_normed = d_normed + dot(d_pre, w_in_ref[:, cols], ((1,), (1,)))

    n0, n1 = normed_f[0], normed_f[1]
    d0, d1 = d_normed[:, :LANES], d_normed[:, LANES:]
    mean_d = jnp.sum(d0 + d1, axis=-1, keepdims=True) * (1.0 / C)
    mean_dn = jnp.sum(d0 * n0 + d1 * n1, axis=-1, keepdims=True) * (1.0 / C)
    for h, (d_half, n_half) in enumerate(((d0, n0), (d1, n1))):
        got = inv_std * (d_half - mean_d - n_half * mean_dn)
        for q in range(PIX // 8):
            d_conv[h, pl.ds(q * DC_PITCH + 8, 8), :] = got[q * 8 : q * 8 + 8]

    x_rows = HALF_ROWS // 2 // nx
    y_rows = HALF_ROWS // 2 // ny
    last = HALF_ROWS // 2 // (nx * ny)
    for n, copy in enumerate(first):
        copy.wait_recv()
        place = pl.ds(HALVES * n * CHUNK, HALVES * CHUNK)
        total = part[core, place, :] + r0[place, :].astype(F32)
        half[place, :] = total
        s1[place, :] = total.astype(BF16)
    second = []
    for d in range(1, nx):
        second.append(
            send(
                s1.at[rows(xs[d - 1] * x_rows, x_rows)],
                r1.at[pl.ds((d - 1) * x_rows, x_rows)],
                x_peers[d - 1],
            )
        )
    r1_y = (nx - 1) * x_rows
    for d in range(1, ny):
        second.append(
            send(
                s1.at[rows(HALF_ROWS // 2 + ys[d - 1] * y_rows, y_rows)],
                r1.at[pl.ds(r1_y + (d - 1) * y_rows, y_rows)],
                y_peers[d - 1],
            )
        )

    def back_block(i, _):
        h, blk = lax.div(i, 4), lax.rem(i, 4)
        base = pl.multiple_of(blk * (OUT_ROWS * DC_PITCH), 8)
        acc = [
            [jnp.zeros((8, LANES), F32) for _ in range(2)]
            for _ in range(OUT_ROWS + TAPS - 1)
        ]
        for b in range(TAPS):
            weight = [taps_b[h, pl.ds((a * TAPS + b) * 8, 8), :] for a in range(TAPS)]
            for ii in range(OUT_ROWS):
                cells = [
                    d_conv[h, pl.ds(base + (ii * DC_PITCH + 8 * (v + 1) - b), 8), :]
                    for v in range(2)
                ]
                for a in range(TAPS):
                    for v in range(2):
                        acc[ii + a][v] += cells[v] * weight[a]
        lanes = rows(h * LANES, LANES)
        out = pl.multiple_of(blk * BLOCK, BLOCK)
        for rr in range(OUT_ROWS + TAPS - 1):
            row = jnp.concatenate(acc[rr], axis=0)
            high = row.astype(BF16)
            d_pad_hi[pl.ds(out + rr * 16, 16), lanes] = high
            d_pad_lo[pl.ds(out + rr * 16, 16), lanes] = (row - high.astype(F32)).astype(
                BF16
            )
        return 0

    lax.fori_loop(0, 4 * HALVES, back_block, 0)
    rim = []
    for slot, peer in ((0, before), (2, ahead)):
        rim_send[slot // 2] = dot(spread[pl.ds(slot * PIX, PIX), :], d_pad_hi[...]).astype(
            BF16
        )
        rim.append(send(rim_send.at[slot // 2], rim_recv.at[slot // 2], peer))
    own = spread[pl.ds(PIX, PIX), :]
    grad_own = dot(own, d_pad_hi[...]) + dot(own, d_pad_lo[...])

    for copy in second:
        copy.wait_recv()
    got_a = half[rows(x * x_rows, x_rows), :]
    for d in range(1, nx):
        got_a = got_a + r1[pl.ds((d - 1) * x_rows, x_rows), :].astype(F32)
    got_b = half[rows(HALF_ROWS // 2 + y * y_rows, y_rows), :]
    for d in range(1, ny):
        got_b = got_b + r1[pl.ds(r1_y + (d - 1) * y_rows, y_rows), :].astype(F32)
    t1[pl.ds(0, x_rows), :] = got_a
    t1[pl.ds(x_rows, y_rows), :] = got_b
    s2[pl.ds(0, x_rows), :] = got_a.astype(BF16)
    s2[pl.ds(x_rows, y_rows), :] = got_b.astype(BF16)
    third = []
    for d in range(1, ny):
        third.append(
            send(
                s2.at[rows(ys[d - 1] * last, last)],
                r2.at[pl.ds((d - 1) * last, last)],
                y_peers[d - 1],
            )
        )
    r2_x = (ny - 1) * last
    for d in range(1, nx):
        third.append(
            send(
                s2.at[rows(x_rows + xs[d - 1] * last, last)],
                r2.at[pl.ds(r2_x + (d - 1) * last, last)],
                x_peers[d - 1],
            )
        )

    def tap_block(i, _):
        h, blk = lax.div(i, 4), lax.rem(i, 4)
        base = pl.multiple_of(blk * BLOCK, BLOCK)
        dc_base = pl.multiple_of(blk * (OUT_ROWS * DC_PITCH), 8)
        grads = [
            d_conv[h, pl.ds(dc_base + (ii * DC_PITCH + 8), 8), :] for ii in range(OUT_ROWS)
        ]
        for b in range(TAPS):
            acc = [tap_acc[h, pl.ds((a * TAPS + b) * 8, 8), :] for a in range(TAPS)]
            for rr in range(OUT_ROWS + TAPS - 1):
                cell = padded[h, pl.ds(base + (rr * 16 + b), 8), :]
                for a in range(TAPS):
                    if 0 <= rr - a < OUT_ROWS:
                        acc[a] += cell * grads[rr - a]
            for a in range(TAPS):
                tap_acc[h, pl.ds((a * TAPS + b) * 8, 8), :] = acc[a]
        return 0

    lax.fori_loop(0, 4 * HALVES, tap_block, 0)
    for h in range(HALVES):
        kb[pl.ds(h * 64, TAPS * TAPS), :] = jnp.sum(
            tap_acc[h].reshape(TAPS * TAPS, 8, LANES), axis=1
        )
    k_rows = KROWS // nz
    kz = [
        send(kb.at[rows(zs[d - 1] * k_rows, k_rows)], kr_z.at[d - 1], z_peers[d - 1])
        for d in range(1, nz)
    ]

    for copy in third:
        copy.wait_recv()
    got_a = t1[rows(y * last, last), :]
    for d in range(1, ny):
        got_a = got_a + r2[pl.ds((d - 1) * last, last), :].astype(F32)
    got_b = t1[rows(x_rows + x * last, last), :]
    for d in range(1, nx):
        got_b = got_b + r2[pl.ds(r2_x + (d - 1) * last, last), :].astype(F32)
    zb[pl.ds(0, last), :] = got_a
    zb[pl.ds(last, last), :] = got_b
    z_rows = 2 * last // nz
    fourth = [
        send(zb.at[rows(zs[d - 1] * z_rows, z_rows)], r3.at[d - 1], z_peers[d - 1])
        for d in range(1, nz)
    ]

    for copy in rim:
        copy.wait_recv()
    gf_ref[...] = (
        cot_ref[...].astype(F32)
        + grad_own
        + rim_recv[0].astype(F32)
        + rim_recv[1].astype(F32)
    ).astype(BF16)

    for copy in kz:
        copy.wait_recv()
    k_sum = kb[rows(z * k_rows, k_rows), :]
    for d in range(1, nz):
        k_sum = k_sum + kr_z[d - 1]
    k_core[0] = k_sum
    kc = send(k_core.at[0], k_core.at[1], sibling)

    norm = 1.0 / math.sqrt(PIX * tiles_n * nzhi * ny * 2)
    for copy in fourth:
        copy.wait_recv()
    z_sum = zb[rows(z * z_rows, z_rows), :]
    for d in range(1, nz):
        z_sum = z_sum + r3[d - 1]
    z_place = rows(z * z_rows, z_rows)
    zg[z_place, :] = z_sum * norm
    fifth = [send(zg.at[z_place], zg.at[z_place], peer) for peer in z_peers]

    kc.wait_recv()
    k_x[x] = k_core[0] + k_core[1]
    kx = [send(k_x.at[x], k_x.at[x], peer) for peer in x_peers]

    for copy in fifth:
        copy.wait_recv()
    core_base = core * HALF_ROWS
    b_base = core_base + HALF_ROWS // 2
    place_a = rows(core_base + x * x_rows + y * last, last)
    place_b = rows(b_base + y * y_rows + x * last, last)
    full[place_a, :] = zg[pl.ds(0, last), :].astype(BF16)
    full[place_b, :] = zg[pl.ds(last, last), :].astype(BF16)
    sixth = [send(full.at[place_a], full.at[place_a], peer) for peer in y_peers]
    sixth += [send(full.at[place_b], full.at[place_b], peer) for peer in x_peers]

    for copy in kx:
        copy.wait_recv()
    k_sum = k_x[0]
    for v in range(1, nx):
        k_sum = k_sum + k_x[v]
    k_y[y] = k_sum
    ky = [send(k_y.at[y], k_y.at[y], peer) for peer in y_peers]

    for copy in sixth:
        copy.wait_recv()
    block_a = rows(core_base + x * x_rows, x_rows)
    block_b = rows(b_base + y * y_rows, y_rows)
    seventh_a = [send(full.at[block_a], full.at[block_a], peer) for peer in x_peers]
    seventh_b = [send(full.at[block_b], full.at[block_b], peer) for peer in y_peers]
    eighth = [send(full.at[block], full.at[block], sibling) for block in (block_a, block_b)]

    for copy in ky:
        copy.wait_recv()
    k_sum = k_y[0]
    for v in range(1, ny):
        k_sum = k_sum + k_y[v]
    k_place = rows(z * k_rows, k_rows)
    k_z[k_place, :] = k_sum * norm
    kg = [send(k_z.at[k_place], k_z.at[k_place], peer) for peer in z_peers]

    for d in range(1, nx):
        seventh_a[d - 1].wait_recv()
        block = rows(core_base + lax.rem(x + nx - d, nx) * x_rows, x_rows)
        eighth.append(send(full.at[block], full.at[block], sibling))
    for d in range(1, ny):
        seventh_b[d - 1].wait_recv()
        block = rows(b_base + lax.rem(y + ny - d, ny) * y_rows, y_rows)
        eighth.append(send(full.at[block], full.at[block], sibling))

    for copy in kg:
        copy.wait_recv()
    for h in range(HALVES):
        gk_ref[:, pl.ds(h * LANES, LANES)] = k_z[pl.ds(h * 64, TAPS * TAPS), :]
    for copy in eighth:
        copy.wait_recv()
    for n in range(CHUNKS):
        for h in range(HALVES):
            j = HALVES * n + h
            gwi_ref[:, pl.ds(j * LANES, LANES)] = full[pl.ds(j * CHUNK, CHUNK), :].astype(
                F32
            )
            gwo_ref[pl.ds(n * CHUNK, CHUNK), pl.ds(h * LANES, LANES)] = full[
                pl.ds(HALF_ROWS + j * CHUNK, CHUNK), :
            ].astype(F32)
    for copy in started:
        copy.wait_send()


def body(sizes, features, cotangent, kernel, weight_in, weight_out, near, code):
    nx, nzlo, nzhi, ny = sizes
    nz = nzlo * nzhi
    x_rows = HALF_ROWS // 2 // nx
    y_rows = HALF_ROWS // 2 // ny
    last = HALF_ROWS // 2 // (nx * ny)
    k_rows = KROWS // nz
    copies = 16 + 6 * (nx - 1 + ny - 1) + 1 + 4 * (nz - 1)
    vmem = pl.BlockSpec(memory_space=pltpu.VMEM)
    smem = pl.BlockSpec(memory_space=pltpu.SMEM)
    gf, gk, gwi, gwo = pl.pallas_call(
        functools.partial(kernel_body, sizes),
        out_shape=(
            jax.ShapeDtypeStruct((PIX, C), BF16),
            jax.ShapeDtypeStruct((TAPS * TAPS, C), F32),
            jax.ShapeDtypeStruct((C, HID), F32),
            jax.ShapeDtypeStruct((HID, C), F32),
        ),
        in_specs=[smem, smem, vmem, vmem, vmem, vmem, vmem],
        out_specs=(vmem, vmem, vmem, vmem),
        scratch_shapes=[
            pltpu.VMEM((3 * PIX, C), BF16),
            pltpu.VMEM((GRID, 3 * PIX), BF16),
            pltpu.VMEM((3 * PIX, GRID), BF16),
            pltpu.VMEM((HALVES, GRID, LANES), F32),
            pltpu.VMEM((HALVES, TAPS * TAPS * 8, LANES), F32),
            pltpu.VMEM((HALVES, PIX, LANES), F32),
            pltpu.VMEM((HALVES, PIX, LANES), F32),
            pltpu.VMEM((PIX, C), BF16),
            pltpu.VMEM((PIX, C), BF16),
            pltpu.VMEM((PIX, HID), F32),
            pltpu.VMEM((HALVES, PIX // 8 * DC_PITCH, LANES), F32),
            pltpu.VMEM((GRID, C), BF16),
            pltpu.VMEM((GRID, C), BF16),
            pltpu.VMEM((2, PIX, C), BF16),
            pltpu.VMEM((2, PIX, C), BF16),
            pltpu.VMEM((HALVES, TAPS * TAPS * 8, LANES), F32),
            pltpu.VMEM((2, HALF_ROWS, LANES), F32),
            pltpu.VMEM((2, HALF_ROWS, LANES), BF16),
            pltpu.VMEM((HALF_ROWS, LANES), BF16),
            pltpu.VMEM((HALF_ROWS, LANES), F32),
            pltpu.VMEM((HALF_ROWS, LANES), BF16),
            pltpu.VMEM(((nx - 1) * x_rows + (ny - 1) * y_rows, LANES), BF16),
            pltpu.VMEM((x_rows + y_rows, LANES), F32),
            pltpu.VMEM((x_rows + y_rows, LANES), BF16),
            pltpu.VMEM(((nx + ny - 2) * last, LANES), BF16),
            pltpu.VMEM((2 * last, LANES), F32),
            pltpu.VMEM((nz - 1, 2 * last // nz, LANES), F32),
            pltpu.VMEM((2 * last, LANES), F32),
            pltpu.VMEM((2 * HALF_ROWS, LANES), BF16),
            pltpu.VMEM((KROWS, LANES), F32),
            pltpu.VMEM((nz - 1, k_rows, LANES), F32),
            pltpu.VMEM((2, k_rows, LANES), F32),
            pltpu.VMEM((nx, k_rows, LANES), F32),
            pltpu.VMEM((ny, k_rows, LANES), F32),
            pltpu.VMEM((KROWS, LANES), F32),
            pltpu.SemaphoreType.DMA((copies,)),
            pltpu.SemaphoreType.DMA((copies,)),
        ],
        compiler_params=pltpu.CompilerParams(
            collective_id=0, has_side_effects=True, vmem_limit_bytes=48 << 20
        ),
        name="block_step",
    )(
        near,
        code,
        features.reshape(PIX, C),
        cotangent.reshape(PIX, C),
        kernel,
        weight_in,
        weight_out,
    )
    return gf.reshape(1, 1, TILE, TILE, C), gk, gwi, gwo


def solution(mesh):
    sizes = FACTORS[(mesh.shape["tile"], mesh.shape["ens"])]
    in_specs = (
        P("ens", "tile", None, None, None),
        P("ens", "tile", None, None, None),
        P(),
        P(),
        P(),
        P("tile", None),
        P("tile", None),
    )
    out_specs = (P("ens", "tile", None, None, None), P(), P(), P())
    return jax.shard_map(
        functools.partial(body, sizes),
        mesh=mesh,
        in_specs=in_specs,
        out_specs=out_specs,
        check_vma=False,
    )
```

```python
import functools
import math

import jax
import jax.numpy as jnp
from jax import lax
from jax.experimental import pallas as pl
from jax.experimental.pallas import tpu as pltpu
from jax.sharding import PartitionSpec as P

C = 256
HID = 1024
TAPS = 7
HALO = 6
TILE = 16
PIX = TILE * TILE
LANES = 128
HALVES = C // LANES
BLOCK = 16 * 16
GRID = 4 * BLOCK
OUT_ROWS = 8
DC_PITCH = 24
CHUNK = 256
CHUNKS = HID // CHUNK
HALF_ROWS = C * HID // LANES
KROWS = 128
F32 = jnp.float32
BF16 = jnp.bfloat16
FACTORS = {(32, 16): (4, 8, 2, 4, 4), (4, 4): (1, 4, 1, 2, 2), (8, 2): (2, 4, 1, 1, 2)}


def source_pixels(index, offset, step_k, step_m):
    r = 2 * ((index >> 4) & 15) + (index >> 9) - HALO
    c = 2 * (index & 15) + ((index >> 8) & 1) - HALO
    r_in = (r >= 0) & (r < TILE)
    c_in = (c >= 0) & (c < TILE)
    found = jnp.where(r_in & c_in, PIX + TILE * r + c, -1)
    sides = (
        (c_in & (r < 0), -1 - r, c),
        (c_in & (r >= TILE) & (r < TILE + HALO), r - TILE, c),
        (r_in & (c < 0), -1 - c, r),
        (r_in & (c >= TILE) & (c < TILE + HALO), c - TILE, r),
    )
    for s, (mask, depth, along) in enumerate(sides):
        found = jnp.where(mask, offset[s] + step_k[s] * depth + step_m[s] * along, found)
    return found


def dot(a, b, contract=((1,), (0,))):
    return lax.dot_general(a, b, (contract, ((), ())), preferred_element_type=F32)


def kernel_body(
    sizes,
    near_ref,
    code_ref,
    x_hbm,
    cot_hbm,
    taps_hbm,
    w_in_hbm,
    w_out_hbm,
    gf_ref,
    gk_ref,
    full,
    cot_ref,
    taps_ref,
    w_in_ref,
    w_out_ref,
    tiles,
    gather,
    spread,
    padded,
    taps_b,
    conv,
    normed_f,
    normed_b,
    cot_p,
    d_hidden,
    d_conv,
    d_pad_hi,
    d_pad_lo,
    rim_send,
    rim_recv,
    tap_acc,
    part,
    part_b,
    r0,
    half,
    s1,
    r1,
    t1,
    s2,
    r2,
    zs,
    kb,
    kr,
    kc,
    kr_x,
    k_q,
    k_s,
    k_all,
    local_sem,
    send_sem,
    recv_sem,
):
    nx, nzlo, nzhi, ny, nq = sizes
    nz = nzlo * nzhi
    ns = nz // nq
    tiles_n = nzlo * nx
    me_t = lax.axis_index("tile")
    me_e = lax.axis_index("ens")
    x = lax.rem(me_t, nx)
    zlo = lax.div(me_t, nx)
    core = lax.rem(me_e, 2)
    y = lax.rem(lax.div(me_e, 2), ny)
    zhi = lax.div(me_e, 2 * ny)
    z = zhi * nzlo + zlo
    q = lax.rem(z, nq)
    group = lax.div(z, nq)

    def at(tile, ens):
        return {"tile": tile, "ens": ens}

    def chip(x_at, y_at, z_at):
        return at(
            lax.rem(z_at, nzlo) * nx + x_at, (lax.div(z_at, nzlo) * ny + y_at) * 2 + core
        )

    before = at(lax.rem(me_t + tiles_n - 1, tiles_n), me_e)
    ahead = at(lax.rem(me_t + 1, tiles_n), me_e)
    sibling = at(me_t, me_e + 1 - 2 * core)
    xs = [lax.rem(x + d, nx) for d in range(1, nx)]
    ys = [lax.rem(y + d, ny) for d in range(1, ny)]
    x_peers = [chip(v, y, z) for v in xs]
    y_peers = [chip(x, v, z) for v in ys]
    yq_peers, xq_peers, only_q = [], [], []
    for d in range(max(nx, ny)):
        for dq in range(nq):
            if d == 0 and dq == 0:
                continue
            qv = lax.rem(q + dq, nq)
            if d < ny:
                yv = lax.rem(y + d, ny)
                yq_peers.append((chip(x, yv, group * nq + qv), yv * nq + qv))
            if 0 < d < nx or d == 0:
                xv = lax.rem(x + d, nx)
                xq_peers.append((chip(xv, y, group * nq + qv), xv * nq + qv))
            if d == 0:
                only_q.append(yq_peers[-1][0])
    far_peers = [chip(x, y, lax.rem(z + d * nq, nz)) for d in range(1, ns)]
    peers = [before, ahead, sibling, *far_peers, *only_q]
    peers += [peer for peer, _ in yq_peers[nq - 1 :]] + [peer for peer, _ in xq_peers[nq - 1 :]]

    barrier = pltpu.get_barrier_semaphore()
    for peer in peers:
        pl.semaphore_signal(
            barrier, inc=1, device_id=peer, device_id_type=pl.DeviceIdType.MESH
        )
    loads = [
        pltpu.make_async_copy(src, dst, local_sem.at[n])
        for n, (src, dst) in enumerate(
            (
                (x_hbm, tiles.at[pl.ds(PIX, PIX)]),
                (cot_hbm, cot_ref),
                (w_out_hbm, w_out_ref),
                (taps_hbm, taps_ref),
                (w_in_hbm, w_in_ref),
            )
        )
    ]
    for load in loads:
        load.start()
    pl.semaphore_wait(barrier, len(peers))

    started = []

    def send(src, dst, peer):
        n = len(started)
        copy = pltpu.make_async_remote_copy(
            src_ref=src,
            dst_ref=dst,
            send_sem=send_sem.at[n],
            recv_sem=recv_sem.at[n],
            device_id=peer,
            device_id_type=pl.DeviceIdType.MESH,
        )
        copy.start()
        started.append(copy)
        return copy

    def rows(start, size):
        return pl.ds(pl.multiple_of(start, size), size)

    halo = [
        send(x_hbm, tiles.at[pl.ds(2 * PIX, PIX)], before),
        send(x_hbm, tiles.at[pl.ds(0, PIX)], ahead),
    ]

    for load in loads:
        load.wait()
    offset, step_k, step_m = [], [], []
    for s in range(4):
        code = code_ref[0, s]
        slot = lax.rem(near_ref[0, s] - me_t + (tiles_n + 1), tiles_n)
        edge = lax.rem(code, 4)
        flip = lax.div(code, 4)
        along_rows = lax.div(edge, 2)
        far = lax.rem(edge, 2)
        mult_k = TILE - (TILE - 1) * along_rows
        mult_m = 1 + (TILE - 1) * along_rows
        offset.append(slot * PIX + (TILE - 1) * (mult_k * far + mult_m * flip))
        step_k.append(mult_k * (1 - 2 * far))
        step_m.append(mult_m * (1 - 2 * flip))

    def one_hot(mask):
        return jnp.where(mask, 1.0, 0.0).astype(BF16)

    def fill_gather(i, _):
        cells = i * LANES + lax.broadcasted_iota(jnp.int32, (LANES, 1), 0)
        found = source_pixels(cells, offset, step_k, step_m)
        pixel = lax.broadcasted_iota(jnp.int32, (LANES, 3 * PIX), 1)
        gather[rows(i * LANES, LANES), :] = one_hot(found == pixel)
        return 0

    lax.fori_loop(0, GRID // LANES, fill_gather, 0)
    cells_row = lax.broadcasted_iota(jnp.int32, (1, GRID), 1)
    found_row = source_pixels(cells_row, offset, step_k, step_m)

    def fill_spread(i, _):
        pixel = i * 64 + lax.broadcasted_iota(jnp.int32, (64, GRID), 0)
        spread[rows(i * 64, 64), :] = one_hot(pixel == found_row)
        return 0

    lax.fori_loop(0, 3 * PIX // 64, fill_spread, 0)

    order = lax.broadcasted_iota(jnp.int32, (PIX, 1), 0)
    natural = (2 * ((order >> 3) & 7) + (order >> 7)) * TILE + 2 * (order & 7) + (
        (order >> 6) & 1
    )
    reorder = one_hot(natural == lax.broadcasted_iota(jnp.int32, (PIX, PIX), 1))
    cot_p[...] = dot(reorder, cot_ref[...]).astype(BF16)
    for n in range(CHUNKS):
        cols = pl.ds(n * CHUNK, CHUNK)
        d_hidden[:, cols] = dot(cot_p[...], w_out_ref[cols, :], ((1,), (1,)))
    for h in range(HALVES):
        lanes = pl.ds(h * LANES, LANES)
        for tap in range(TAPS * TAPS):
            taps_b[h, pl.ds(tap * 8, 8), :] = jnp.broadcast_to(
                taps_ref[pl.ds(tap, 1), lanes], (8, LANES)
            )
    d_conv[...] = jnp.zeros_like(d_conv)
    d_pad_hi[...] = jnp.zeros_like(d_pad_hi)
    d_pad_lo[...] = jnp.zeros_like(d_pad_lo)
    tap_acc[...] = jnp.zeros_like(tap_acc)
    kb[...] = jnp.zeros_like(kb)

    for copy in halo:
        copy.wait_recv()

    def assemble(i, _):
        got = dot(gather[rows(i * BLOCK, BLOCK), :], tiles[...])
        for h in range(HALVES):
            padded[h, rows(i * BLOCK, BLOCK), :] = got[:, h * LANES : (h + 1) * LANES]
        return 0

    lax.fori_loop(0, 4, assemble, 0)

    def conv_block(i, _):
        h, blk = lax.div(i, 4), lax.rem(i, 4)
        base = pl.multiple_of(blk * BLOCK, BLOCK)
        acc = [jnp.zeros((8, LANES), F32) for _ in range(OUT_ROWS)]
        for b in range(TAPS):
            weight = [taps_b[h, pl.ds((a * TAPS + b) * 8, 8), :] for a in range(TAPS)]
            for rr in range(OUT_ROWS + TAPS - 1):
                cell = padded[h, pl.ds(base + (rr * 16 + b), 8), :]
                for a in range(TAPS):
                    if 0 <= rr - a < OUT_ROWS:
                        acc[rr - a] += cell * weight[a]
        out = pl.multiple_of(blk * 64, 64)
        for ii in range(OUT_ROWS):
            conv[h, pl.ds(out + ii * 8, 8), :] = acc[ii]
        return 0

    lax.fori_loop(0, 4 * HALVES, conv_block, 0)

    c0, c1 = conv[0], conv[1]
    mean = jnp.sum(c0 + c1, axis=-1, keepdims=True) * (1.0 / C)
    c0, c1 = c0 - mean, c1 - mean
    var = jnp.sum(c0 * c0 + c1 * c1, axis=-1, keepdims=True) * (1.0 / C)
    inv_std = lax.rsqrt(var + 1e-06)
    for h, centred in enumerate((c0, c1)):
        scaled = centred * inv_std
        normed_f[h] = scaled
        normed_b[:, pl.ds(h * LANES, LANES)] = scaled.astype(BF16)

    root = math.sqrt(2.0 / math.pi)
    first = []
    d_normed = jnp.zeros((PIX, C), F32)
    for n in range(CHUNKS):
        cols = pl.ds(n * CHUNK, CHUNK)
        pre = dot(normed_b[...], w_in_ref[:, cols])
        square = pre * pre
        bent = jnp.tanh(root * pre * (1.0 + 0.044715 * square))
        up = 0.5 * (1.0 + bent)
        hidden = (pre * up).astype(BF16)
        slope = up + 0.5 * pre * (1.0 - bent * bent) * (
            root * (1.0 + 3 * 0.044715 * square)
        )
        d_pre = (d_hidden[:, cols] * slope).astype(BF16)
        got_in = dot(normed_b[...], d_pre, ((0,), (0,)))
        got_out = dot(hidden, cot_p[...], ((0,), (0,)))
        for side, got in enumerate((got_in, got_out)):
            for h in range(HALVES):
                piece = got[:, h * LANES : (h + 1) * LANES]
                place = pl.ds((HALVES * n + h) * CHUNK, CHUNK)
                part[side, place, :] = piece
                part_b[side, place, :] = piece.astype(BF16)
        place = pl.ds(HALVES * n * CHUNK, HALVES * CHUNK)
        first.append(send(part_b.at[1 - core, place], r0.at[place], sibling))
        d_normed = d_normed + dot(d_pre, w_in_ref[:, cols], ((1,), (1,)))

    n0, n1 = normed_f[0], normed_f[1]
    d0, d1 = d_normed[:, :LANES], d_normed[:, LANES:]
    mean_d = jnp.sum(d0 + d1, axis=-1, keepdims=True) * (1.0 / C)
    mean_dn = jnp.sum(d0 * n0 + d1 * n1, axis=-1, keepdims=True) * (1.0 / C)
    for h, (d_half, n_half) in enumerate(((d0, n0), (d1, n1))):
        got = inv_std * (d_half - mean_d - n_half * mean_dn)
        for row in range(PIX // 8):
            d_conv[h, pl.ds(row * DC_PITCH + 8, 8), :] = got[row * 8 : row * 8 + 8]

    x_rows = HALF_ROWS // 2 // nx
    y_rows = HALF_ROWS // 2 // ny
    last = HALF_ROWS // 2 // (nx * ny * nq)
    for n, copy in enumerate(first):
        copy.wait_recv()
        place = pl.ds(HALVES * n * CHUNK, HALVES * CHUNK)
        total = part[core, place, :] + r0[place, :].astype(F32)
        half[place, :] = total
        s1[place, :] = total.astype(BF16)
    second = []
    for d in range(1, nx):
        second.append(
            send(
                s1.at[rows(xs[d - 1] * x_rows, x_rows)],
                r1.at[pl.ds((d - 1) * x_rows, x_rows)],
                x_peers[d - 1],
            )
        )
    r1_y = (nx - 1) * x_rows
    for d in range(1, ny):
        second.append(
            send(
                s1.at[rows(HALF_ROWS // 2 + ys[d - 1] * y_rows, y_rows)],
                r1.at[pl.ds(r1_y + (d - 1) * y_rows, y_rows)],
                y_peers[d - 1],
            )
        )

    def tap_block(i, _):
        h, blk = lax.div(i, 4), lax.rem(i, 4)
        base = pl.multiple_of(blk * BLOCK, BLOCK)
        dc_base = pl.multiple_of(blk * (OUT_ROWS * DC_PITCH), 8)
        grads = [
            d_conv[h, pl.ds(dc_base + (ii * DC_PITCH + 8), 8), :] for ii in range(OUT_ROWS)
        ]
        for b in range(TAPS):
            acc = [tap_acc[h, pl.ds((a * TAPS + b) * 8, 8), :] for a in range(TAPS)]
            for rr in range(OUT_ROWS + TAPS - 1):
                cell = padded[h, pl.ds(base + (rr * 16 + b), 8), :]
                for a in range(TAPS):
                    if 0 <= rr - a < OUT_ROWS:
                        acc[a] += cell * grads[rr - a]
            for a in range(TAPS):
                tap_acc[h, pl.ds((a * TAPS + b) * 8, 8), :] = acc[a]
        return 0

    lax.fori_loop(0, 4 * HALVES, tap_block, 0)
    for h in range(HALVES):
        kb[pl.ds(h * 64, TAPS * TAPS), :] = jnp.sum(
            tap_acc[h].reshape(TAPS * TAPS, 8, LANES), axis=1
        )
    k_half = KROWS // 2
    k_rows = k_half // nx
    k1 = send(kb.at[rows((1 - core) * k_half, k_half)], kr, sibling)

    def back_block(i, _):
        h, blk = lax.div(i, 4), lax.rem(i, 4)
        base = pl.multiple_of(blk * (OUT_ROWS * DC_PITCH), 8)
        acc = [
            [jnp.zeros((8, LANES), F32) for _ in range(2)]
            for _ in range(OUT_ROWS + TAPS - 1)
        ]
        for b in range(TAPS):
            weight = [taps_b[h, pl.ds((a * TAPS + b) * 8, 8), :] for a in range(TAPS)]
            for ii in range(OUT_ROWS):
                cells = [
                    d_conv[h, pl.ds(base + (ii * DC_PITCH + 8 * (v + 1) - b), 8), :]
                    for v in range(2)
                ]
                for a in range(TAPS):
                    for v in range(2):
                        acc[ii + a][v] += cells[v] * weight[a]
        lanes = rows(h * LANES, LANES)
        out = pl.multiple_of(blk * BLOCK, BLOCK)
        for rr in range(OUT_ROWS + TAPS - 1):
            row = jnp.concatenate(acc[rr], axis=0)
            high = row.astype(BF16)
            d_pad_hi[pl.ds(out + rr * 16, 16), lanes] = high
            d_pad_lo[pl.ds(out + rr * 16, 16), lanes] = (row - high.astype(F32)).astype(
                BF16
            )
        return 0

    lax.fori_loop(0, 4 * HALVES, back_block, 0)
    rim = []
    for slot, peer in ((0, before), (2, ahead)):
        rim_send[slot // 2] = dot(spread[pl.ds(slot * PIX, PIX), :], d_pad_hi[...]).astype(
            BF16
        )
        rim.append(send(rim_send.at[slot // 2], rim_recv.at[slot // 2], peer))
    own = spread[pl.ds(PIX, PIX), :]
    grad_own = dot(own, d_pad_hi[...]) + dot(own, d_pad_lo[...])

    for copy in second:
        copy.wait_recv()
    got_a = half[rows(x * x_rows, x_rows), :]
    for d in range(1, nx):
        got_a = got_a + r1[pl.ds((d - 1) * x_rows, x_rows), :].astype(F32)
    got_b = half[rows(HALF_ROWS // 2 + y * y_rows, y_rows), :]
    for d in range(1, ny):
        got_b = got_b + r1[pl.ds(r1_y + (d - 1) * y_rows, y_rows), :].astype(F32)
    t1[pl.ds(0, x_rows), :] = got_a
    t1[pl.ds(x_rows, y_rows), :] = got_b
    s2[pl.ds(0, x_rows), :] = got_a.astype(BF16)
    s2[pl.ds(x_rows, y_rows), :] = got_b.astype(BF16)
    third = []
    for n, (peer, place) in enumerate(yq_peers):
        third.append(send(s2.at[rows(place * last, last)], r2.at[pl.ds(n * last, last)], peer))
    r2_x = len(yq_peers) * last
    for n, (peer, place) in enumerate(xq_peers):
        third.append(
            send(
                s2.at[rows(x_rows + place * last, last)],
                r2.at[pl.ds(r2_x + n * last, last)],
                peer,
            )
        )

    k1.wait_recv()
    kc[...] = kb[rows(core * k_half, k_half), :] + kr[...]
    k2 = [
        send(kc.at[rows(xs[d - 1] * k_rows, k_rows)], kr_x.at[d - 1], x_peers[d - 1])
        for d in range(1, nx)
    ]

    for copy in rim:
        copy.wait_recv()
    gf_ref[...] = (
        cot_ref[...].astype(F32)
        + grad_own
        + rim_recv[0].astype(F32)
        + rim_recv[1].astype(F32)
    ).astype(BF16)

    norm = 1.0 / math.sqrt(PIX * tiles_n * nzhi * ny * 2)
    for copy in third:
        copy.wait_recv()
    place_y = y * nq + q
    place_x = x * nq + q
    got_a = t1[rows(place_y * last, last), :]
    for n in range(len(yq_peers)):
        got_a = got_a + r2[pl.ds(n * last, last), :].astype(F32)
    got_b = t1[rows(x_rows + place_x * last, last), :]
    for n in range(len(xq_peers)):
        got_b = got_b + r2[pl.ds(r2_x + n * last, last), :].astype(F32)
    zs[group, pl.ds(0, last), :] = got_a.astype(BF16)
    zs[group, pl.ds(last, last), :] = got_b.astype(BF16)
    fourth = [send(zs.at[group], zs.at[group], peer) for peer in far_peers]

    for copy in k2:
        copy.wait_recv()
    k_sum = kc[rows(x * k_rows, k_rows), :]
    for d in range(1, nx):
        k_sum = k_sum + kr_x[d - 1]
    k_q[place_y] = k_sum
    k3 = [send(k_q.at[place_y], k_q.at[place_y], peer) for peer, _ in yq_peers]

    for copy in fourth:
        copy.wait_recv()
    total = zs[0].astype(F32)
    for n in range(1, ns):
        total = total + zs[n].astype(F32)
    total = (total * norm).astype(BF16)
    core_base = core * HALF_ROWS
    b_base = core_base + HALF_ROWS // 2
    place_a = rows(core_base + x * x_rows + place_y * last, last)
    place_b = rows(b_base + y * y_rows + place_x * last, last)
    full[place_a, :] = total[:last]
    full[place_b, :] = total[last:]
    fifth = [send(full.at[place_a], full.at[place_a], peer) for peer, _ in yq_peers]
    fifth += [send(full.at[place_b], full.at[place_b], peer) for peer, _ in xq_peers]

    for copy in k3:
        copy.wait_recv()
    k_sum = k_q[0]
    for n in range(1, ny * nq):
        k_sum = k_sum + k_q[n]
    k_s[group] = k_sum
    k4 = [send(k_s.at[group], k_s.at[group], peer) for peer in far_peers]

    for copy in fifth:
        copy.wait_recv()
    block_a = rows(core_base + x * x_rows, x_rows)
    block_b = rows(b_base + y * y_rows, y_rows)
    seventh_a = [send(full.at[block_a], full.at[block_a], peer) for peer in x_peers]
    seventh_b = [send(full.at[block_b], full.at[block_b], peer) for peer in y_peers]
    eighth = [send(full.at[block], full.at[block], sibling) for block in (block_a, block_b)]

    for copy in k4:
        copy.wait_recv()
    k_sum = k_s[0]
    for n in range(1, ns):
        k_sum = k_sum + k_s[n]
    k_place = rows(core * k_half + x * k_rows, k_rows)
    k_all[k_place, :] = k_sum * norm
    k5 = [send(k_all.at[k_place], k_all.at[k_place], peer) for peer in x_peers]
    for copy in k5:
        copy.wait_recv()
    k_mine = rows(core * k_half, k_half)
    k6 = send(k_all.at[k_mine], k_all.at[k_mine], sibling)

    for d in range(1, nx):
        seventh_a[d - 1].wait_recv()
        block = rows(core_base + lax.rem(x + nx - d, nx) * x_rows, x_rows)
        eighth.append(send(full.at[block], full.at[block], sibling))
    for d in range(1, ny):
        seventh_b[d - 1].wait_recv()
        block = rows(b_base + lax.rem(y + ny - d, ny) * y_rows, y_rows)
        eighth.append(send(full.at[block], full.at[block], sibling))

    k6.wait_recv()
    for h in range(HALVES):
        gk_ref[:, pl.ds(h * LANES, LANES)] = k_all[pl.ds(h * 64, TAPS * TAPS), :]
    for copy in eighth:
        copy.wait_recv()
    for copy in started:
        copy.wait_send()


def unpack_body(gf_in, gk_in, full, gf_ref, gk_ref, gwi_ref, gwo_ref, gwi, gwo, sem):
    copies = [
        pltpu.make_async_copy(gf_in, gf_ref, sem.at[0]),
        pltpu.make_async_copy(gk_in, gk_ref, sem.at[1]),
    ]
    for copy in copies:
        copy.start()
    for n in range(CHUNKS):
        for h in range(HALVES):
            j = HALVES * n + h
            gwi[pl.ds(0, C), pl.ds(j * LANES, LANES)] = full[pl.ds(j * C, C), :].astype(F32)
            gwo[pl.ds(n * CHUNK, CHUNK), pl.ds(h * LANES, LANES)] = full[
                pl.ds(HALF_ROWS + j * CHUNK, CHUNK), :
            ].astype(F32)
        for m, (src, dst) in enumerate(
            (
                (gwo.at[pl.ds(n * CHUNK, CHUNK)], gwo_ref.at[pl.ds(n * CHUNK, CHUNK)]),
                (
                    gwi.at[pl.ds(0, C), pl.ds(n * CHUNK, CHUNK)],
                    gwi_ref.at[pl.ds(0, C), pl.ds(n * CHUNK, CHUNK)],
                ),
            )
        ):
            copy = pltpu.make_async_copy(src, dst, sem.at[2 + 2 * n + m])
            copy.start()
            copies.append(copy)
    for copy in copies:
        copy.wait()


def body(sizes, features, cotangent, kernel, weight_in, weight_out, near, code):
    nx, nzlo, nzhi, ny, nq = sizes
    ns = nzlo * nzhi // nq
    x_rows = HALF_ROWS // 2 // nx
    y_rows = HALF_ROWS // 2 // ny
    last = HALF_ROWS // 2 // (nx * ny * nq)
    k_half = KROWS // 2
    k_rows = k_half // nx
    in_group = nx * nq - 1 + ny * nq - 1
    copies = 24 + 6 * (nx + ny) + 2 * in_group + ny * nq + 2 * ns
    vmem = pl.BlockSpec(memory_space=pltpu.VMEM)
    smem = pl.BlockSpec(memory_space=pltpu.SMEM)
    hbm = pl.BlockSpec(memory_space=pl.ANY)
    big = pl.BlockSpec(memory_space=pltpu.HBM)
    gf, gk, full = pl.pallas_call(
        functools.partial(kernel_body, sizes),
        out_shape=(
            jax.ShapeDtypeStruct((PIX, C), BF16),
            jax.ShapeDtypeStruct((TAPS * TAPS, C), F32),
            jax.ShapeDtypeStruct((2 * HALF_ROWS, LANES), BF16),
        ),
        in_specs=[smem] * 2 + [big] * 5,
        out_specs=(vmem, vmem, vmem),
        scratch_shapes=[
            pltpu.VMEM((PIX, C), BF16),
            pltpu.VMEM((TAPS * TAPS, C), F32),
            pltpu.VMEM((C, HID), BF16),
            pltpu.VMEM((HID, C), BF16),
            pltpu.VMEM((3 * PIX, C), BF16),
            pltpu.VMEM((GRID, 3 * PIX), BF16),
            pltpu.VMEM((3 * PIX, GRID), BF16),
            pltpu.VMEM((HALVES, GRID, LANES), F32),
            pltpu.VMEM((HALVES, TAPS * TAPS * 8, LANES), F32),
            pltpu.VMEM((HALVES, PIX, LANES), F32),
            pltpu.VMEM((HALVES, PIX, LANES), F32),
            pltpu.VMEM((PIX, C), BF16),
            pltpu.VMEM((PIX, C), BF16),
            pltpu.VMEM((PIX, HID), F32),
            pltpu.VMEM((HALVES, PIX // 8 * DC_PITCH, LANES), F32),
            pltpu.VMEM((GRID, C), BF16),
            pltpu.VMEM((GRID, C), BF16),
            pltpu.VMEM((2, PIX, C), BF16),
            pltpu.VMEM((2, PIX, C), BF16),
            pltpu.VMEM((HALVES, TAPS * TAPS * 8, LANES), F32),
            pltpu.VMEM((2, HALF_ROWS, LANES), F32),
            pltpu.VMEM((2, HALF_ROWS, LANES), BF16),
            pltpu.VMEM((HALF_ROWS, LANES), BF16),
            pltpu.VMEM((HALF_ROWS, LANES), F32),
            pltpu.VMEM((HALF_ROWS, LANES), BF16),
            pltpu.VMEM((max(1, nx - 1) * x_rows + max(1, ny - 1) * y_rows, LANES), BF16),
            pltpu.VMEM((x_rows + y_rows, LANES), F32),
            pltpu.VMEM((x_rows + y_rows, LANES), BF16),
            pltpu.VMEM((in_group * last, LANES), BF16),
            pltpu.VMEM((ns, 2 * last, LANES), BF16),
            pltpu.VMEM((KROWS, LANES), F32),
            pltpu.VMEM((k_half, LANES), F32),
            pltpu.VMEM((k_half, LANES), F32),
            pltpu.VMEM((max(1, nx - 1), k_rows, LANES), F32),
            pltpu.VMEM((ny * nq, k_rows, LANES), F32),
            pltpu.VMEM((ns, k_rows, LANES), F32),
            pltpu.VMEM((KROWS, LANES), F32),
            pltpu.SemaphoreType.DMA((5,)),
            pltpu.SemaphoreType.DMA((copies,)),
            pltpu.SemaphoreType.DMA((copies,)),
        ],
        compiler_params=pltpu.CompilerParams(
            collective_id=0, has_side_effects=True, vmem_limit_bytes=61 << 20
        ),
        name="block_step",
    )(
        near,
        code,
        features.reshape(PIX, C),
        cotangent.reshape(PIX, C),
        kernel,
        weight_in,
        weight_out,
    )
    gf, gk, gwi, gwo = pl.pallas_call(
        unpack_body,
        out_shape=(
            jax.ShapeDtypeStruct((PIX, C), BF16),
            jax.ShapeDtypeStruct((TAPS * TAPS, C), F32),
            jax.ShapeDtypeStruct((C, HID), F32),
            jax.ShapeDtypeStruct((HID, C), F32),
        ),
        in_specs=[vmem, vmem, vmem],
        out_specs=(hbm, hbm, hbm, hbm),
        scratch_shapes=[
            pltpu.VMEM((C, HID), F32),
            pltpu.VMEM((HID, C), F32),
            pltpu.SemaphoreType.DMA((2 + 2 * CHUNKS,)),
        ],
        compiler_params=pltpu.CompilerParams(vmem_limit_bytes=12 << 20),
        name="unpack",
    )(gf, gk, full)
    return gf.reshape(1, 1, TILE, TILE, C), gk, gwi, gwo


def solution(mesh):
    sizes = FACTORS[(mesh.shape["tile"], mesh.shape["ens"])]
    in_specs = (
        P("ens", "tile", None, None, None),
        P("ens", "tile", None, None, None),
        P(),
        P(),
        P(),
        P("tile", None),
        P("tile", None),
    )
    out_specs = (P("ens", "tile", None, None, None), P(), P(), P())
    return jax.shard_map(
        functools.partial(body, sizes),
        mesh=mesh,
        in_specs=in_specs,
        out_specs=out_specs,
        check_vma=False,
    )
```

```python
import functools
import math

import jax
import jax.numpy as jnp
from jax import lax
from jax.experimental import pallas as pl
from jax.experimental.pallas import tpu as pltpu
from jax.sharding import PartitionSpec as P

C = 256
HID = 1024
TAPS = 7
HALO = 6
TILE = 16
PIX = TILE * TILE
LANES = 128
HALVES = C // LANES
OWN = 2 * PIX
BLOCK = 16 * 16
GRID = 4 * BLOCK
OUT_ROWS = 8
DC_PITCH = 24
CHUNK = 256
CHUNKS = HID // CHUNK
HALF_ROWS = C * HID // LANES
KROWS = 128
F32 = jnp.float32
BF16 = jnp.bfloat16
FACTORS = {(32, 16): (4, 8, 2, 4, 4), (4, 4): (1, 4, 1, 2, 2), (8, 2): (2, 4, 1, 1, 2)}


def source_pixels(index, offset, step_k, step_m):
    r = 2 * ((index >> 4) & 15) + (index >> 9) - HALO
    c = 2 * (index & 15) + ((index >> 8) & 1) - HALO
    r_in = (r >= 0) & (r < TILE)
    c_in = (c >= 0) & (c < TILE)
    found = jnp.where(r_in & c_in, OWN + TILE * r + c, -1)
    sides = (
        (c_in & (r < 0), -1 - r, c),
        (c_in & (r >= TILE) & (r < TILE + HALO), r - TILE, c),
        (r_in & (c < 0), -1 - c, r),
        (r_in & (c >= TILE) & (c < TILE + HALO), c - TILE, r),
    )
    for s, (mask, depth, along) in enumerate(sides):
        found = jnp.where(mask, offset[s] + step_k[s] * depth + step_m[s] * along, found)
    return found


def dot(a, b, contract=((1,), (0,))):
    return lax.dot_general(a, b, (contract, ((), ())), preferred_element_type=F32)


def kernel_body(
    sizes,
    near_hbm,
    code_hbm,
    x_hbm,
    cot_hbm,
    taps_hbm,
    w_in_hbm,
    w_out_hbm,
    gf_ref,
    gk_ref,
    full,
    near_ref,
    code_ref,
    cot_ref,
    taps_ref,
    w_in_ref,
    w_out_ref,
    tiles,
    gather,
    spread,
    padded,
    taps_b,
    conv,
    normed_f,
    normed_b,
    cot_p,
    d_hidden,
    d_conv,
    d_pad_hi,
    d_pad_lo,
    rim_send,
    rim_recv,
    tap_acc,
    part,
    part_b,
    r0,
    half,
    s1,
    r1,
    t1,
    s2,
    r2,
    zs,
    kb,
    kr,
    kc,
    kr_x,
    k_q,
    k_s,
    k_all,
    local_sem,
    send_sem,
    recv_sem,
):
    nx, nzlo, nzhi, ny, nq = sizes
    nz = nzlo * nzhi
    ns = nz // nq
    tiles_n = nzlo * nx
    me_t = lax.axis_index("tile")
    me_e = lax.axis_index("ens")
    x = lax.rem(me_t, nx)
    zlo = lax.div(me_t, nx)
    core = lax.rem(me_e, 2)
    y = lax.rem(lax.div(me_e, 2), ny)
    zhi = lax.div(me_e, 2 * ny)
    z = zhi * nzlo + zlo
    q = lax.rem(z, nq)
    group = lax.div(z, nq)

    def at(tile, ens):
        return {"tile": tile, "ens": ens}

    def chip(x_at, y_at, z_at):
        return at(
            lax.rem(z_at, nzlo) * nx + x_at, (lax.div(z_at, nzlo) * ny + y_at) * 2 + core
        )

    before = at(lax.rem(me_t + tiles_n - 1, tiles_n), me_e)
    ahead = at(lax.rem(me_t + 1, tiles_n), me_e)
    sibling = at(me_t, me_e + 1 - 2 * core)
    xs = [lax.rem(x + d, nx) for d in range(1, nx)]
    ys = [lax.rem(y + d, ny) for d in range(1, ny)]
    x_peers = [chip(v, y, z) for v in xs]
    y_peers = [chip(x, v, z) for v in ys]
    yq_peers, xq_peers, only_q = [], [], []
    for d in range(max(nx, ny)):
        for dq in range(nq):
            if d == 0 and dq == 0:
                continue
            qv = lax.rem(q + dq, nq)
            if d < ny:
                yv = lax.rem(y + d, ny)
                yq_peers.append((chip(x, yv, group * nq + qv), yv * nq + qv))
            if 0 < d < nx or d == 0:
                xv = lax.rem(x + d, nx)
                xq_peers.append((chip(xv, y, group * nq + qv), xv * nq + qv))
            if d == 0:
                only_q.append(yq_peers[-1][0])
    far_peers = [chip(x, y, lax.rem(z + d * nq, nz)) for d in range(1, ns)]
    peers = [before, ahead, sibling, *far_peers, *only_q]
    peers += [peer for peer, _ in yq_peers[nq - 1 :]] + [peer for peer, _ in xq_peers[nq - 1 :]]

    barrier = pltpu.get_barrier_semaphore()
    for peer in peers:
        pl.semaphore_signal(
            barrier, inc=1, device_id=peer, device_id_type=pl.DeviceIdType.MESH
        )
    loads = [
        pltpu.make_async_copy(src, dst, local_sem.at[n])
        for n, (src, dst) in enumerate(
            (
                (near_hbm, near_ref),
                (code_hbm, code_ref),
                (x_hbm, tiles.at[pl.ds(OWN, PIX)]),
                (cot_hbm, cot_ref),
                (w_out_hbm, w_out_ref),
                (taps_hbm, taps_ref),
                (w_in_hbm, w_in_ref),
            )
        )
    ]
    for load in loads:
        load.start()
    pl.semaphore_wait(barrier, len(peers))

    started = []

    def send(src, dst, peer):
        n = len(started)
        copy = pltpu.make_async_remote_copy(
            src_ref=src,
            dst_ref=dst,
            send_sem=send_sem.at[n],
            recv_sem=recv_sem.at[n],
            device_id=peer,
            device_id_type=pl.DeviceIdType.MESH,
        )
        copy.start()
        started.append(copy)
        return copy

    def rows(start, size):
        return pl.ds(pl.multiple_of(start, size), size)

    halo = [
        send(x_hbm, tiles.at[pl.ds(PIX, PIX)], before),
        send(x_hbm, tiles.at[pl.ds(0, PIX)], ahead),
    ]

    for load in loads:
        load.wait()
    offset, step_k, step_m = [], [], []
    for s in range(4):
        code = code_ref[0, s]
        slot = lax.rem(2 * lax.rem(near_ref[0, s] - me_t + (tiles_n + 1), tiles_n), 3)
        edge = lax.rem(code, 4)
        flip = lax.div(code, 4)
        along_rows = lax.div(edge, 2)
        far = lax.rem(edge, 2)
        mult_k = TILE - (TILE - 1) * along_rows
        mult_m = 1 + (TILE - 1) * along_rows
        offset.append(slot * PIX + (TILE - 1) * (mult_k * far + mult_m * flip))
        step_k.append(mult_k * (1 - 2 * far))
        step_m.append(mult_m * (1 - 2 * flip))

    def one_hot(mask):
        return jnp.where(mask, 1.0, 0.0).astype(BF16)

    def fill_gather(i, _):
        cells = i * LANES + lax.broadcasted_iota(jnp.int32, (LANES, 1), 0)
        found = source_pixels(cells, offset, step_k, step_m)
        pixel = lax.broadcasted_iota(jnp.int32, (LANES, 3 * PIX), 1)
        gather[rows(i * LANES, LANES), :] = one_hot(found == pixel)
        return 0

    lax.fori_loop(0, GRID // LANES, fill_gather, 0)
    cells_row = lax.broadcasted_iota(jnp.int32, (1, GRID), 1)
    found_row = source_pixels(cells_row, offset, step_k, step_m)

    def fill_spread(i, _):
        pixel = i * 64 + lax.broadcasted_iota(jnp.int32, (64, GRID), 0)
        spread[rows(i * 64, 64), :] = one_hot(pixel == found_row)
        return 0

    lax.fori_loop(0, 3 * PIX // 64, fill_spread, 0)

    order = lax.broadcasted_iota(jnp.int32, (PIX, 1), 0)
    natural = (2 * ((order >> 3) & 7) + (order >> 7)) * TILE + 2 * (order & 7) + (
        (order >> 6) & 1
    )
    reorder = one_hot(natural == lax.broadcasted_iota(jnp.int32, (PIX, PIX), 1))
    cot_p[...] = dot(reorder, cot_ref[...]).astype(BF16)
    for n in range(CHUNKS):
        cols = pl.ds(n * CHUNK, CHUNK)
        d_hidden[:, cols] = dot(cot_p[...], w_out_ref[cols, :], ((1,), (1,)))
    for h in range(HALVES):
        lanes = pl.ds(h * LANES, LANES)
        for tap in range(TAPS * TAPS):
            taps_b[h, pl.ds(tap * 8, 8), :] = jnp.broadcast_to(
                taps_ref[pl.ds(tap, 1), lanes], (8, LANES)
            )
    d_conv[...] = jnp.zeros_like(d_conv)
    d_pad_hi[...] = jnp.zeros_like(d_pad_hi)
    d_pad_lo[...] = jnp.zeros_like(d_pad_lo)
    tap_acc[...] = jnp.zeros_like(tap_acc)
    kb[...] = jnp.zeros_like(kb)

    inner = [
        dot(gather[pl.ds(i * BLOCK, BLOCK), pl.ds(OWN, PIX)], tiles[pl.ds(OWN, PIX), :])
        for i in range(4)
    ]
    for i in range(4):
        for h in range(HALVES):
            padded[h, pl.ds(i * BLOCK, BLOCK), :] = inner[i][:, h * LANES : (h + 1) * LANES]

    for copy in halo:
        copy.wait_recv()
    for i in range(4):
        got = dot(gather[pl.ds(i * BLOCK, BLOCK), pl.ds(0, OWN)], tiles[pl.ds(0, OWN), :])
        for h in range(HALVES):
            padded[h, pl.ds(i * BLOCK, BLOCK), :] += got[:, h * LANES : (h + 1) * LANES]

    def conv_block(i, _):
        h, blk = lax.div(i, 4), lax.rem(i, 4)
        base = pl.multiple_of(blk * BLOCK, BLOCK)
        acc = [jnp.zeros((8, LANES), F32) for _ in range(OUT_ROWS)]
        for b in range(TAPS):
            weight = [taps_b[h, pl.ds((a * TAPS + b) * 8, 8), :] for a in range(TAPS)]
            for rr in range(OUT_ROWS + TAPS - 1):
                cell = padded[h, pl.ds(base + (rr * 16 + b), 8), :]
                for a in range(TAPS):
                    if 0 <= rr - a < OUT_ROWS:
                        acc[rr - a] += cell * weight[a]
        out = pl.multiple_of(blk * 64, 64)
        for ii in range(OUT_ROWS):
            conv[h, pl.ds(out + ii * 8, 8), :] = acc[ii]
        return 0

    lax.fori_loop(0, 4 * HALVES, conv_block, 0)

    c0, c1 = conv[0], conv[1]
    mean = jnp.sum(c0 + c1, axis=-1, keepdims=True) * (1.0 / C)
    c0, c1 = c0 - mean, c1 - mean
    var = jnp.sum(c0 * c0 + c1 * c1, axis=-1, keepdims=True) * (1.0 / C)
    inv_std = lax.rsqrt(var + 1e-06)
    for h, centred in enumerate((c0, c1)):
        scaled = centred * inv_std
        normed_f[h] = scaled
        normed_b[:, pl.ds(h * LANES, LANES)] = scaled.astype(BF16)

    x_rows = HALF_ROWS // 2 // nx
    y_rows = HALF_ROWS // 2 // ny
    last = HALF_ROWS // 2 // (nx * ny * nq)
    r1_y = (nx - 1) * x_rows

    def chip_sum(n):
        first[n].wait_recv()
        place = pl.ds(HALVES * n * CHUNK, HALVES * CHUNK)
        total = part[core, place, :] + r0[place, :].astype(F32)
        half[place, :] = total
        s1[place, :] = total.astype(BF16)

    root = math.sqrt(2.0 / math.pi)
    first = []
    d_normed = jnp.zeros((PIX, C), F32)
    for n in range(CHUNKS):
        cols = pl.ds(n * CHUNK, CHUNK)
        pre = dot(normed_b[...], w_in_ref[:, cols])
        square = pre * pre
        bent = jnp.tanh(root * pre * (1.0 + 0.044715 * square))
        up = 0.5 * (1.0 + bent)
        hidden = (pre * up).astype(BF16)
        slope = up + 0.5 * pre * (1.0 - bent * bent) * (
            root * (1.0 + 3 * 0.044715 * square)
        )
        d_pre = (d_hidden[:, cols] * slope).astype(BF16)
        got_in = dot(normed_b[...], d_pre, ((0,), (0,)))
        got_out = dot(hidden, cot_p[...], ((0,), (0,)))
        for side, got in enumerate((got_in, got_out)):
            for h in range(HALVES):
                piece = got[:, h * LANES : (h + 1) * LANES]
                place = pl.ds((HALVES * n + h) * CHUNK, CHUNK)
                part[side, place, :] = piece
                part_b[side, place, :] = piece.astype(BF16)
        place = pl.ds(HALVES * n * CHUNK, HALVES * CHUNK)
        first.append(send(part_b.at[1 - core, place], r0.at[place], sibling))
        d_normed = d_normed + dot(d_pre, w_in_ref[:, cols], ((1,), (1,)))
        if n == CHUNKS // 2:
            for m in range(CHUNKS // 2):
                chip_sum(m)
            second_a = [
                send(
                    s1.at[rows(xs[d - 1] * x_rows, x_rows)],
                    r1.at[pl.ds((d - 1) * x_rows, x_rows)],
                    x_peers[d - 1],
                )
                for d in range(1, nx)
            ]

    n0, n1 = normed_f[0], normed_f[1]
    d0, d1 = d_normed[:, :LANES], d_normed[:, LANES:]
    mean_d = jnp.sum(d0 + d1, axis=-1, keepdims=True) * (1.0 / C)
    mean_dn = jnp.sum(d0 * n0 + d1 * n1, axis=-1, keepdims=True) * (1.0 / C)
    for h, (d_half, n_half) in enumerate(((d0, n0), (d1, n1))):
        got = inv_std * (d_half - mean_d - n_half * mean_dn)
        for row in range(PIX // 8):
            d_conv[h, pl.ds(row * DC_PITCH + 8, 8), :] = got[row * 8 : row * 8 + 8]

    for m in range(CHUNKS // 2, CHUNKS):
        chip_sum(m)
    second_b = [
        send(
            s1.at[rows(HALF_ROWS // 2 + ys[d - 1] * y_rows, y_rows)],
            r1.at[pl.ds(r1_y + (d - 1) * y_rows, y_rows)],
            y_peers[d - 1],
        )
        for d in range(1, ny)
    ]

    def tap_block(i, _):
        h, blk = lax.div(i, 4), lax.rem(i, 4)
        base = pl.multiple_of(blk * BLOCK, BLOCK)
        dc_base = pl.multiple_of(blk * (OUT_ROWS * DC_PITCH), 8)
        grads = [
            d_conv[h, pl.ds(dc_base + (ii * DC_PITCH + 8), 8), :] for ii in range(OUT_ROWS)
        ]
        for b in range(TAPS):
            acc = [tap_acc[h, pl.ds((a * TAPS + b) * 8, 8), :] for a in range(TAPS)]
            for rr in range(OUT_ROWS + TAPS - 1):
                cell = padded[h, pl.ds(base + (rr * 16 + b), 8), :]
                for a in range(TAPS):
                    if 0 <= rr - a < OUT_ROWS:
                        acc[a] += cell * grads[rr - a]
            for a in range(TAPS):
                tap_acc[h, pl.ds((a * TAPS + b) * 8, 8), :] = acc[a]
        return 0

    lax.fori_loop(0, 4 * HALVES, tap_block, 0)
    for h in range(HALVES):
        kb[pl.ds(h * 64, TAPS * TAPS), :] = jnp.sum(
            tap_acc[h].reshape(TAPS * TAPS, 8, LANES), axis=1
        )
    k_half = KROWS // 2
    k_rows = k_half // nx
    k1 = send(kb.at[rows((1 - core) * k_half, k_half)], kr, sibling)

    for copy in second_a:
        copy.wait_recv()
    got_a = half[rows(x * x_rows, x_rows), :]
    for d in range(1, nx):
        got_a = got_a + r1[pl.ds((d - 1) * x_rows, x_rows), :].astype(F32)
    t1[pl.ds(0, x_rows), :] = got_a
    s2[pl.ds(0, x_rows), :] = got_a.astype(BF16)
    third = [
        send(s2.at[rows(place * last, last)], r2.at[pl.ds(n * last, last)], peer)
        for n, (peer, place) in enumerate(yq_peers)
    ]
    for copy in second_b:
        copy.wait_recv()
    got_b = half[rows(HALF_ROWS // 2 + y * y_rows, y_rows), :]
    for d in range(1, ny):
        got_b = got_b + r1[pl.ds(r1_y + (d - 1) * y_rows, y_rows), :].astype(F32)
    t1[pl.ds(x_rows, y_rows), :] = got_b
    s2[pl.ds(x_rows, y_rows), :] = got_b.astype(BF16)
    r2_x = len(yq_peers) * last
    third += [
        send(
            s2.at[rows(x_rows + place * last, last)],
            r2.at[pl.ds(r2_x + n * last, last)],
            peer,
        )
        for n, (peer, place) in enumerate(xq_peers)
    ]

    def back_block(i, _):
        h, blk = lax.div(i, 4), lax.rem(i, 4)
        base = pl.multiple_of(blk * (OUT_ROWS * DC_PITCH), 8)
        acc = [
            [jnp.zeros((8, LANES), F32) for _ in range(2)]
            for _ in range(OUT_ROWS + TAPS - 1)
        ]
        for b in range(TAPS):
            weight = [taps_b[h, pl.ds((a * TAPS + b) * 8, 8), :] for a in range(TAPS)]
            for ii in range(OUT_ROWS):
                cells = [
                    d_conv[h, pl.ds(base + (ii * DC_PITCH + 8 * (v + 1) - b), 8), :]
                    for v in range(2)
                ]
                for a in range(TAPS):
                    for v in range(2):
                        acc[ii + a][v] += cells[v] * weight[a]
        lanes = rows(h * LANES, LANES)
        out = pl.multiple_of(blk * BLOCK, BLOCK)
        for rr in range(OUT_ROWS + TAPS - 1):
            row = jnp.concatenate(acc[rr], axis=0)
            high = row.astype(BF16)
            d_pad_hi[pl.ds(out + rr * 16, 16), lanes] = high
            d_pad_lo[pl.ds(out + rr * 16, 16), lanes] = (row - high.astype(F32)).astype(
                BF16
            )
        return 0

    lax.fori_loop(0, 4 * HALVES, back_block, 0)
    rim = []
    for slot, peer in enumerate((before, ahead)):
        rim_send[slot] = dot(spread[pl.ds(slot * PIX, PIX), :], d_pad_hi[...]).astype(
            BF16
        )
        rim.append(send(rim_send.at[slot], rim_recv.at[slot], peer))
    own = spread[pl.ds(OWN, PIX), :]
    grad_own = dot(own, d_pad_hi[...]) + dot(own, d_pad_lo[...])

    k1.wait_recv()
    kc[...] = kb[rows(core * k_half, k_half), :] + kr[...]
    k2 = [
        send(kc.at[rows(xs[d - 1] * k_rows, k_rows)], kr_x.at[d - 1], x_peers[d - 1])
        for d in range(1, nx)
    ]

    for copy in rim:
        copy.wait_recv()
    gf_ref[...] = (
        cot_ref[...].astype(F32)
        + grad_own
        + rim_recv[0].astype(F32)
        + rim_recv[1].astype(F32)
    ).astype(BF16)

    norm = 1.0 / math.sqrt(PIX * tiles_n * nzhi * ny * 2)
    for copy in third:
        copy.wait_recv()
    place_y = y * nq + q
    place_x = x * nq + q
    got_a = t1[rows(place_y * last, last), :]
    for n in range(len(yq_peers)):
        got_a = got_a + r2[pl.ds(n * last, last), :].astype(F32)
    got_b = t1[rows(x_rows + place_x * last, last), :]
    for n in range(len(xq_peers)):
        got_b = got_b + r2[pl.ds(r2_x + n * last, last), :].astype(F32)
    zs[group, pl.ds(0, last), :] = got_a.astype(BF16)
    zs[group, pl.ds(last, last), :] = got_b.astype(BF16)
    fourth = [send(zs.at[group], zs.at[group], peer) for peer in far_peers]

    for copy in k2:
        copy.wait_recv()
    k_sum = kc[rows(x * k_rows, k_rows), :]
    for d in range(1, nx):
        k_sum = k_sum + kr_x[d - 1]
    k_q[place_y] = k_sum
    k3 = [send(k_q.at[place_y], k_q.at[place_y], peer) for peer, _ in yq_peers]

    for copy in fourth:
        copy.wait_recv()
    total = zs[0].astype(F32)
    for n in range(1, ns):
        total = total + zs[n].astype(F32)
    total = (total * norm).astype(BF16)
    core_base = core * HALF_ROWS
    b_base = core_base + HALF_ROWS // 2
    place_a = rows(core_base + x * x_rows + place_y * last, last)
    place_b = rows(b_base + y * y_rows + place_x * last, last)
    full[place_a, :] = total[:last]
    full[place_b, :] = total[last:]
    fifth_a = [send(full.at[place_a], full.at[place_a], peer) for peer, _ in yq_peers]
    fifth_b = [send(full.at[place_b], full.at[place_b], peer) for peer, _ in xq_peers]

    for copy in k3:
        copy.wait_recv()
    k_sum = k_q[0]
    for n in range(1, ny * nq):
        k_sum = k_sum + k_q[n]
    k_s[group] = k_sum
    k4 = [send(k_s.at[group], k_s.at[group], peer) for peer in far_peers]

    block_a = rows(core_base + x * x_rows, x_rows)
    block_b = rows(b_base + y * y_rows, y_rows)
    for copy in fifth_a:
        copy.wait_recv()
    seventh_a = [send(full.at[block_a], full.at[block_a], peer) for peer in x_peers]
    for copy in fifth_b:
        copy.wait_recv()
    seventh_b = [send(full.at[block_b], full.at[block_b], peer) for peer in y_peers]
    eighth = [send(full.at[block], full.at[block], sibling) for block in (block_a, block_b)]

    for copy in k4:
        copy.wait_recv()
    k_sum = k_s[0]
    for n in range(1, ns):
        k_sum = k_sum + k_s[n]
    k_place = rows(core * k_half + x * k_rows, k_rows)
    k_all[k_place, :] = k_sum * norm
    k5 = [send(k_all.at[k_place], k_all.at[k_place], peer) for peer in x_peers]
    for copy in k5:
        copy.wait_recv()
    k_mine = rows(core * k_half, k_half)
    k6 = send(k_all.at[k_mine], k_all.at[k_mine], sibling)

    for d in range(1, nx):
        seventh_a[d - 1].wait_recv()
        block = rows(core_base + lax.rem(x + nx - d, nx) * x_rows, x_rows)
        eighth.append(send(full.at[block], full.at[block], sibling))
    for d in range(1, ny):
        seventh_b[d - 1].wait_recv()
        block = rows(b_base + lax.rem(y + ny - d, ny) * y_rows, y_rows)
        eighth.append(send(full.at[block], full.at[block], sibling))

    k6.wait_recv()
    for h in range(HALVES):
        gk_ref[:, pl.ds(h * LANES, LANES)] = k_all[pl.ds(h * 64, TAPS * TAPS), :]
    for copy in eighth:
        copy.wait_recv()
    for copy in started:
        copy.wait_send()


def unpack_body(gf_in, gk_in, full, gf_ref, gk_ref, gwi_ref, gwo_ref, gwi, gwo, sem):
    copies = [
        pltpu.make_async_copy(gf_in, gf_ref, sem.at[0]),
        pltpu.make_async_copy(gk_in, gk_ref, sem.at[1]),
    ]
    for copy in copies:
        copy.start()
    for n in range(CHUNKS):
        for h in range(HALVES):
            j = HALVES * n + h
            gwi[pl.ds(0, C), pl.ds(j * LANES, LANES)] = full[pl.ds(j * C, C), :].astype(F32)
            gwo[pl.ds(n * CHUNK, CHUNK), pl.ds(h * LANES, LANES)] = full[
                pl.ds(HALF_ROWS + j * CHUNK, CHUNK), :
            ].astype(F32)
        for m, (src, dst) in enumerate(
            (
                (gwo.at[pl.ds(n * CHUNK, CHUNK)], gwo_ref.at[pl.ds(n * CHUNK, CHUNK)]),
                (
                    gwi.at[pl.ds(0, C), pl.ds(n * CHUNK, CHUNK)],
                    gwi_ref.at[pl.ds(0, C), pl.ds(n * CHUNK, CHUNK)],
                ),
            )
        ):
            copy = pltpu.make_async_copy(src, dst, sem.at[2 + 2 * n + m])
            copy.start()
            copies.append(copy)
    for copy in copies:
        copy.wait()


def body(sizes, features, cotangent, kernel, weight_in, weight_out, near, code):
    nx, nzlo, nzhi, ny, nq = sizes
    ns = nzlo * nzhi // nq
    x_rows = HALF_ROWS // 2 // nx
    y_rows = HALF_ROWS // 2 // ny
    last = HALF_ROWS // 2 // (nx * ny * nq)
    k_half = KROWS // 2
    k_rows = k_half // nx
    in_group = nx * nq - 1 + ny * nq - 1
    copies = 24 + 6 * (nx + ny) + 2 * in_group + ny * nq + 2 * ns
    vmem = pl.BlockSpec(memory_space=pltpu.VMEM)
    hbm = pl.BlockSpec(memory_space=pl.ANY)
    big = pl.BlockSpec(memory_space=pltpu.HBM)
    gf, gk, full = pl.pallas_call(
        functools.partial(kernel_body, sizes),
        out_shape=(
            jax.ShapeDtypeStruct((PIX, C), BF16),
            jax.ShapeDtypeStruct((TAPS * TAPS, C), F32),
            jax.ShapeDtypeStruct((2 * HALF_ROWS, LANES), BF16),
        ),
        in_specs=[big] * 7,
        out_specs=(vmem, vmem, vmem),
        scratch_shapes=[
            pltpu.SMEM((1, 4), jnp.int32),
            pltpu.SMEM((1, 4), jnp.int32),
            pltpu.VMEM((PIX, C), BF16),
            pltpu.VMEM((TAPS * TAPS, C), F32),
            pltpu.VMEM((C, HID), BF16),
            pltpu.VMEM((HID, C), BF16),
            pltpu.VMEM((3 * PIX, C), BF16),
            pltpu.VMEM((GRID, 3 * PIX), BF16),
            pltpu.VMEM((3 * PIX, GRID), BF16),
            pltpu.VMEM((HALVES, GRID, LANES), F32),
            pltpu.VMEM((HALVES, TAPS * TAPS * 8, LANES), F32),
            pltpu.VMEM((HALVES, PIX, LANES), F32),
            pltpu.VMEM((HALVES, PIX, LANES), F32),
            pltpu.VMEM((PIX, C), BF16),
            pltpu.VMEM((PIX, C), BF16),
            pltpu.VMEM((PIX, HID), F32),
            pltpu.VMEM((HALVES, PIX // 8 * DC_PITCH, LANES), F32),
            pltpu.VMEM((GRID, C), BF16),
            pltpu.VMEM((GRID, C), BF16),
            pltpu.VMEM((2, PIX, C), BF16),
            pltpu.VMEM((2, PIX, C), BF16),
            pltpu.VMEM((HALVES, TAPS * TAPS * 8, LANES), F32),
            pltpu.VMEM((2, HALF_ROWS, LANES), F32),
            pltpu.VMEM((2, HALF_ROWS, LANES), BF16),
            pltpu.VMEM((HALF_ROWS, LANES), BF16),
            pltpu.VMEM((HALF_ROWS, LANES), F32),
            pltpu.VMEM((HALF_ROWS, LANES), BF16),
            pltpu.VMEM((max(1, nx - 1) * x_rows + max(1, ny - 1) * y_rows, LANES), BF16),
            pltpu.VMEM((x_rows + y_rows, LANES), F32),
            pltpu.VMEM((x_rows + y_rows, LANES), BF16),
            pltpu.VMEM((in_group * last, LANES), BF16),
            pltpu.VMEM((ns, 2 * last, LANES), BF16),
            pltpu.VMEM((KROWS, LANES), F32),
            pltpu.VMEM((k_half, LANES), F32),
            pltpu.VMEM((k_half, LANES), F32),
            pltpu.VMEM((max(1, nx - 1), k_rows, LANES), F32),
            pltpu.VMEM((ny * nq, k_rows, LANES), F32),
            pltpu.VMEM((ns, k_rows, LANES), F32),
            pltpu.VMEM((KROWS, LANES), F32),
            pltpu.SemaphoreType.DMA((7,)),
            pltpu.SemaphoreType.DMA((copies,)),
            pltpu.SemaphoreType.DMA((copies,)),
        ],
        compiler_params=pltpu.CompilerParams(
            collective_id=0, has_side_effects=True, vmem_limit_bytes=40 << 20
        ),
        name="block_step",
    )(
        *(
            pltpu.with_memory_space_constraint(v, pltpu.HBM)
            for v in (
                near,
                code,
                features.reshape(PIX, C),
                cotangent.reshape(PIX, C),
                kernel,
                weight_in,
                weight_out,
            )
        ),
    )
    gf, gk, gwi, gwo = pl.pallas_call(
        unpack_body,
        out_shape=(
            jax.ShapeDtypeStruct((PIX, C), BF16),
            jax.ShapeDtypeStruct((TAPS * TAPS, C), F32),
            jax.ShapeDtypeStruct((C, HID), F32),
            jax.ShapeDtypeStruct((HID, C), F32),
        ),
        in_specs=[vmem, vmem, vmem],
        out_specs=(hbm, hbm, hbm, hbm),
        scratch_shapes=[
            pltpu.VMEM((C, HID), F32),
            pltpu.VMEM((HID, C), F32),
            pltpu.SemaphoreType.DMA((2 + 2 * CHUNKS,)),
        ],
        compiler_params=pltpu.CompilerParams(vmem_limit_bytes=12 << 20),
        name="unpack",
    )(gf, gk, full)
    return gf.reshape(1, 1, TILE, TILE, C), gk, gwi, gwo


def solution(mesh):
    sizes = FACTORS[(mesh.shape["tile"], mesh.shape["ens"])]
    in_specs = (
        P("ens", "tile", None, None, None),
        P("ens", "tile", None, None, None),
        P(),
        P(),
        P(),
        P("tile", None),
        P("tile", None),
    )
    out_specs = (P("ens", "tile", None, None, None), P(), P(), P())
    return jax.shard_map(
        functools.partial(body, sizes),
        mesh=mesh,
        in_specs=in_specs,
        out_specs=out_specs,
        check_vma=False,
    )
```

```python
import functools
import math

import jax
import jax.numpy as jnp
from jax import lax
from jax.experimental import pallas as pl
from jax.experimental.pallas import tpu as pltpu
from jax.sharding import PartitionSpec as P

C = 256
HID = 1024
TAPS = 7
HALO = 6
TILE = 16
PIX = TILE * TILE
LANES = 128
HALVES = C // LANES
OWN = 2 * PIX
BLOCK = 16 * 16
GRID = 4 * BLOCK
OUT_ROWS = 8
DC_PITCH = 24
CHUNK = 256
CHUNKS = HID // CHUNK
HALF_ROWS = C * HID // LANES
KROWS = 128
F32 = jnp.float32
BF16 = jnp.bfloat16
FACTORS = {(32, 16): (4, 8, 2, 4, 4), (4, 4): (1, 4, 1, 2, 2), (8, 2): (2, 4, 1, 1, 2)}


def source_pixels(index, offset, step_k, step_m):
    r = 2 * ((index >> 4) & 15) + (index >> 9) - HALO
    c = 2 * (index & 15) + ((index >> 8) & 1) - HALO
    r_in = (r >= 0) & (r < TILE)
    c_in = (c >= 0) & (c < TILE)
    found = jnp.where(r_in & c_in, OWN + TILE * r + c, -1)
    sides = (
        (c_in & (r < 0), -1 - r, c),
        (c_in & (r >= TILE) & (r < TILE + HALO), r - TILE, c),
        (r_in & (c < 0), -1 - c, r),
        (r_in & (c >= TILE) & (c < TILE + HALO), c - TILE, r),
    )
    for s, (mask, depth, along) in enumerate(sides):
        found = jnp.where(mask, offset[s] + step_k[s] * depth + step_m[s] * along, found)
    return found


def dot(a, b, contract=((1,), (0,))):
    return lax.dot_general(a, b, (contract, ((), ())), preferred_element_type=F32)


def kernel_body(
    sizes,
    near_hbm,
    code_hbm,
    x_hbm,
    cot_hbm,
    taps_hbm,
    w_in_hbm,
    w_out_hbm,
    gf_ref,
    gk_ref,
    full,
    near_ref,
    code_ref,
    cot_ref,
    taps_ref,
    w_in_ref,
    w_out_ref,
    tiles,
    gather,
    spread,
    padded,
    taps_b,
    conv,
    normed_f,
    normed_b,
    cot_p,
    d_hidden,
    d_conv,
    d_pad_hi,
    d_pad_lo,
    rim_send,
    rim_recv,
    own_grad,
    tap_acc,
    part,
    part_b,
    r0,
    half,
    s1,
    r1,
    t1,
    s2,
    r2,
    zs,
    kb,
    kr,
    kc,
    kr_x,
    k_q,
    k_s,
    k_all,
    local_sem,
    send_sem,
    recv_sem,
):
    nx, nzlo, nzhi, ny, nq = sizes
    nz = nzlo * nzhi
    ns = nz // nq
    tiles_n = nzlo * nx
    me_t = lax.axis_index("tile")
    me_e = lax.axis_index("ens")
    x = lax.rem(me_t, nx)
    zlo = lax.div(me_t, nx)
    core = lax.rem(me_e, 2)
    y = lax.rem(lax.div(me_e, 2), ny)
    zhi = lax.div(me_e, 2 * ny)
    z = zhi * nzlo + zlo
    q = lax.rem(z, nq)
    group = lax.div(z, nq)

    def at(tile, ens):
        return {"tile": tile, "ens": ens}

    def chip(x_at, y_at, z_at):
        return at(
            lax.rem(z_at, nzlo) * nx + x_at, (lax.div(z_at, nzlo) * ny + y_at) * 2 + core
        )

    before = at(lax.rem(me_t + tiles_n - 1, tiles_n), me_e)
    ahead = at(lax.rem(me_t + 1, tiles_n), me_e)
    sibling = at(me_t, me_e + 1 - 2 * core)
    xs = [lax.rem(x + d, nx) for d in range(1, nx)]
    ys = [lax.rem(y + d, ny) for d in range(1, ny)]
    x_peers = [chip(v, y, z) for v in xs]
    y_peers = [chip(x, v, z) for v in ys]
    yq_peers, xq_peers, only_q = [], [], []
    for d in range(max(nx, ny)):
        for dq in range(nq):
            if d == 0 and dq == 0:
                continue
            qv = lax.rem(q + dq, nq)
            if d < ny:
                yv = lax.rem(y + d, ny)
                yq_peers.append((chip(x, yv, group * nq + qv), yv * nq + qv))
            if 0 < d < nx or d == 0:
                xv = lax.rem(x + d, nx)
                xq_peers.append((chip(xv, y, group * nq + qv), xv * nq + qv))
            if d == 0:
                only_q.append(yq_peers[-1][0])
    far_peers = [chip(x, y, lax.rem(z + d * nq, nz)) for d in range(1, ns)]
    peers = [before, ahead, sibling, *far_peers, *only_q]
    peers += [peer for peer, _ in yq_peers[nq - 1 :]] + [peer for peer, _ in xq_peers[nq - 1 :]]

    barrier = pltpu.get_barrier_semaphore()
    for peer in peers:
        pl.semaphore_signal(
            barrier, inc=1, device_id=peer, device_id_type=pl.DeviceIdType.MESH
        )
    loads = [
        pltpu.make_async_copy(src, dst, local_sem.at[n])
        for n, (src, dst) in enumerate(
            (
                (near_hbm, near_ref),
                (code_hbm, code_ref),
                (x_hbm, tiles.at[pl.ds(OWN, PIX)]),
                (cot_hbm, cot_ref),
                (w_out_hbm, w_out_ref),
                (taps_hbm, taps_ref),
                (w_in_hbm, w_in_ref),
            )
        )
    ]
    for load in loads:
        load.start()
    pl.semaphore_wait(barrier, len(peers))

    started = []

    def send(src, dst, peer):
        n = len(started)
        copy = pltpu.make_async_remote_copy(
            src_ref=src,
            dst_ref=dst,
            send_sem=send_sem.at[n],
            recv_sem=recv_sem.at[n],
            device_id=peer,
            device_id_type=pl.DeviceIdType.MESH,
        )
        copy.start()
        started.append(copy)
        return copy

    def rows(start, size):
        return pl.ds(pl.multiple_of(start, size), size)

    halo = [
        send(x_hbm, tiles.at[pl.ds(PIX, PIX)], before),
        send(x_hbm, tiles.at[pl.ds(0, PIX)], ahead),
    ]

    for load in loads:
        load.wait()
    offset, step_k, step_m = [], [], []
    for s in range(4):
        code = code_ref[0, s]
        slot = lax.rem(2 * lax.rem(near_ref[0, s] - me_t + (tiles_n + 1), tiles_n), 3)
        edge = lax.rem(code, 4)
        flip = lax.div(code, 4)
        along_rows = lax.div(edge, 2)
        far = lax.rem(edge, 2)
        mult_k = TILE - (TILE - 1) * along_rows
        mult_m = 1 + (TILE - 1) * along_rows
        offset.append(slot * PIX + (TILE - 1) * (mult_k * far + mult_m * flip))
        step_k.append(mult_k * (1 - 2 * far))
        step_m.append(mult_m * (1 - 2 * flip))

    def one_hot(mask):
        return jnp.where(mask, 1.0, 0.0).astype(BF16)

    def fill_gather(i, _):
        cells = i * LANES + lax.broadcasted_iota(jnp.int32, (LANES, 1), 0)
        found = source_pixels(cells, offset, step_k, step_m)
        pixel = lax.broadcasted_iota(jnp.int32, (LANES, 3 * PIX), 1)
        gather[rows(i * LANES, LANES), :] = one_hot(found == pixel)
        return 0

    lax.fori_loop(0, GRID // LANES, fill_gather, 0)
    cells_row = lax.broadcasted_iota(jnp.int32, (1, GRID), 1)
    found_row = source_pixels(cells_row, offset, step_k, step_m)

    def fill_spread(i, _):
        pixel = i * 64 + lax.broadcasted_iota(jnp.int32, (64, GRID), 0)
        spread[rows(i * 64, 64), :] = one_hot(pixel == found_row)
        return 0

    lax.fori_loop(0, 3 * PIX // 64, fill_spread, 0)

    order = lax.broadcasted_iota(jnp.int32, (PIX, 1), 0)
    natural = (2 * ((order >> 3) & 7) + (order >> 7)) * TILE + 2 * (order & 7) + (
        (order >> 6) & 1
    )
    reorder = one_hot(natural == lax.broadcasted_iota(jnp.int32, (PIX, PIX), 1))
    cot_p[...] = dot(reorder, cot_ref[...]).astype(BF16)
    for n in range(CHUNKS):
        cols = pl.ds(n * CHUNK, CHUNK)
        d_hidden[:, cols] = dot(cot_p[...], w_out_ref[cols, :], ((1,), (1,)))
    for h in range(HALVES):
        lanes = pl.ds(h * LANES, LANES)
        for tap in range(TAPS * TAPS):
            taps_b[h, pl.ds(tap * 8, 8), :] = jnp.broadcast_to(
                taps_ref[pl.ds(tap, 1), lanes], (8, LANES)
            )
    d_conv[...] = jnp.zeros_like(d_conv)
    d_pad_hi[...] = jnp.zeros_like(d_pad_hi)
    d_pad_lo[...] = jnp.zeros_like(d_pad_lo)
    tap_acc[...] = jnp.zeros_like(tap_acc)
    kb[...] = jnp.zeros_like(kb)

    inner = [
        dot(gather[pl.ds(i * BLOCK, BLOCK), pl.ds(OWN, PIX)], tiles[pl.ds(OWN, PIX), :])
        for i in range(4)
    ]
    for i in range(4):
        for h in range(HALVES):
            padded[h, pl.ds(i * BLOCK, BLOCK), :] = inner[i][:, h * LANES : (h + 1) * LANES]

    for copy in halo:
        copy.wait_recv()
    for i in range(4):
        got = dot(gather[pl.ds(i * BLOCK, BLOCK), pl.ds(0, OWN)], tiles[pl.ds(0, OWN), :])
        for h in range(HALVES):
            padded[h, pl.ds(i * BLOCK, BLOCK), :] += got[:, h * LANES : (h + 1) * LANES]

    def conv_block(i, _):
        h, blk = lax.div(i, 4), lax.rem(i, 4)
        base = pl.multiple_of(blk * BLOCK, BLOCK)
        acc = [jnp.zeros((8, LANES), F32) for _ in range(OUT_ROWS)]
        for b in range(TAPS):
            weight = [taps_b[h, pl.ds((a * TAPS + b) * 8, 8), :] for a in range(TAPS)]
            for rr in range(OUT_ROWS + TAPS - 1):
                cell = padded[h, pl.ds(base + (rr * 16 + b), 8), :]
                for a in range(TAPS):
                    if 0 <= rr - a < OUT_ROWS:
                        acc[rr - a] += cell * weight[a]
        out = pl.multiple_of(blk * 64, 64)
        for ii in range(OUT_ROWS):
            conv[h, pl.ds(out + ii * 8, 8), :] = acc[ii]
        return 0

    lax.fori_loop(0, 4 * HALVES, conv_block, 0)

    c0, c1 = conv[0], conv[1]
    mean = jnp.sum(c0 + c1, axis=-1, keepdims=True) * (1.0 / C)
    c0, c1 = c0 - mean, c1 - mean
    var = jnp.sum(c0 * c0 + c1 * c1, axis=-1, keepdims=True) * (1.0 / C)
    inv_std = lax.rsqrt(var + 1e-06)
    for h, centred in enumerate((c0, c1)):
        scaled = centred * inv_std
        normed_f[h] = scaled
        normed_b[:, pl.ds(h * LANES, LANES)] = scaled.astype(BF16)

    x_rows = HALF_ROWS // 2 // nx
    y_rows = HALF_ROWS // 2 // ny
    last = HALF_ROWS // 2 // (nx * ny * nq)
    r1_y = (nx - 1) * x_rows

    def chip_sum(n):
        first[n].wait_recv()
        place = pl.ds(HALVES * n * CHUNK, HALVES * CHUNK)
        total = part[core, place, :] + r0[place, :].astype(F32)
        half[place, :] = total
        s1[place, :] = total.astype(BF16)

    root = math.sqrt(2.0 / math.pi)
    first = []
    d_normed = jnp.zeros((PIX, C), F32)
    for n in range(CHUNKS):
        cols = pl.ds(n * CHUNK, CHUNK)
        pre = dot(normed_b[...], w_in_ref[:, cols])
        square = pre * pre
        bent = jnp.tanh(root * pre * (1.0 + 0.044715 * square))
        up = 0.5 * (1.0 + bent)
        hidden = (pre * up).astype(BF16)
        slope = up + 0.5 * pre * (1.0 - bent * bent) * (
            root * (1.0 + 3 * 0.044715 * square)
        )
        d_pre = (d_hidden[:, cols] * slope).astype(BF16)
        got_in = dot(normed_b[...], d_pre, ((0,), (0,)))
        got_out = dot(hidden, cot_p[...], ((0,), (0,)))
        for side, got in enumerate((got_in, got_out)):
            for h in range(HALVES):
                piece = got[:, h * LANES : (h + 1) * LANES]
                place = pl.ds((HALVES * n + h) * CHUNK, CHUNK)
                part[side, place, :] = piece
                part_b[side, place, :] = piece.astype(BF16)
        place = pl.ds(HALVES * n * CHUNK, HALVES * CHUNK)
        first.append(send(part_b.at[1 - core, place], r0.at[place], sibling))
        d_normed = d_normed + dot(d_pre, w_in_ref[:, cols], ((1,), (1,)))
    for m in range(CHUNKS // 2):
        chip_sum(m)
    second_a = [
        send(
            s1.at[rows(xs[d - 1] * x_rows, x_rows)],
            r1.at[pl.ds((d - 1) * x_rows, x_rows)],
            x_peers[d - 1],
        )
        for d in range(1, nx)
    ]

    n0, n1 = normed_f[0], normed_f[1]
    d0, d1 = d_normed[:, :LANES], d_normed[:, LANES:]
    mean_d = jnp.sum(d0 + d1, axis=-1, keepdims=True) * (1.0 / C)
    mean_dn = jnp.sum(d0 * n0 + d1 * n1, axis=-1, keepdims=True) * (1.0 / C)
    for h, (d_half, n_half) in enumerate(((d0, n0), (d1, n1))):
        got = inv_std * (d_half - mean_d - n_half * mean_dn)
        for row in range(PIX // 8):
            d_conv[h, pl.ds(row * DC_PITCH + 8, 8), :] = got[row * 8 : row * 8 + 8]

    for m in range(CHUNKS // 2, CHUNKS):
        chip_sum(m)
    second_b = [
        send(
            s1.at[rows(HALF_ROWS // 2 + ys[d - 1] * y_rows, y_rows)],
            r1.at[pl.ds(r1_y + (d - 1) * y_rows, y_rows)],
            y_peers[d - 1],
        )
        for d in range(1, ny)
    ]

    def tap_block(i, _):
        h, blk = lax.div(i, 4), lax.rem(i, 4)
        base = pl.multiple_of(blk * BLOCK, BLOCK)
        dc_base = pl.multiple_of(blk * (OUT_ROWS * DC_PITCH), 8)
        grads = [
            d_conv[h, pl.ds(dc_base + (ii * DC_PITCH + 8), 8), :] for ii in range(OUT_ROWS)
        ]
        for b in range(TAPS):
            acc = [tap_acc[h, pl.ds((a * TAPS + b) * 8, 8), :] for a in range(TAPS)]
            for rr in range(OUT_ROWS + TAPS - 1):
                cell = padded[h, pl.ds(base + (rr * 16 + b), 8), :]
                for a in range(TAPS):
                    if 0 <= rr - a < OUT_ROWS:
                        acc[a] += cell * grads[rr - a]
            for a in range(TAPS):
                tap_acc[h, pl.ds((a * TAPS + b) * 8, 8), :] = acc[a]
        return 0

    lax.fori_loop(0, 4 * HALVES, tap_block, 0)
    for h in range(HALVES):
        kb[pl.ds(h * 64, TAPS * TAPS), :] = jnp.sum(
            tap_acc[h].reshape(TAPS * TAPS, 8, LANES), axis=1
        )
    k_half = KROWS // 2
    k_rows = k_half // nx
    k1 = send(kb.at[rows((1 - core) * k_half, k_half)], kr, sibling)

    for copy in second_a:
        copy.wait_recv()
    got_a = half[rows(x * x_rows, x_rows), :]
    for d in range(1, nx):
        got_a = got_a + r1[pl.ds((d - 1) * x_rows, x_rows), :].astype(F32)
    t1[pl.ds(0, x_rows), :] = got_a
    s2[pl.ds(0, x_rows), :] = got_a.astype(BF16)
    third = [
        send(s2.at[rows(place * last, last)], r2.at[pl.ds(n * last, last)], peer)
        for n, (peer, place) in enumerate(yq_peers)
    ]
    for copy in second_b:
        copy.wait_recv()
    got_b = half[rows(HALF_ROWS // 2 + y * y_rows, y_rows), :]
    for d in range(1, ny):
        got_b = got_b + r1[pl.ds(r1_y + (d - 1) * y_rows, y_rows), :].astype(F32)
    t1[pl.ds(x_rows, y_rows), :] = got_b
    s2[pl.ds(x_rows, y_rows), :] = got_b.astype(BF16)
    r2_x = len(yq_peers) * last
    third += [
        send(
            s2.at[rows(x_rows + place * last, last)],
            r2.at[pl.ds(r2_x + n * last, last)],
            peer,
        )
        for n, (peer, place) in enumerate(xq_peers)
    ]

    def back_block(i, _):
        h, blk = lax.div(i, 4), lax.rem(i, 4)
        base = pl.multiple_of(blk * (OUT_ROWS * DC_PITCH), 8)
        acc = [
            [jnp.zeros((8, LANES), F32) for _ in range(2)]
            for _ in range(OUT_ROWS + TAPS - 1)
        ]
        for b in range(TAPS):
            weight = [taps_b[h, pl.ds((a * TAPS + b) * 8, 8), :] for a in range(TAPS)]
            for ii in range(OUT_ROWS):
                cells = [
                    d_conv[h, pl.ds(base + (ii * DC_PITCH + 8 * (v + 1) - b), 8), :]
                    for v in range(2)
                ]
                for a in range(TAPS):
                    for v in range(2):
                        acc[ii + a][v] += cells[v] * weight[a]
        lanes = rows(h * LANES, LANES)
        out = pl.multiple_of(blk * BLOCK, BLOCK)
        for rr in range(OUT_ROWS + TAPS - 1):
            row = jnp.concatenate(acc[rr], axis=0)
            high = row.astype(BF16)
            d_pad_hi[pl.ds(out + rr * 16, 16), lanes] = high
            d_pad_lo[pl.ds(out + rr * 16, 16), lanes] = (row - high.astype(F32)).astype(
                BF16
            )
        return 0

    lax.fori_loop(0, 4 * HALVES, back_block, 0)
    rim = []
    for slot, peer in enumerate((before, ahead)):
        rim_send[slot] = dot(spread[pl.ds(slot * PIX, PIX), :], d_pad_hi[...]).astype(
            BF16
        )
        rim.append(send(rim_send.at[slot], rim_recv.at[slot], peer))

    k1.wait_recv()
    kc[...] = kb[rows(core * k_half, k_half), :] + kr[...]
    k2 = [
        send(kc.at[rows(xs[d - 1] * k_rows, k_rows)], kr_x.at[d - 1], x_peers[d - 1])
        for d in range(1, nx)
    ]

    norm = 1.0 / math.sqrt(PIX * tiles_n * nzhi * ny * 2)
    for copy in third:
        copy.wait_recv()
    place_y = y * nq + q
    place_x = x * nq + q
    got_a = t1[rows(place_y * last, last), :]
    for n in range(len(yq_peers)):
        got_a = got_a + r2[pl.ds(n * last, last), :].astype(F32)
    got_b = t1[rows(x_rows + place_x * last, last), :]
    for n in range(len(xq_peers)):
        got_b = got_b + r2[pl.ds(r2_x + n * last, last), :].astype(F32)
    zs[group, pl.ds(0, last), :] = got_a.astype(BF16)
    zs[group, pl.ds(last, last), :] = got_b.astype(BF16)
    fourth = [send(zs.at[group], zs.at[group], peer) for peer in far_peers]

    own = spread[pl.ds(OWN, PIX), :]
    own_grad[...] = dot(own, d_pad_hi[...]) + dot(own, d_pad_lo[...])
    for copy in k2:
        copy.wait_recv()
    k_sum = kc[rows(x * k_rows, k_rows), :]
    for d in range(1, nx):
        k_sum = k_sum + kr_x[d - 1]
    k_q[place_y] = k_sum
    k3 = [send(k_q.at[place_y], k_q.at[place_y], peer) for peer, _ in yq_peers]

    for copy in fourth:
        copy.wait_recv()
    total = zs[0].astype(F32)
    for n in range(1, ns):
        total = total + zs[n].astype(F32)
    total = (total * norm).astype(BF16)
    core_base = core * HALF_ROWS
    b_base = core_base + HALF_ROWS // 2
    place_a = rows(core_base + x * x_rows + place_y * last, last)
    place_b = rows(b_base + y * y_rows + place_x * last, last)
    full[place_a, :] = total[:last]
    full[place_b, :] = total[last:]
    fifth_a = [send(full.at[place_a], full.at[place_a], peer) for peer, _ in yq_peers]
    fifth_b = [send(full.at[place_b], full.at[place_b], peer) for peer, _ in xq_peers]

    for copy in k3:
        copy.wait_recv()
    k_sum = k_q[0]
    for n in range(1, ny * nq):
        k_sum = k_sum + k_q[n]
    k_s[group] = k_sum
    k4 = [send(k_s.at[group], k_s.at[group], peer) for peer in far_peers]

    block_a = rows(core_base + x * x_rows, x_rows)
    block_b = rows(b_base + y * y_rows, y_rows)
    for copy in fifth_a:
        copy.wait_recv()
    seventh_a = [send(full.at[block_a], full.at[block_a], peer) for peer in x_peers]
    for copy in fifth_b:
        copy.wait_recv()
    seventh_b = [send(full.at[block_b], full.at[block_b], peer) for peer in y_peers]
    eighth = [send(full.at[block], full.at[block], sibling) for block in (block_a, block_b)]

    for copy in rim:
        copy.wait_recv()
    gf_ref[...] = (
        cot_ref[...].astype(F32)
        + own_grad[...]
        + rim_recv[0].astype(F32)
        + rim_recv[1].astype(F32)
    ).astype(BF16)

    for copy in k4:
        copy.wait_recv()
    k_sum = k_s[0]
    for n in range(1, ns):
        k_sum = k_sum + k_s[n]
    k_place = rows(core * k_half + x * k_rows, k_rows)
    k_all[k_place, :] = k_sum * norm
    k5 = [send(k_all.at[k_place], k_all.at[k_place], peer) for peer in x_peers]
    for copy in k5:
        copy.wait_recv()
    k_mine = rows(core * k_half, k_half)
    k6 = send(k_all.at[k_mine], k_all.at[k_mine], sibling)

    for d in range(1, nx):
        seventh_a[d - 1].wait_recv()
        block = rows(core_base + lax.rem(x + nx - d, nx) * x_rows, x_rows)
        eighth.append(send(full.at[block], full.at[block], sibling))
    for d in range(1, ny):
        seventh_b[d - 1].wait_recv()
        block = rows(b_base + lax.rem(y + ny - d, ny) * y_rows, y_rows)
        eighth.append(send(full.at[block], full.at[block], sibling))

    k6.wait_recv()
    for h in range(HALVES):
        gk_ref[:, pl.ds(h * LANES, LANES)] = k_all[pl.ds(h * 64, TAPS * TAPS), :]
    for copy in eighth:
        copy.wait_recv()
    for copy in started:
        copy.wait_send()


def unpack_body(gf_in, gk_in, full, gf_ref, gk_ref, gwi_ref, gwo_ref, gwi, gwo, sem):
    copies = [
        pltpu.make_async_copy(gf_in, gf_ref, sem.at[0]),
        pltpu.make_async_copy(gk_in, gk_ref, sem.at[1]),
    ]
    for copy in copies:
        copy.start()
    for n in range(CHUNKS):
        for h in range(HALVES):
            j = HALVES * n + h
            gwi[pl.ds(0, C), pl.ds(j * LANES, LANES)] = full[pl.ds(j * C, C), :].astype(F32)
            gwo[pl.ds(n * CHUNK, CHUNK), pl.ds(h * LANES, LANES)] = full[
                pl.ds(HALF_ROWS + j * CHUNK, CHUNK), :
            ].astype(F32)
        for m, (src, dst) in enumerate(
            (
                (gwo.at[pl.ds(n * CHUNK, CHUNK)], gwo_ref.at[pl.ds(n * CHUNK, CHUNK)]),
                (
                    gwi.at[pl.ds(0, C), pl.ds(n * CHUNK, CHUNK)],
                    gwi_ref.at[pl.ds(0, C), pl.ds(n * CHUNK, CHUNK)],
                ),
            )
        ):
            copy = pltpu.make_async_copy(src, dst, sem.at[2 + 2 * n + m])
            copy.start()
            copies.append(copy)
    for copy in copies:
        copy.wait()


def body(sizes, features, cotangent, kernel, weight_in, weight_out, near, code):
    nx, nzlo, nzhi, ny, nq = sizes
    ns = nzlo * nzhi // nq
    x_rows = HALF_ROWS // 2 // nx
    y_rows = HALF_ROWS // 2 // ny
    last = HALF_ROWS // 2 // (nx * ny * nq)
    k_half = KROWS // 2
    k_rows = k_half // nx
    in_group = nx * nq - 1 + ny * nq - 1
    copies = 24 + 6 * (nx + ny) + 2 * in_group + ny * nq + 2 * ns
    vmem = pl.BlockSpec(memory_space=pltpu.VMEM)
    hbm = pl.BlockSpec(memory_space=pl.ANY)
    big = pl.BlockSpec(memory_space=pltpu.HBM)
    gf, gk, full = pl.pallas_call(
        functools.partial(kernel_body, sizes),
        out_shape=(
            jax.ShapeDtypeStruct((PIX, C), BF16),
            jax.ShapeDtypeStruct((TAPS * TAPS, C), F32),
            jax.ShapeDtypeStruct((2 * HALF_ROWS, LANES), BF16),
        ),
        in_specs=[big] * 7,
        out_specs=(vmem, vmem, vmem),
        scratch_shapes=[
            pltpu.SMEM((1, 4), jnp.int32),
            pltpu.SMEM((1, 4), jnp.int32),
            pltpu.VMEM((PIX, C), BF16),
            pltpu.VMEM((TAPS * TAPS, C), F32),
            pltpu.VMEM((C, HID), BF16),
            pltpu.VMEM((HID, C), BF16),
            pltpu.VMEM((3 * PIX, C), BF16),
            pltpu.VMEM((GRID, 3 * PIX), BF16),
            pltpu.VMEM((3 * PIX, GRID), BF16),
            pltpu.VMEM((HALVES, GRID, LANES), F32),
            pltpu.VMEM((HALVES, TAPS * TAPS * 8, LANES), F32),
            pltpu.VMEM((HALVES, PIX, LANES), F32),
            pltpu.VMEM((HALVES, PIX, LANES), F32),
            pltpu.VMEM((PIX, C), BF16),
            pltpu.VMEM((PIX, C), BF16),
            pltpu.VMEM((PIX, HID), F32),
            pltpu.VMEM((HALVES, PIX // 8 * DC_PITCH, LANES), F32),
            pltpu.VMEM((GRID, C), BF16),
            pltpu.VMEM((GRID, C), BF16),
            pltpu.VMEM((2, PIX, C), BF16),
            pltpu.VMEM((2, PIX, C), BF16),
            pltpu.VMEM((PIX, C), F32),
            pltpu.VMEM((HALVES, TAPS * TAPS * 8, LANES), F32),
            pltpu.VMEM((2, HALF_ROWS, LANES), F32),
            pltpu.VMEM((2, HALF_ROWS, LANES), BF16),
            pltpu.VMEM((HALF_ROWS, LANES), BF16),
            pltpu.VMEM((HALF_ROWS, LANES), F32),
            pltpu.VMEM((HALF_ROWS, LANES), BF16),
            pltpu.VMEM((max(1, nx - 1) * x_rows + max(1, ny - 1) * y_rows, LANES), BF16),
            pltpu.VMEM((x_rows + y_rows, LANES), F32),
            pltpu.VMEM((x_rows + y_rows, LANES), BF16),
            pltpu.VMEM((in_group * last, LANES), BF16),
            pltpu.VMEM((ns, 2 * last, LANES), BF16),
            pltpu.VMEM((KROWS, LANES), F32),
            pltpu.VMEM((k_half, LANES), F32),
            pltpu.VMEM((k_half, LANES), F32),
            pltpu.VMEM((max(1, nx - 1), k_rows, LANES), F32),
            pltpu.VMEM((ny * nq, k_rows, LANES), F32),
            pltpu.VMEM((ns, k_rows, LANES), F32),
            pltpu.VMEM((KROWS, LANES), F32),
            pltpu.SemaphoreType.DMA((7,)),
            pltpu.SemaphoreType.DMA((copies,)),
            pltpu.SemaphoreType.DMA((copies,)),
        ],
        compiler_params=pltpu.CompilerParams(
            collective_id=0, has_side_effects=True, vmem_limit_bytes=40 << 20
        ),
        name="block_step",
    )(
        *(
            pltpu.with_memory_space_constraint(v, pltpu.HBM)
            for v in (
                near,
                code,
                features.reshape(PIX, C),
                cotangent.reshape(PIX, C),
                kernel,
                weight_in,
                weight_out,
            )
        ),
    )
    gf, gk, gwi, gwo = pl.pallas_call(
        unpack_body,
        out_shape=(
            jax.ShapeDtypeStruct((PIX, C), BF16),
            jax.ShapeDtypeStruct((TAPS * TAPS, C), F32),
            jax.ShapeDtypeStruct((C, HID), F32),
            jax.ShapeDtypeStruct((HID, C), F32),
        ),
        in_specs=[vmem, vmem, vmem],
        out_specs=(hbm, hbm, hbm, hbm),
        scratch_shapes=[
            pltpu.VMEM((C, HID), F32),
            pltpu.VMEM((HID, C), F32),
            pltpu.SemaphoreType.DMA((2 + 2 * CHUNKS,)),
        ],
        compiler_params=pltpu.CompilerParams(vmem_limit_bytes=12 << 20),
        name="unpack",
    )(gf, gk, full)
    return gf.reshape(1, 1, TILE, TILE, C), gk, gwi, gwo


def solution(mesh):
    sizes = FACTORS[(mesh.shape["tile"], mesh.shape["ens"])]
    in_specs = (
        P("ens", "tile", None, None, None),
        P("ens", "tile", None, None, None),
        P(),
        P(),
        P(),
        P("tile", None),
        P("tile", None),
    )
    out_specs = (P("ens", "tile", None, None, None), P(), P(), P())
    return jax.shard_map(
        functools.partial(body, sizes),
        mesh=mesh,
        in_specs=in_specs,
        out_specs=out_specs,
        check_vma=False,
    )
```

```python
import functools
import math

import jax
import jax.numpy as jnp
from jax import lax
from jax.experimental import pallas as pl
from jax.experimental.pallas import tpu as pltpu
from jax.sharding import PartitionSpec as P

C = 256
HID = 1024
TAPS = 7
HALO = 6
TILE = 16
PIX = TILE * TILE
LANES = 128
HALVES = C // LANES
OWN = 2 * PIX
BLOCK = 16 * 16
GRID = 4 * BLOCK
OUT_ROWS = 8
DC_PITCH = 24
CHUNK = 256
CHUNKS = HID // CHUNK
HALF_ROWS = C * HID // LANES
KROWS = 128
F32 = jnp.float32
BF16 = jnp.bfloat16
FACTORS = {(32, 16): (4, 8, 2, 4, 4), (4, 4): (1, 4, 1, 2, 2), (8, 2): (2, 4, 1, 1, 2)}


def source_pixels(index, offset, step_k, step_m):
    r = 2 * ((index >> 4) & 15) + (index >> 9) - HALO
    c = 2 * (index & 15) + ((index >> 8) & 1) - HALO
    r_in = (r >= 0) & (r < TILE)
    c_in = (c >= 0) & (c < TILE)
    found = jnp.where(r_in & c_in, OWN + TILE * r + c, -1)
    sides = (
        (c_in & (r < 0), -1 - r, c),
        (c_in & (r >= TILE) & (r < TILE + HALO), r - TILE, c),
        (r_in & (c < 0), -1 - c, r),
        (r_in & (c >= TILE) & (c < TILE + HALO), c - TILE, r),
    )
    for s, (mask, depth, along) in enumerate(sides):
        found = jnp.where(mask, offset[s] + step_k[s] * depth + step_m[s] * along, found)
    return found


def far_first(n):
    return sorted(range(1, n), key=lambda d: -min(d, n - d))


def dot(a, b, contract=((1,), (0,))):
    return lax.dot_general(a, b, (contract, ((), ())), preferred_element_type=F32)


def kernel_body(
    sizes,
    near_hbm,
    code_hbm,
    x_hbm,
    cot_hbm,
    taps_hbm,
    w_in_hbm,
    w_out_hbm,
    gf_ref,
    gk_ref,
    full,
    near_ref,
    code_ref,
    cot_ref,
    taps_ref,
    w_in_ref,
    w_out_ref,
    tiles,
    gather,
    spread,
    padded,
    taps_b,
    conv,
    normed_f,
    normed_b,
    cot_p,
    d_hidden,
    d_conv,
    d_pad_hi,
    d_pad_lo,
    rim_send,
    rim_recv,
    own_grad,
    tap_acc,
    part,
    part_b,
    r0,
    half,
    s1,
    r1,
    t1,
    s2,
    r2,
    zs,
    kb,
    kr,
    kc,
    kr_x,
    k_q,
    k_s,
    k_all,
    local_sem,
    send_sem,
    recv_sem,
):
    nx, nzlo, nzhi, ny, nq = sizes
    nz = nzlo * nzhi
    ns = nz // nq
    tiles_n = nzlo * nx
    me_t = lax.axis_index("tile")
    me_e = lax.axis_index("ens")
    x = lax.rem(me_t, nx)
    zlo = lax.div(me_t, nx)
    core = lax.rem(me_e, 2)
    y = lax.rem(lax.div(me_e, 2), ny)
    zhi = lax.div(me_e, 2 * ny)
    z = zhi * nzlo + zlo
    q = lax.rem(z, nq)
    group = lax.div(z, nq)

    def at(tile, ens):
        return {"tile": tile, "ens": ens}

    def chip(x_at, y_at, z_at):
        return at(
            lax.rem(z_at, nzlo) * nx + x_at, (lax.div(z_at, nzlo) * ny + y_at) * 2 + core
        )

    before = at(lax.rem(me_t + tiles_n - 1, tiles_n), me_e)
    ahead = at(lax.rem(me_t + 1, tiles_n), me_e)
    sibling = at(me_t, me_e + 1 - 2 * core)
    x_steps, y_steps, far_steps = far_first(nx), far_first(ny), far_first(ns)
    xs = [lax.rem(x + d, nx) for d in x_steps]
    ys = [lax.rem(y + d, ny) for d in y_steps]
    x_peers = [chip(v, y, z) for v in xs]
    y_peers = [chip(x, v, z) for v in ys]
    yq_peers, xq_peers, only_q = [], [], []
    for d in range(max(nx, ny)):
        for dq in range(nq):
            if d == 0 and dq == 0:
                continue
            qv = lax.rem(q + dq, nq)
            if d < ny:
                yv = lax.rem(y + d, ny)
                yq_peers.append((chip(x, yv, group * nq + qv), yv * nq + qv, (d, dq, ny)))
            if 0 < d < nx or d == 0:
                xv = lax.rem(x + d, nx)
                xq_peers.append((chip(xv, y, group * nq + qv), xv * nq + qv, (d, dq, nx)))
            if d == 0:
                only_q.append(yq_peers[-1][0])
    far_peers = [chip(x, y, lax.rem(z + d * nq, nz)) for d in far_steps]
    peers = [before, ahead, sibling, *far_peers, *only_q]
    peers += [pair[0] for pair in yq_peers[nq - 1 :] + xq_peers[nq - 1 :]]

    def reach(pair):
        d, dq, n = pair[2]
        return -min(d, n - d) - min(dq, nq - dq)

    yq_peers = [pair[:2] for pair in sorted(yq_peers, key=reach)]
    xq_peers = [pair[:2] for pair in sorted(xq_peers, key=reach)]

    barrier = pltpu.get_barrier_semaphore()
    for peer in peers:
        pl.semaphore_signal(
            barrier, inc=1, device_id=peer, device_id_type=pl.DeviceIdType.MESH
        )
    loads = [
        pltpu.make_async_copy(src, dst, local_sem.at[n])
        for n, (src, dst) in enumerate(
            (
                (x_hbm, tiles.at[pl.ds(OWN, PIX)]),
                (near_hbm, near_ref),
                (code_hbm, code_ref),
                (cot_hbm, cot_ref),
                (w_out_hbm, w_out_ref),
                (taps_hbm, taps_ref),
                (w_in_hbm, w_in_ref),
            )
        )
    ]
    for load in loads:
        load.start()
    loads[0].wait()
    pl.semaphore_wait(barrier, len(peers))

    started = []

    def send(src, dst, peer):
        n = len(started)
        copy = pltpu.make_async_remote_copy(
            src_ref=src,
            dst_ref=dst,
            send_sem=send_sem.at[n],
            recv_sem=recv_sem.at[n],
            device_id=peer,
            device_id_type=pl.DeviceIdType.MESH,
        )
        copy.start()
        started.append(copy)
        return copy

    def rows(start, size):
        return pl.ds(pl.multiple_of(start, size), size)

    halo = [
        send(tiles.at[pl.ds(OWN, PIX)], tiles.at[pl.ds(PIX, PIX)], before),
        send(tiles.at[pl.ds(OWN, PIX)], tiles.at[pl.ds(0, PIX)], ahead),
    ]

    for load in loads[1:]:
        load.wait()
    offset, step_k, step_m = [], [], []
    for s in range(4):
        code = code_ref[0, s]
        slot = lax.rem(2 * lax.rem(near_ref[0, s] - me_t + (tiles_n + 1), tiles_n), 3)
        edge = lax.rem(code, 4)
        flip = lax.div(code, 4)
        along_rows = lax.div(edge, 2)
        far = lax.rem(edge, 2)
        mult_k = TILE - (TILE - 1) * along_rows
        mult_m = 1 + (TILE - 1) * along_rows
        offset.append(slot * PIX + (TILE - 1) * (mult_k * far + mult_m * flip))
        step_k.append(mult_k * (1 - 2 * far))
        step_m.append(mult_m * (1 - 2 * flip))

    def one_hot(mask):
        return jnp.where(mask, 1.0, 0.0).astype(BF16)

    def fill_gather(i, _):
        cells = i * LANES + lax.broadcasted_iota(jnp.int32, (LANES, 1), 0)
        found = source_pixels(cells, offset, step_k, step_m)
        pixel = lax.broadcasted_iota(jnp.int32, (LANES, 3 * PIX), 1)
        gather[rows(i * LANES, LANES), :] = one_hot(found == pixel)
        return 0

    lax.fori_loop(0, GRID // LANES, fill_gather, 0)
    cells_row = lax.broadcasted_iota(jnp.int32, (1, GRID), 1)
    found_row = source_pixels(cells_row, offset, step_k, step_m)

    def fill_spread(i, _):
        pixel = i * 64 + lax.broadcasted_iota(jnp.int32, (64, GRID), 0)
        spread[rows(i * 64, 64), :] = one_hot(pixel == found_row)
        return 0

    lax.fori_loop(0, 3 * PIX // 64, fill_spread, 0)

    order = lax.broadcasted_iota(jnp.int32, (PIX, 1), 0)
    natural = (2 * ((order >> 3) & 7) + (order >> 7)) * TILE + 2 * (order & 7) + (
        (order >> 6) & 1
    )
    reorder = one_hot(natural == lax.broadcasted_iota(jnp.int32, (PIX, PIX), 1))
    cot_p[...] = dot(reorder, cot_ref[...]).astype(BF16)
    for n in range(CHUNKS):
        cols = pl.ds(n * CHUNK, CHUNK)
        d_hidden[:, cols] = dot(cot_p[...], w_out_ref[cols, :], ((1,), (1,)))
    for h in range(HALVES):
        lanes = pl.ds(h * LANES, LANES)
        for tap in range(TAPS * TAPS):
            taps_b[h, pl.ds(tap * 8, 8), :] = jnp.broadcast_to(
                taps_ref[pl.ds(tap, 1), lanes], (8, LANES)
            )
    d_conv[...] = jnp.zeros_like(d_conv)
    d_pad_hi[...] = jnp.zeros_like(d_pad_hi)
    d_pad_lo[...] = jnp.zeros_like(d_pad_lo)
    tap_acc[...] = jnp.zeros_like(tap_acc)
    kb[...] = jnp.zeros_like(kb)

    inner = [
        dot(gather[pl.ds(i * BLOCK, BLOCK), pl.ds(OWN, PIX)], tiles[pl.ds(OWN, PIX), :])
        for i in range(4)
    ]
    for i in range(4):
        for h in range(HALVES):
            padded[h, pl.ds(i * BLOCK, BLOCK), :] = inner[i][:, h * LANES : (h + 1) * LANES]

    for copy in halo:
        copy.wait_recv()
    for i in range(4):
        got = dot(gather[pl.ds(i * BLOCK, BLOCK), pl.ds(0, OWN)], tiles[pl.ds(0, OWN), :])
        for h in range(HALVES):
            padded[h, pl.ds(i * BLOCK, BLOCK), :] += got[:, h * LANES : (h + 1) * LANES]

    def conv_block(i, _):
        h, blk = lax.div(i, 4), lax.rem(i, 4)
        base = pl.multiple_of(blk * BLOCK, BLOCK)
        acc = [jnp.zeros((8, LANES), F32) for _ in range(OUT_ROWS)]
        for b in range(TAPS):
            weight = [taps_b[h, pl.ds((a * TAPS + b) * 8, 8), :] for a in range(TAPS)]
            for rr in range(OUT_ROWS + TAPS - 1):
                cell = padded[h, pl.ds(base + (rr * 16 + b), 8), :]
                for a in range(TAPS):
                    if 0 <= rr - a < OUT_ROWS:
                        acc[rr - a] += cell * weight[a]
        out = pl.multiple_of(blk * 64, 64)
        for ii in range(OUT_ROWS):
            conv[h, pl.ds(out + ii * 8, 8), :] = acc[ii]
        return 0

    lax.fori_loop(0, 4 * HALVES, conv_block, 0)

    c0, c1 = conv[0], conv[1]
    mean = jnp.sum(c0 + c1, axis=-1, keepdims=True) * (1.0 / C)
    c0, c1 = c0 - mean, c1 - mean
    var = jnp.sum(c0 * c0 + c1 * c1, axis=-1, keepdims=True) * (1.0 / C)
    inv_std = lax.rsqrt(var + 1e-06)
    for h, centred in enumerate((c0, c1)):
        scaled = centred * inv_std
        normed_f[h] = scaled
        normed_b[:, pl.ds(h * LANES, LANES)] = scaled.astype(BF16)

    x_rows = HALF_ROWS // 2 // nx
    y_rows = HALF_ROWS // 2 // ny
    last = HALF_ROWS // 2 // (nx * ny * nq)
    r1_y = (nx - 1) * x_rows

    def chip_sum(n):
        first[n].wait_recv()
        place = pl.ds(HALVES * n * CHUNK, HALVES * CHUNK)
        total = part[core, place, :] + r0[place, :].astype(F32)
        half[place, :] = total
        s1[place, :] = total.astype(BF16)

    root = math.sqrt(2.0 / math.pi)
    first = []
    d_normed = jnp.zeros((PIX, C), F32)
    for n in range(CHUNKS):
        cols = pl.ds(n * CHUNK, CHUNK)
        pre = dot(normed_b[...], w_in_ref[:, cols])
        square = pre * pre
        bent = jnp.tanh(root * pre * (1.0 + 0.044715 * square))
        up = 0.5 * (1.0 + bent)
        hidden = (pre * up).astype(BF16)
        slope = up + 0.5 * pre * (1.0 - bent * bent) * (
            root * (1.0 + 3 * 0.044715 * square)
        )
        d_pre = (d_hidden[:, cols] * slope).astype(BF16)
        got_in = dot(normed_b[...], d_pre, ((0,), (0,)))
        got_out = dot(hidden, cot_p[...], ((0,), (0,)))
        for side, got in enumerate((got_in, got_out)):
            for h in range(HALVES):
                piece = got[:, h * LANES : (h + 1) * LANES]
                place = pl.ds((HALVES * n + h) * CHUNK, CHUNK)
                part[side, place, :] = piece
                part_b[side, place, :] = piece.astype(BF16)
        place = pl.ds(HALVES * n * CHUNK, HALVES * CHUNK)
        first.append(send(part_b.at[1 - core, place], r0.at[place], sibling))
        d_normed = d_normed + dot(d_pre, w_in_ref[:, cols], ((1,), (1,)))
    for m in range(CHUNKS // 2):
        chip_sum(m)
    second_a = [
        send(
            s1.at[rows(xs[d - 1] * x_rows, x_rows)],
            r1.at[pl.ds((d - 1) * x_rows, x_rows)],
            x_peers[d - 1],
        )
        for d in range(1, nx)
    ]

    n0, n1 = normed_f[0], normed_f[1]
    d0, d1 = d_normed[:, :LANES], d_normed[:, LANES:]
    mean_d = jnp.sum(d0 + d1, axis=-1, keepdims=True) * (1.0 / C)
    mean_dn = jnp.sum(d0 * n0 + d1 * n1, axis=-1, keepdims=True) * (1.0 / C)
    for h, (d_half, n_half) in enumerate(((d0, n0), (d1, n1))):
        got = inv_std * (d_half - mean_d - n_half * mean_dn)
        for row in range(PIX // 8):
            d_conv[h, pl.ds(row * DC_PITCH + 8, 8), :] = got[row * 8 : row * 8 + 8]

    for m in range(CHUNKS // 2, CHUNKS):
        chip_sum(m)
    second_b = [
        send(
            s1.at[rows(HALF_ROWS // 2 + ys[d - 1] * y_rows, y_rows)],
            r1.at[pl.ds(r1_y + (d - 1) * y_rows, y_rows)],
            y_peers[d - 1],
        )
        for d in range(1, ny)
    ]

    def tap_block(i, _):
        h, blk = lax.div(i, 4), lax.rem(i, 4)
        base = pl.multiple_of(blk * BLOCK, BLOCK)
        dc_base = pl.multiple_of(blk * (OUT_ROWS * DC_PITCH), 8)
        grads = [
            d_conv[h, pl.ds(dc_base + (ii * DC_PITCH + 8), 8), :] for ii in range(OUT_ROWS)
        ]
        for b in range(TAPS):
            acc = [tap_acc[h, pl.ds((a * TAPS + b) * 8, 8), :] for a in range(TAPS)]
            for rr in range(OUT_ROWS + TAPS - 1):
                cell = padded[h, pl.ds(base + (rr * 16 + b), 8), :]
                for a in range(TAPS):
                    if 0 <= rr - a < OUT_ROWS:
                        acc[a] += cell * grads[rr - a]
            for a in range(TAPS):
                tap_acc[h, pl.ds((a * TAPS + b) * 8, 8), :] = acc[a]
        return 0

    lax.fori_loop(0, 4 * HALVES, tap_block, 0)
    for h in range(HALVES):
        kb[pl.ds(h * 64, TAPS * TAPS), :] = jnp.sum(
            tap_acc[h].reshape(TAPS * TAPS, 8, LANES), axis=1
        )
    k_half = KROWS // 2
    k_rows = k_half // nx
    k1 = send(kb.at[rows((1 - core) * k_half, k_half)], kr, sibling)

    for copy in second_a:
        copy.wait_recv()
    got_a = half[rows(x * x_rows, x_rows), :]
    for d in range(1, nx):
        got_a = got_a + r1[pl.ds((d - 1) * x_rows, x_rows), :].astype(F32)
    t1[pl.ds(0, x_rows), :] = got_a
    s2[pl.ds(0, x_rows), :] = got_a.astype(BF16)
    third = [
        send(s2.at[rows(place * last, last)], r2.at[pl.ds(n * last, last)], peer)
        for n, (peer, place) in enumerate(yq_peers)
    ]
    for copy in second_b:
        copy.wait_recv()
    got_b = half[rows(HALF_ROWS // 2 + y * y_rows, y_rows), :]
    for d in range(1, ny):
        got_b = got_b + r1[pl.ds(r1_y + (d - 1) * y_rows, y_rows), :].astype(F32)
    t1[pl.ds(x_rows, y_rows), :] = got_b
    s2[pl.ds(x_rows, y_rows), :] = got_b.astype(BF16)
    r2_x = len(yq_peers) * last
    third += [
        send(
            s2.at[rows(x_rows + place * last, last)],
            r2.at[pl.ds(r2_x + n * last, last)],
            peer,
        )
        for n, (peer, place) in enumerate(xq_peers)
    ]

    def back_block(i, _):
        h, blk = lax.div(i, 4), lax.rem(i, 4)
        base = pl.multiple_of(blk * (OUT_ROWS * DC_PITCH), 8)
        acc = [
            [jnp.zeros((8, LANES), F32) for _ in range(2)]
            for _ in range(OUT_ROWS + TAPS - 1)
        ]
        for b in range(TAPS):
            weight = [taps_b[h, pl.ds((a * TAPS + b) * 8, 8), :] for a in range(TAPS)]
            for ii in range(OUT_ROWS):
                cells = [
                    d_conv[h, pl.ds(base + (ii * DC_PITCH + 8 * (v + 1) - b), 8), :]
                    for v in range(2)
                ]
                for a in range(TAPS):
                    for v in range(2):
                        acc[ii + a][v] += cells[v] * weight[a]
        lanes = rows(h * LANES, LANES)
        out = pl.multiple_of(blk * BLOCK, BLOCK)
        for rr in range(OUT_ROWS + TAPS - 1):
            row = jnp.concatenate(acc[rr], axis=0)
            high = row.astype(BF16)
            d_pad_hi[pl.ds(out + rr * 16, 16), lanes] = high
            d_pad_lo[pl.ds(out + rr * 16, 16), lanes] = (row - high.astype(F32)).astype(
                BF16
            )
        return 0

    lax.fori_loop(0, 4 * HALVES, back_block, 0)
    rim = []
    for slot, peer in enumerate((before, ahead)):
        rim_send[slot] = dot(spread[pl.ds(slot * PIX, PIX), :], d_pad_hi[...]).astype(
            BF16
        )
        rim.append(send(rim_send.at[slot], rim_recv.at[slot], peer))

    k1.wait_recv()
    kc[...] = kb[rows(core * k_half, k_half), :] + kr[...]
    k2 = [
        send(kc.at[rows(xs[d - 1] * k_rows, k_rows)], kr_x.at[d - 1], x_peers[d - 1])
        for d in range(1, nx)
    ]

    norm = 1.0 / math.sqrt(PIX * tiles_n * nzhi * ny * 2)
    for copy in third:
        copy.wait_recv()
    place_y = y * nq + q
    place_x = x * nq + q
    got_a = t1[rows(place_y * last, last), :]
    for n in range(len(yq_peers)):
        got_a = got_a + r2[pl.ds(n * last, last), :].astype(F32)
    got_b = t1[rows(x_rows + place_x * last, last), :]
    for n in range(len(xq_peers)):
        got_b = got_b + r2[pl.ds(r2_x + n * last, last), :].astype(F32)
    zs[group, pl.ds(0, last), :] = got_a.astype(BF16)
    zs[group, pl.ds(last, last), :] = got_b.astype(BF16)
    fourth = [send(zs.at[group], zs.at[group], peer) for peer in far_peers]

    own = spread[pl.ds(OWN, PIX), :]
    own_grad[...] = dot(own, d_pad_hi[...]) + dot(own, d_pad_lo[...])
    for copy in k2:
        copy.wait_recv()
    k_sum = kc[rows(x * k_rows, k_rows), :]
    for d in range(1, nx):
        k_sum = k_sum + kr_x[d - 1]
    k_q[place_y] = k_sum
    k3 = [send(k_q.at[place_y], k_q.at[place_y], peer) for peer, _ in yq_peers]

    for copy in fourth:
        copy.wait_recv()
    total = zs[0].astype(F32)
    for n in range(1, ns):
        total = total + zs[n].astype(F32)
    total = (total * norm).astype(BF16)
    core_base = core * HALF_ROWS
    b_base = core_base + HALF_ROWS // 2
    place_a = rows(core_base + x * x_rows + place_y * last, last)
    place_b = rows(b_base + y * y_rows + place_x * last, last)
    full[place_a, :] = total[:last]
    full[place_b, :] = total[last:]
    fifth_a = [send(full.at[place_a], full.at[place_a], peer) for peer, _ in yq_peers]
    fifth_b = [send(full.at[place_b], full.at[place_b], peer) for peer, _ in xq_peers]

    for copy in k3:
        copy.wait_recv()
    k_sum = k_q[0]
    for n in range(1, ny * nq):
        k_sum = k_sum + k_q[n]
    k_s[group] = k_sum
    k4 = [send(k_s.at[group], k_s.at[group], peer) for peer in far_peers]

    block_a = rows(core_base + x * x_rows, x_rows)
    block_b = rows(b_base + y * y_rows, y_rows)
    for copy in fifth_a:
        copy.wait_recv()
    seventh_a = [send(full.at[block_a], full.at[block_a], peer) for peer in x_peers]
    for copy in fifth_b:
        copy.wait_recv()
    seventh_b = [send(full.at[block_b], full.at[block_b], peer) for peer in y_peers]
    eighth = [send(full.at[block], full.at[block], sibling) for block in (block_a, block_b)]

    for copy in rim:
        copy.wait_recv()
    gf_ref[...] = (
        cot_ref[...].astype(F32)
        + own_grad[...]
        + rim_recv[0].astype(F32)
        + rim_recv[1].astype(F32)
    ).astype(BF16)

    for copy in k4:
        copy.wait_recv()
    k_sum = k_s[0]
    for n in range(1, ns):
        k_sum = k_sum + k_s[n]
    k_place = rows(core * k_half + x * k_rows, k_rows)
    k_all[k_place, :] = k_sum * norm
    k5 = [send(k_all.at[k_place], k_all.at[k_place], peer) for peer in x_peers]
    for copy in k5:
        copy.wait_recv()
    k_mine = rows(core * k_half, k_half)
    k6 = send(k_all.at[k_mine], k_all.at[k_mine], sibling)

    for d, copy in sorted(zip(x_steps, seventh_a), key=lambda pair: -x_steps.index(pair[0])):
        copy.wait_recv()
        block = rows(core_base + lax.rem(x + nx - d, nx) * x_rows, x_rows)
        eighth.append(send(full.at[block], full.at[block], sibling))
    for d, copy in sorted(zip(y_steps, seventh_b), key=lambda pair: -y_steps.index(pair[0])):
        copy.wait_recv()
        block = rows(b_base + lax.rem(y + ny - d, ny) * y_rows, y_rows)
        eighth.append(send(full.at[block], full.at[block], sibling))

    k6.wait_recv()
    for h in range(HALVES):
        gk_ref[:, pl.ds(h * LANES, LANES)] = k_all[pl.ds(h * 64, TAPS * TAPS), :]
    for copy in eighth:
        copy.wait_recv()
    for copy in started:
        copy.wait_send()


def unpack_body(gf_in, gk_in, full, gf_ref, gk_ref, gwi_ref, gwo_ref, gwi, gwo, sem):
    copies = [
        pltpu.make_async_copy(gf_in, gf_ref, sem.at[0]),
        pltpu.make_async_copy(gk_in, gk_ref, sem.at[1]),
    ]
    for copy in copies:
        copy.start()
    for n in range(CHUNKS):
        for h in range(HALVES):
            j = HALVES * n + h
            gwi[pl.ds(0, C), pl.ds(j * LANES, LANES)] = full[pl.ds(j * C, C), :].astype(F32)
            gwo[pl.ds(n * CHUNK, CHUNK), pl.ds(h * LANES, LANES)] = full[
                pl.ds(HALF_ROWS + j * CHUNK, CHUNK), :
            ].astype(F32)
        for m, (src, dst) in enumerate(
            (
                (gwo.at[pl.ds(n * CHUNK, CHUNK)], gwo_ref.at[pl.ds(n * CHUNK, CHUNK)]),
                (
                    gwi.at[pl.ds(0, C), pl.ds(n * CHUNK, CHUNK)],
                    gwi_ref.at[pl.ds(0, C), pl.ds(n * CHUNK, CHUNK)],
                ),
            )
        ):
            copy = pltpu.make_async_copy(src, dst, sem.at[2 + 2 * n + m])
            copy.start()
            copies.append(copy)
    for copy in copies:
        copy.wait()


def body(sizes, features, cotangent, kernel, weight_in, weight_out, near, code):
    nx, nzlo, nzhi, ny, nq = sizes
    ns = nzlo * nzhi // nq
    x_rows = HALF_ROWS // 2 // nx
    y_rows = HALF_ROWS // 2 // ny
    last = HALF_ROWS // 2 // (nx * ny * nq)
    k_half = KROWS // 2
    k_rows = k_half // nx
    in_group = nx * nq - 1 + ny * nq - 1
    copies = 24 + 6 * (nx + ny) + 2 * in_group + ny * nq + 2 * ns
    vmem = pl.BlockSpec(memory_space=pltpu.VMEM)
    hbm = pl.BlockSpec(memory_space=pl.ANY)
    big = pl.BlockSpec(memory_space=pltpu.HBM)
    gf, gk, full = pl.pallas_call(
        functools.partial(kernel_body, sizes),
        out_shape=(
            jax.ShapeDtypeStruct((PIX, C), BF16),
            jax.ShapeDtypeStruct((TAPS * TAPS, C), F32),
            jax.ShapeDtypeStruct((2 * HALF_ROWS, LANES), BF16),
        ),
        in_specs=[big] * 7,
        out_specs=(vmem, vmem, vmem),
        scratch_shapes=[
            pltpu.SMEM((1, 4), jnp.int32),
            pltpu.SMEM((1, 4), jnp.int32),
            pltpu.VMEM((PIX, C), BF16),
            pltpu.VMEM((TAPS * TAPS, C), F32),
            pltpu.VMEM((C, HID), BF16),
            pltpu.VMEM((HID, C), BF16),
            pltpu.VMEM((3 * PIX, C), BF16),
            pltpu.VMEM((GRID, 3 * PIX), BF16),
            pltpu.VMEM((3 * PIX, GRID), BF16),
            pltpu.VMEM((HALVES, GRID, LANES), F32),
            pltpu.VMEM((HALVES, TAPS * TAPS * 8, LANES), F32),
            pltpu.VMEM((HALVES, PIX, LANES), F32),
            pltpu.VMEM((HALVES, PIX, LANES), F32),
            pltpu.VMEM((PIX, C), BF16),
            pltpu.VMEM((PIX, C), BF16),
            pltpu.VMEM((PIX, HID), F32),
            pltpu.VMEM((HALVES, PIX // 8 * DC_PITCH, LANES), F32),
            pltpu.VMEM((GRID, C), BF16),
            pltpu.VMEM((GRID, C), BF16),
            pltpu.VMEM((2, PIX, C), BF16),
            pltpu.VMEM((2, PIX, C), BF16),
            pltpu.VMEM((PIX, C), F32),
            pltpu.VMEM((HALVES, TAPS * TAPS * 8, LANES), F32),
            pltpu.VMEM((2, HALF_ROWS, LANES), F32),
            pltpu.VMEM((2, HALF_ROWS, LANES), BF16),
            pltpu.VMEM((HALF_ROWS, LANES), BF16),
            pltpu.VMEM((HALF_ROWS, LANES), F32),
            pltpu.VMEM((HALF_ROWS, LANES), BF16),
            pltpu.VMEM((max(1, nx - 1) * x_rows + max(1, ny - 1) * y_rows, LANES), BF16),
            pltpu.VMEM((x_rows + y_rows, LANES), F32),
            pltpu.VMEM((x_rows + y_rows, LANES), BF16),
            pltpu.VMEM((in_group * last, LANES), BF16),
            pltpu.VMEM((ns, 2 * last, LANES), BF16),
            pltpu.VMEM((KROWS, LANES), F32),
            pltpu.VMEM((k_half, LANES), F32),
            pltpu.VMEM((k_half, LANES), F32),
            pltpu.VMEM((max(1, nx - 1), k_rows, LANES), F32),
            pltpu.VMEM((ny * nq, k_rows, LANES), F32),
            pltpu.VMEM((ns, k_rows, LANES), F32),
            pltpu.VMEM((KROWS, LANES), F32),
            pltpu.SemaphoreType.DMA((7,)),
            pltpu.SemaphoreType.DMA((copies,)),
            pltpu.SemaphoreType.DMA((copies,)),
        ],
        compiler_params=pltpu.CompilerParams(
            collective_id=0, has_side_effects=True, vmem_limit_bytes=40 << 20
        ),
        name="block_step",
    )(
        *(
            pltpu.with_memory_space_constraint(v, pltpu.HBM)
            for v in (
                near,
                code,
                features.reshape(PIX, C),
                cotangent.reshape(PIX, C),
                kernel,
                weight_in,
                weight_out,
            )
        ),
    )
    gf, gk, gwi, gwo = pl.pallas_call(
        unpack_body,
        out_shape=(
            jax.ShapeDtypeStruct((PIX, C), BF16),
            jax.ShapeDtypeStruct((TAPS * TAPS, C), F32),
            jax.ShapeDtypeStruct((C, HID), F32),
            jax.ShapeDtypeStruct((HID, C), F32),
        ),
        in_specs=[vmem, vmem, vmem],
        out_specs=(hbm, hbm, hbm, hbm),
        scratch_shapes=[
            pltpu.VMEM((C, HID), F32),
            pltpu.VMEM((HID, C), F32),
            pltpu.SemaphoreType.DMA((2 + 2 * CHUNKS,)),
        ],
        compiler_params=pltpu.CompilerParams(vmem_limit_bytes=12 << 20),
        name="unpack",
    )(gf, gk, full)
    return gf.reshape(1, 1, TILE, TILE, C), gk, gwi, gwo


def solution(mesh):
    sizes = FACTORS[(mesh.shape["tile"], mesh.shape["ens"])]
    in_specs = (
        P("ens", "tile", None, None, None),
        P("ens", "tile", None, None, None),
        P(),
        P(),
        P(),
        P("tile", None),
        P("tile", None),
    )
    out_specs = (P("ens", "tile", None, None, None), P(), P(), P())
    return jax.shard_map(
        functools.partial(body, sizes),
        mesh=mesh,
        in_specs=in_specs,
        out_specs=out_specs,
        check_vma=False,
    )
```

```python
import functools
import math

import jax
import jax.numpy as jnp
from jax import lax
from jax.experimental import pallas as pl
from jax.experimental.pallas import tpu as pltpu
from jax.sharding import PartitionSpec as P

C = 256
HID = 1024
TAPS = 7
HALO = 6
TILE = 16
PIX = TILE * TILE
LANES = 128
HALVES = C // LANES
OWN = 2 * PIX
BLOCK = 16 * 16
GRID = 4 * BLOCK
OUT_ROWS = 8
DC_PITCH = 24
CHUNK = 256
CHUNKS = HID // CHUNK
HALF_ROWS = C * HID // LANES
KROWS = 128
F32 = jnp.float32
BF16 = jnp.bfloat16
FACTORS = {(32, 16): (4, 8, 2, 4, 4), (4, 4): (1, 4, 1, 2, 2), (8, 2): (2, 4, 1, 1, 2)}


def source_pixels(index, offset, step_k, step_m):
    r = 2 * ((index >> 4) & 15) + (index >> 9) - HALO
    c = 2 * (index & 15) + ((index >> 8) & 1) - HALO
    r_in = (r >= 0) & (r < TILE)
    c_in = (c >= 0) & (c < TILE)
    found = jnp.where(r_in & c_in, OWN + TILE * r + c, -1)
    sides = (
        (c_in & (r < 0), -1 - r, c),
        (c_in & (r >= TILE) & (r < TILE + HALO), r - TILE, c),
        (r_in & (c < 0), -1 - c, r),
        (r_in & (c >= TILE) & (c < TILE + HALO), c - TILE, r),
    )
    for s, (mask, depth, along) in enumerate(sides):
        found = jnp.where(mask, offset[s] + step_k[s] * depth + step_m[s] * along, found)
    return found


def far_first(n):
    return sorted(range(1, n), key=lambda d: -min(d, n - d))


def dot(a, b, contract=((1,), (0,))):
    return lax.dot_general(a, b, (contract, ((), ())), preferred_element_type=F32)


def kernel_body(
    sizes,
    near_hbm,
    code_hbm,
    x_hbm,
    cot_hbm,
    taps_hbm,
    w_in_hbm,
    w_out_hbm,
    gf_ref,
    gk_ref,
    gwi_ref,
    gwo_ref,
    near_ref,
    code_ref,
    cot_ref,
    taps_ref,
    w_in_ref,
    w_out_ref,
    tiles,
    gather,
    spread,
    padded,
    taps_b,
    conv,
    normed_f,
    normed_b,
    cot_p,
    d_hidden,
    d_conv,
    d_pad_hi,
    d_pad_lo,
    rim_send,
    rim_recv,
    own_grad,
    tap_acc,
    part,
    part_b,
    r0,
    half,
    s1,
    r1,
    t1,
    s2,
    r2,
    zs,
    kb,
    kr,
    kc,
    kr_x,
    k_q,
    k_s,
    k_all,
    full,
    local_sem,
    send_sem,
    recv_sem,
):
    nx, nzlo, nzhi, ny, nq = sizes
    nz = nzlo * nzhi
    ns = nz // nq
    tiles_n = nzlo * nx
    me_t = lax.axis_index("tile")
    me_e = lax.axis_index("ens")
    x = lax.rem(me_t, nx)
    zlo = lax.div(me_t, nx)
    core = lax.rem(me_e, 2)
    y = lax.rem(lax.div(me_e, 2), ny)
    zhi = lax.div(me_e, 2 * ny)
    z = zhi * nzlo + zlo
    q = lax.rem(z, nq)
    group = lax.div(z, nq)

    def at(tile, ens):
        return {"tile": tile, "ens": ens}

    def chip(x_at, y_at, z_at):
        return at(
            lax.rem(z_at, nzlo) * nx + x_at, (lax.div(z_at, nzlo) * ny + y_at) * 2 + core
        )

    before = at(lax.rem(me_t + tiles_n - 1, tiles_n), me_e)
    ahead = at(lax.rem(me_t + 1, tiles_n), me_e)
    sibling = at(me_t, me_e + 1 - 2 * core)
    x_steps, y_steps, far_steps = far_first(nx), far_first(ny), far_first(ns)
    xs = [lax.rem(x + d, nx) for d in x_steps]
    ys = [lax.rem(y + d, ny) for d in y_steps]
    x_peers = [chip(v, y, z) for v in xs]
    y_peers = [chip(x, v, z) for v in ys]
    yq_peers, xq_peers, only_q = [], [], []
    for d in range(max(nx, ny)):
        for dq in range(nq):
            if d == 0 and dq == 0:
                continue
            qv = lax.rem(q + dq, nq)
            if d < ny:
                yv = lax.rem(y + d, ny)
                yq_peers.append((chip(x, yv, group * nq + qv), yv * nq + qv, (d, dq, ny)))
            if 0 < d < nx or d == 0:
                xv = lax.rem(x + d, nx)
                xq_peers.append((chip(xv, y, group * nq + qv), xv * nq + qv, (d, dq, nx)))
            if d == 0:
                only_q.append(yq_peers[-1][0])
    far_peers = [chip(x, y, lax.rem(z + d * nq, nz)) for d in far_steps]
    peers = [before, ahead, sibling, *far_peers, *only_q]
    peers += [pair[0] for pair in yq_peers[nq - 1 :] + xq_peers[nq - 1 :]]

    def reach(pair):
        d, dq, n = pair[2]
        return -min(d, n - d) - min(dq, nq - dq)

    yq_peers = [pair[:2] for pair in sorted(yq_peers, key=reach)]
    xq_peers = [pair[:2] for pair in sorted(xq_peers, key=reach)]

    barrier = pltpu.get_barrier_semaphore()
    for peer in peers:
        pl.semaphore_signal(
            barrier, inc=1, device_id=peer, device_id_type=pl.DeviceIdType.MESH
        )
    loads = [
        pltpu.make_async_copy(src, dst, local_sem.at[n])
        for n, (src, dst) in enumerate(
            (
                (x_hbm, tiles.at[pl.ds(OWN, PIX)]),
                (near_hbm, near_ref),
                (code_hbm, code_ref),
                (cot_hbm, cot_ref),
                (w_out_hbm, w_out_ref),
                (taps_hbm, taps_ref),
                (w_in_hbm, w_in_ref),
            )
        )
    ]
    for load in loads:
        load.start()
    loads[0].wait()
    pl.semaphore_wait(barrier, len(peers))

    started = []

    def send(src, dst, peer):
        n = len(started)
        copy = pltpu.make_async_remote_copy(
            src_ref=src,
            dst_ref=dst,
            send_sem=send_sem.at[n],
            recv_sem=recv_sem.at[n],
            device_id=peer,
            device_id_type=pl.DeviceIdType.MESH,
        )
        copy.start()
        started.append(copy)
        return copy

    def rows(start, size):
        return pl.ds(pl.multiple_of(start, size), size)

    halo = [
        send(tiles.at[pl.ds(OWN, PIX)], tiles.at[pl.ds(PIX, PIX)], before),
        send(tiles.at[pl.ds(OWN, PIX)], tiles.at[pl.ds(0, PIX)], ahead),
    ]

    for load in loads[1:]:
        load.wait()
    offset, step_k, step_m = [], [], []
    for s in range(4):
        code = code_ref[0, s]
        slot = lax.rem(2 * lax.rem(near_ref[0, s] - me_t + (tiles_n + 1), tiles_n), 3)
        edge = lax.rem(code, 4)
        flip = lax.div(code, 4)
        along_rows = lax.div(edge, 2)
        far = lax.rem(edge, 2)
        mult_k = TILE - (TILE - 1) * along_rows
        mult_m = 1 + (TILE - 1) * along_rows
        offset.append(slot * PIX + (TILE - 1) * (mult_k * far + mult_m * flip))
        step_k.append(mult_k * (1 - 2 * far))
        step_m.append(mult_m * (1 - 2 * flip))

    def one_hot(mask):
        return jnp.where(mask, 1.0, 0.0).astype(BF16)

    def fill_gather(i, _):
        cells = i * LANES + lax.broadcasted_iota(jnp.int32, (LANES, 1), 0)
        found = source_pixels(cells, offset, step_k, step_m)
        pixel = lax.broadcasted_iota(jnp.int32, (LANES, 3 * PIX), 1)
        gather[rows(i * LANES, LANES), :] = one_hot(found == pixel)
        return 0

    lax.fori_loop(0, GRID // LANES, fill_gather, 0)
    cells_row = lax.broadcasted_iota(jnp.int32, (1, GRID), 1)
    found_row = source_pixels(cells_row, offset, step_k, step_m)

    def fill_spread(i, _):
        pixel = i * 64 + lax.broadcasted_iota(jnp.int32, (64, GRID), 0)
        spread[rows(i * 64, 64), :] = one_hot(pixel == found_row)
        return 0

    lax.fori_loop(0, 3 * PIX // 64, fill_spread, 0)

    order = lax.broadcasted_iota(jnp.int32, (PIX, 1), 0)
    natural = (2 * ((order >> 3) & 7) + (order >> 7)) * TILE + 2 * (order & 7) + (
        (order >> 6) & 1
    )
    reorder = one_hot(natural == lax.broadcasted_iota(jnp.int32, (PIX, PIX), 1))
    cot_p[...] = dot(reorder, cot_ref[...]).astype(BF16)
    for n in range(CHUNKS):
        cols = pl.ds(n * CHUNK, CHUNK)
        d_hidden[:, cols] = dot(cot_p[...], w_out_ref[cols, :], ((1,), (1,)))
    for h in range(HALVES):
        lanes = pl.ds(h * LANES, LANES)
        for tap in range(TAPS * TAPS):
            taps_b[h, pl.ds(tap * 8, 8), :] = jnp.broadcast_to(
                taps_ref[pl.ds(tap, 1), lanes], (8, LANES)
            )
    d_conv[...] = jnp.zeros_like(d_conv)
    d_pad_hi[...] = jnp.zeros_like(d_pad_hi)
    d_pad_lo[...] = jnp.zeros_like(d_pad_lo)
    tap_acc[...] = jnp.zeros_like(tap_acc)
    kb[...] = jnp.zeros_like(kb)

    inner = [
        dot(gather[pl.ds(i * BLOCK, BLOCK), pl.ds(OWN, PIX)], tiles[pl.ds(OWN, PIX), :])
        for i in range(4)
    ]
    for i in range(4):
        for h in range(HALVES):
            padded[h, pl.ds(i * BLOCK, BLOCK), :] = inner[i][:, h * LANES : (h + 1) * LANES]

    for copy in halo:
        copy.wait_recv()
    for i in range(4):
        got = dot(gather[pl.ds(i * BLOCK, BLOCK), pl.ds(0, OWN)], tiles[pl.ds(0, OWN), :])
        for h in range(HALVES):
            padded[h, pl.ds(i * BLOCK, BLOCK), :] += got[:, h * LANES : (h + 1) * LANES]

    def conv_block(i, _):
        h, blk = lax.div(i, 4), lax.rem(i, 4)
        base = pl.multiple_of(blk * BLOCK, BLOCK)
        acc = [jnp.zeros((8, LANES), F32) for _ in range(OUT_ROWS)]
        for b in range(TAPS):
            weight = [taps_b[h, pl.ds((a * TAPS + b) * 8, 8), :] for a in range(TAPS)]
            for rr in range(OUT_ROWS + TAPS - 1):
                cell = padded[h, pl.ds(base + (rr * 16 + b), 8), :]
                for a in range(TAPS):
                    if 0 <= rr - a < OUT_ROWS:
                        acc[rr - a] += cell * weight[a]
        out = pl.multiple_of(blk * 64, 64)
        for ii in range(OUT_ROWS):
            conv[h, pl.ds(out + ii * 8, 8), :] = acc[ii]
        return 0

    lax.fori_loop(0, 4 * HALVES, conv_block, 0)

    c0, c1 = conv[0], conv[1]
    mean = jnp.sum(c0 + c1, axis=-1, keepdims=True) * (1.0 / C)
    c0, c1 = c0 - mean, c1 - mean
    var = jnp.sum(c0 * c0 + c1 * c1, axis=-1, keepdims=True) * (1.0 / C)
    inv_std = lax.rsqrt(var + 1e-06)
    for h, centred in enumerate((c0, c1)):
        scaled = centred * inv_std
        normed_f[h] = scaled
        normed_b[:, pl.ds(h * LANES, LANES)] = scaled.astype(BF16)

    x_rows = HALF_ROWS // 2 // nx
    y_rows = HALF_ROWS // 2 // ny
    last = HALF_ROWS // 2 // (nx * ny * nq)
    r1_y = (nx - 1) * x_rows

    def chip_sum(n):
        first[n].wait_recv()
        place = pl.ds(HALVES * n * CHUNK, HALVES * CHUNK)
        total = part[core, place, :] + r0[place, :].astype(F32)
        half[place, :] = total
        s1[place, :] = total.astype(BF16)

    root = math.sqrt(2.0 / math.pi)
    first = []
    d_normed = jnp.zeros((PIX, C), F32)
    for n in range(CHUNKS):
        cols = pl.ds(n * CHUNK, CHUNK)
        pre = dot(normed_b[...], w_in_ref[:, cols])
        square = pre * pre
        bent = jnp.tanh(root * pre * (1.0 + 0.044715 * square))
        up = 0.5 * (1.0 + bent)
        hidden = (pre * up).astype(BF16)
        slope = up + 0.5 * pre * (1.0 - bent * bent) * (
            root * (1.0 + 3 * 0.044715 * square)
        )
        d_pre = (d_hidden[:, cols] * slope).astype(BF16)
        got_in = dot(normed_b[...], d_pre, ((0,), (0,)))
        got_out = dot(hidden, cot_p[...], ((0,), (0,)))
        for side, got in enumerate((got_in, got_out)):
            for h in range(HALVES):
                piece = got[:, h * LANES : (h + 1) * LANES]
                place = pl.ds((HALVES * n + h) * CHUNK, CHUNK)
                part[side, place, :] = piece
                part_b[side, place, :] = piece.astype(BF16)
        place = pl.ds(HALVES * n * CHUNK, HALVES * CHUNK)
        first.append(send(part_b.at[1 - core, place], r0.at[place], sibling))
        d_normed = d_normed + dot(d_pre, w_in_ref[:, cols], ((1,), (1,)))
    for m in range(CHUNKS // 2):
        chip_sum(m)
    second_a = [
        send(
            s1.at[rows(xs[d - 1] * x_rows, x_rows)],
            r1.at[pl.ds((d - 1) * x_rows, x_rows)],
            x_peers[d - 1],
        )
        for d in range(1, nx)
    ]

    n0, n1 = normed_f[0], normed_f[1]
    d0, d1 = d_normed[:, :LANES], d_normed[:, LANES:]
    mean_d = jnp.sum(d0 + d1, axis=-1, keepdims=True) * (1.0 / C)
    mean_dn = jnp.sum(d0 * n0 + d1 * n1, axis=-1, keepdims=True) * (1.0 / C)
    for h, (d_half, n_half) in enumerate(((d0, n0), (d1, n1))):
        got = inv_std * (d_half - mean_d - n_half * mean_dn)
        for row in range(PIX // 8):
            d_conv[h, pl.ds(row * DC_PITCH + 8, 8), :] = got[row * 8 : row * 8 + 8]

    for m in range(CHUNKS // 2, CHUNKS):
        chip_sum(m)
    second_b = [
        send(
            s1.at[rows(HALF_ROWS // 2 + ys[d - 1] * y_rows, y_rows)],
            r1.at[pl.ds(r1_y + (d - 1) * y_rows, y_rows)],
            y_peers[d - 1],
        )
        for d in range(1, ny)
    ]

    def tap_block(i, _):
        h, blk = lax.div(i, 4), lax.rem(i, 4)
        base = pl.multiple_of(blk * BLOCK, BLOCK)
        dc_base = pl.multiple_of(blk * (OUT_ROWS * DC_PITCH), 8)
        grads = [
            d_conv[h, pl.ds(dc_base + (ii * DC_PITCH + 8), 8), :] for ii in range(OUT_ROWS)
        ]
        for b in range(TAPS):
            acc = [tap_acc[h, pl.ds((a * TAPS + b) * 8, 8), :] for a in range(TAPS)]
            for rr in range(OUT_ROWS + TAPS - 1):
                cell = padded[h, pl.ds(base + (rr * 16 + b), 8), :]
                for a in range(TAPS):
                    if 0 <= rr - a < OUT_ROWS:
                        acc[a] += cell * grads[rr - a]
            for a in range(TAPS):
                tap_acc[h, pl.ds((a * TAPS + b) * 8, 8), :] = acc[a]
        return 0

    lax.fori_loop(0, 4 * HALVES, tap_block, 0)
    for h in range(HALVES):
        kb[pl.ds(h * 64, TAPS * TAPS), :] = jnp.sum(
            tap_acc[h].reshape(TAPS * TAPS, 8, LANES), axis=1
        )
    k_half = KROWS // 2
    k_rows = k_half // nx
    k1 = send(kb.at[rows((1 - core) * k_half, k_half)], kr, sibling)

    for copy in second_a:
        copy.wait_recv()
    got_a = half[rows(x * x_rows, x_rows), :]
    for d in range(1, nx):
        got_a = got_a + r1[pl.ds((d - 1) * x_rows, x_rows), :].astype(F32)
    t1[pl.ds(0, x_rows), :] = got_a
    s2[pl.ds(0, x_rows), :] = got_a.astype(BF16)
    third = [
        send(s2.at[rows(place * last, last)], r2.at[pl.ds(n * last, last)], peer)
        for n, (peer, place) in enumerate(yq_peers)
    ]
    for copy in second_b:
        copy.wait_recv()
    got_b = half[rows(HALF_ROWS // 2 + y * y_rows, y_rows), :]
    for d in range(1, ny):
        got_b = got_b + r1[pl.ds(r1_y + (d - 1) * y_rows, y_rows), :].astype(F32)
    t1[pl.ds(x_rows, y_rows), :] = got_b
    s2[pl.ds(x_rows, y_rows), :] = got_b.astype(BF16)
    r2_x = len(yq_peers) * last
    third += [
        send(
            s2.at[rows(x_rows + place * last, last)],
            r2.at[pl.ds(r2_x + n * last, last)],
            peer,
        )
        for n, (peer, place) in enumerate(xq_peers)
    ]

    def back_block(i, _):
        h, blk = lax.div(i, 4), lax.rem(i, 4)
        base = pl.multiple_of(blk * (OUT_ROWS * DC_PITCH), 8)
        acc = [
            [jnp.zeros((8, LANES), F32) for _ in range(2)]
            for _ in range(OUT_ROWS + TAPS - 1)
        ]
        for b in range(TAPS):
            weight = [taps_b[h, pl.ds((a * TAPS + b) * 8, 8), :] for a in range(TAPS)]
            for ii in range(OUT_ROWS):
                cells = [
                    d_conv[h, pl.ds(base + (ii * DC_PITCH + 8 * (v + 1) - b), 8), :]
                    for v in range(2)
                ]
                for a in range(TAPS):
                    for v in range(2):
                        acc[ii + a][v] += cells[v] * weight[a]
        lanes = rows(h * LANES, LANES)
        out = pl.multiple_of(blk * BLOCK, BLOCK)
        for rr in range(OUT_ROWS + TAPS - 1):
            row = jnp.concatenate(acc[rr], axis=0)
            high = row.astype(BF16)
            d_pad_hi[pl.ds(out + rr * 16, 16), lanes] = high
            d_pad_lo[pl.ds(out + rr * 16, 16), lanes] = (row - high.astype(F32)).astype(
                BF16
            )
        return 0

    lax.fori_loop(0, 4 * HALVES, back_block, 0)
    rim = []
    for slot, peer in enumerate((before, ahead)):
        rim_send[slot] = dot(spread[pl.ds(slot * PIX, PIX), :], d_pad_hi[...]).astype(
            BF16
        )
        rim.append(send(rim_send.at[slot], rim_recv.at[slot], peer))

    k1.wait_recv()
    kc[...] = kb[rows(core * k_half, k_half), :] + kr[...]
    k2 = [
        send(kc.at[rows(xs[d - 1] * k_rows, k_rows)], kr_x.at[d - 1], x_peers[d - 1])
        for d in range(1, nx)
    ]

    norm = 1.0 / math.sqrt(PIX * tiles_n * nzhi * ny * 2)
    for copy in third:
        copy.wait_recv()
    place_y = y * nq + q
    place_x = x * nq + q
    got_a = t1[rows(place_y * last, last), :]
    for n in range(len(yq_peers)):
        got_a = got_a + r2[pl.ds(n * last, last), :].astype(F32)
    got_b = t1[rows(x_rows + place_x * last, last), :]
    for n in range(len(xq_peers)):
        got_b = got_b + r2[pl.ds(r2_x + n * last, last), :].astype(F32)
    zs[group, pl.ds(0, last), :] = got_a.astype(BF16)
    zs[group, pl.ds(last, last), :] = got_b.astype(BF16)
    fourth = [send(zs.at[group], zs.at[group], peer) for peer in far_peers]

    own = spread[pl.ds(OWN, PIX), :]
    own_grad[...] = dot(own, d_pad_hi[...]) + dot(own, d_pad_lo[...])
    for copy in k2:
        copy.wait_recv()
    k_sum = kc[rows(x * k_rows, k_rows), :]
    for d in range(1, nx):
        k_sum = k_sum + kr_x[d - 1]
    k_q[place_y] = k_sum
    k3 = [send(k_q.at[place_y], k_q.at[place_y], peer) for peer, _ in yq_peers]

    for copy in fourth:
        copy.wait_recv()
    total = zs[0].astype(F32)
    for n in range(1, ns):
        total = total + zs[n].astype(F32)
    total = (total * norm).astype(BF16)
    core_base = core * HALF_ROWS
    b_base = core_base + HALF_ROWS // 2
    place_a = rows(core_base + x * x_rows + place_y * last, last)
    place_b = rows(b_base + y * y_rows + place_x * last, last)
    full[place_a, :] = total[:last]
    full[place_b, :] = total[last:]
    fifth_a = [send(full.at[place_a], full.at[place_a], peer) for peer, _ in yq_peers]
    fifth_b = [send(full.at[place_b], full.at[place_b], peer) for peer, _ in xq_peers]

    for copy in k3:
        copy.wait_recv()
    k_sum = k_q[0]
    for n in range(1, ny * nq):
        k_sum = k_sum + k_q[n]
    k_s[group] = k_sum
    k4 = [send(k_s.at[group], k_s.at[group], peer) for peer in far_peers]

    block_a = rows(core_base + x * x_rows, x_rows)
    block_b = rows(b_base + y * y_rows, y_rows)
    for copy in fifth_a:
        copy.wait_recv()
    seventh_a = [send(full.at[block_a], full.at[block_a], peer) for peer in x_peers]
    for copy in fifth_b:
        copy.wait_recv()
    seventh_b = [send(full.at[block_b], full.at[block_b], peer) for peer in y_peers]
    eighth = [send(full.at[block], full.at[block], sibling) for block in (block_a, block_b)]

    for copy in rim:
        copy.wait_recv()
    gf_ref[...] = (
        cot_ref[...].astype(F32)
        + own_grad[...]
        + rim_recv[0].astype(F32)
        + rim_recv[1].astype(F32)
    ).astype(BF16)

    for copy in k4:
        copy.wait_recv()
    k_sum = k_s[0]
    for n in range(1, ns):
        k_sum = k_sum + k_s[n]
    k_place = rows(core * k_half + x * k_rows, k_rows)
    k_all[k_place, :] = k_sum * norm
    k5 = [send(k_all.at[k_place], k_all.at[k_place], peer) for peer in x_peers]
    for copy in k5:
        copy.wait_recv()
    k_mine = rows(core * k_half, k_half)
    k6 = send(k_all.at[k_mine], k_all.at[k_mine], sibling)

    for d, copy in sorted(zip(x_steps, seventh_a), key=lambda pair: -x_steps.index(pair[0])):
        copy.wait_recv()
        block = rows(core_base + lax.rem(x + nx - d, nx) * x_rows, x_rows)
        eighth.append(send(full.at[block], full.at[block], sibling))
    for d, copy in sorted(zip(y_steps, seventh_b), key=lambda pair: -y_steps.index(pair[0])):
        copy.wait_recv()
        block = rows(b_base + lax.rem(y + ny - d, ny) * y_rows, y_rows)
        eighth.append(send(full.at[block], full.at[block], sibling))

    k6.wait_recv()
    for h in range(HALVES):
        gk_ref[:, pl.ds(h * LANES, LANES)] = k_all[pl.ds(h * 64, TAPS * TAPS), :]
    for copy in eighth:
        copy.wait_recv()
    for n in range(CHUNKS):
        for h in range(HALVES):
            j = HALVES * n + h
            gwi_ref[:, pl.ds(j * LANES, LANES)] = full[pl.ds(j * C, C), :].astype(F32)
            gwo_ref[pl.ds(n * CHUNK, CHUNK), pl.ds(h * LANES, LANES)] = full[
                pl.ds(HALF_ROWS + j * CHUNK, CHUNK), :
            ].astype(F32)
    for copy in started:
        copy.wait_send()


def store_body(*refs):
    ins, outs, sem = refs[:4], refs[4:8], refs[8]
    pairs = [(ins[0], outs[0]), (ins[1], outs[1])]
    for src, dst in zip(ins[2:], outs[2:]):
        size = src.shape[0] // 4
        pairs += [
            (src.at[pl.ds(n * size, size)], dst.at[pl.ds(n * size, size)]) for n in range(4)
        ]
    copies = [
        pltpu.make_async_copy(src, dst, sem.at[n]) for n, (src, dst) in enumerate(pairs)
    ]
    for copy in copies:
        copy.start()
    for copy in copies:
        copy.wait()


def body(sizes, features, cotangent, kernel, weight_in, weight_out, near, code):
    nx, nzlo, nzhi, ny, nq = sizes
    ns = nzlo * nzhi // nq
    x_rows = HALF_ROWS // 2 // nx
    y_rows = HALF_ROWS // 2 // ny
    last = HALF_ROWS // 2 // (nx * ny * nq)
    k_half = KROWS // 2
    k_rows = k_half // nx
    in_group = nx * nq - 1 + ny * nq - 1
    copies = 24 + 6 * (nx + ny) + 2 * in_group + ny * nq + 2 * ns
    vmem = pl.BlockSpec(memory_space=pltpu.VMEM)
    hbm = pl.BlockSpec(memory_space=pl.ANY)
    big = pl.BlockSpec(memory_space=pltpu.HBM)
    made = pl.pallas_call(
        functools.partial(kernel_body, sizes),
        out_shape=(
            jax.ShapeDtypeStruct((PIX, C), BF16),
            jax.ShapeDtypeStruct((TAPS * TAPS, C), F32),
            jax.ShapeDtypeStruct((C, HID), F32),
            jax.ShapeDtypeStruct((HID, C), F32),
        ),
        in_specs=[big] * 7,
        out_specs=(vmem, vmem, vmem, vmem),
        scratch_shapes=[
            pltpu.SMEM((1, 4), jnp.int32),
            pltpu.SMEM((1, 4), jnp.int32),
            pltpu.VMEM((PIX, C), BF16),
            pltpu.VMEM((TAPS * TAPS, C), F32),
            pltpu.VMEM((C, HID), BF16),
            pltpu.VMEM((HID, C), BF16),
            pltpu.VMEM((3 * PIX, C), BF16),
            pltpu.VMEM((GRID, 3 * PIX), BF16),
            pltpu.VMEM((3 * PIX, GRID), BF16),
            pltpu.VMEM((HALVES, GRID, LANES), F32),
            pltpu.VMEM((HALVES, TAPS * TAPS * 8, LANES), F32),
            pltpu.VMEM((HALVES, PIX, LANES), F32),
            pltpu.VMEM((HALVES, PIX, LANES), F32),
            pltpu.VMEM((PIX, C), BF16),
            pltpu.VMEM((PIX, C), BF16),
            pltpu.VMEM((PIX, HID), F32),
            pltpu.VMEM((HALVES, PIX // 8 * DC_PITCH, LANES), F32),
            pltpu.VMEM((GRID, C), BF16),
            pltpu.VMEM((GRID, C), BF16),
            pltpu.VMEM((2, PIX, C), BF16),
            pltpu.VMEM((2, PIX, C), BF16),
            pltpu.VMEM((PIX, C), F32),
            pltpu.VMEM((HALVES, TAPS * TAPS * 8, LANES), F32),
            pltpu.VMEM((2, HALF_ROWS, LANES), F32),
            pltpu.VMEM((2, HALF_ROWS, LANES), BF16),
            pltpu.VMEM((HALF_ROWS, LANES), BF16),
            pltpu.VMEM((HALF_ROWS, LANES), F32),
            pltpu.VMEM((HALF_ROWS, LANES), BF16),
            pltpu.VMEM((max(1, nx - 1) * x_rows + max(1, ny - 1) * y_rows, LANES), BF16),
            pltpu.VMEM((x_rows + y_rows, LANES), F32),
            pltpu.VMEM((x_rows + y_rows, LANES), BF16),
            pltpu.VMEM((in_group * last, LANES), BF16),
            pltpu.VMEM((ns, 2 * last, LANES), BF16),
            pltpu.VMEM((KROWS, LANES), F32),
            pltpu.VMEM((k_half, LANES), F32),
            pltpu.VMEM((k_half, LANES), F32),
            pltpu.VMEM((max(1, nx - 1), k_rows, LANES), F32),
            pltpu.VMEM((ny * nq, k_rows, LANES), F32),
            pltpu.VMEM((ns, k_rows, LANES), F32),
            pltpu.VMEM((KROWS, LANES), F32),
            pltpu.VMEM((2 * HALF_ROWS, LANES), BF16),
            pltpu.SemaphoreType.DMA((7,)),
            pltpu.SemaphoreType.DMA((copies,)),
            pltpu.SemaphoreType.DMA((copies,)),
        ],
        compiler_params=pltpu.CompilerParams(
            collective_id=0, has_side_effects=True, vmem_limit_bytes=40 << 20
        ),
        name="block_step",
    )(
        *(
            pltpu.with_memory_space_constraint(v, pltpu.HBM)
            for v in (
                near,
                code,
                features.reshape(PIX, C),
                cotangent.reshape(PIX, C),
                kernel,
                weight_in,
                weight_out,
            )
        ),
    )
    gf, gk, gwi, gwo = pl.pallas_call(
        store_body,
        out_shape=tuple(jax.ShapeDtypeStruct(v.shape, v.dtype) for v in made),
        in_specs=[vmem] * 4,
        out_specs=(hbm,) * 4,
        scratch_shapes=[pltpu.SemaphoreType.DMA((10,))],
        compiler_params=pltpu.CompilerParams(vmem_limit_bytes=4 << 20),
        name="store",
    )(*made)
    return gf.reshape(1, 1, TILE, TILE, C), gk, gwi, gwo


def solution(mesh):
    sizes = FACTORS[(mesh.shape["tile"], mesh.shape["ens"])]
    in_specs = (
        P("ens", "tile", None, None, None),
        P("ens", "tile", None, None, None),
        P(),
        P(),
        P(),
        P("tile", None),
        P("tile", None),
    )
    out_specs = (P("ens", "tile", None, None, None), P(), P(), P())
    return jax.shard_map(
        functools.partial(body, sizes),
        mesh=mesh,
        in_specs=in_specs,
        out_specs=out_specs,
        check_vma=False,
    )
```

```python
import functools
import math

import jax
import jax.numpy as jnp
from jax import lax
from jax.experimental import pallas as pl
from jax.experimental.pallas import tpu as pltpu
from jax.sharding import PartitionSpec as P

C = 256
HID = 1024
TAPS = 7
HALO = 6
TILE = 16
PIX = TILE * TILE
LANES = 128
HALVES = C // LANES
OWN = 2 * PIX
BLOCK = 16 * 16
GRID = 4 * BLOCK
OUT_ROWS = 8
DC_PITCH = 24
CHUNK = 256
CHUNKS = HID // CHUNK
HALF_ROWS = C * HID // LANES
KROWS = 128
F32 = jnp.float32
BF16 = jnp.bfloat16
FACTORS = {(32, 16): (4, 8, 2, 4, 4), (4, 4): (1, 4, 1, 2, 2), (8, 2): (2, 4, 1, 1, 2)}


def source_pixels(index, offset, step_k, step_m):
    r = 2 * ((index >> 4) & 15) + (index >> 9) - HALO
    c = 2 * (index & 15) + ((index >> 8) & 1) - HALO
    r_in = (r >= 0) & (r < TILE)
    c_in = (c >= 0) & (c < TILE)
    found = jnp.where(r_in & c_in, OWN + TILE * r + c, -1)
    sides = (
        (c_in & (r < 0), -1 - r, c),
        (c_in & (r >= TILE) & (r < TILE + HALO), r - TILE, c),
        (r_in & (c < 0), -1 - c, r),
        (r_in & (c >= TILE) & (c < TILE + HALO), c - TILE, r),
    )
    for s, (mask, depth, along) in enumerate(sides):
        found = jnp.where(mask, offset[s] + step_k[s] * depth + step_m[s] * along, found)
    return found


def far_first(n):
    return sorted(range(1, n), key=lambda d: -min(d, n - d))


def dot(a, b, contract=((1,), (0,))):
    return lax.dot_general(a, b, (contract, ((), ())), preferred_element_type=F32)


def kernel_body(
    sizes,
    near_hbm,
    code_hbm,
    x_hbm,
    cot_hbm,
    taps_hbm,
    w_in_hbm,
    w_out_hbm,
    gf_ref,
    gk_ref,
    gwi_ref,
    gwo_ref,
    near_ref,
    code_ref,
    cot_ref,
    taps_ref,
    w_in_ref,
    w_out_ref,
    tiles,
    gather,
    spread,
    padded,
    taps_b,
    conv,
    normed_f,
    normed_b,
    cot_p,
    d_hidden,
    d_conv,
    d_pad_hi,
    d_pad_lo,
    rim_send,
    rim_recv,
    own_grad,
    tap_acc,
    part,
    part_b,
    r0,
    s1,
    r1,
    t1,
    s2,
    r2,
    zs,
    kb,
    kr,
    kc,
    kr_x,
    k_q,
    k_s,
    k_all,
    full,
    local_sem,
    send_sem,
    recv_sem,
):
    nx, nzlo, nzhi, ny, nq = sizes
    nz = nzlo * nzhi
    ns = nz // nq
    tiles_n = nzlo * nx
    me_t = lax.axis_index("tile")
    me_e = lax.axis_index("ens")
    x = lax.rem(me_t, nx)
    zlo = lax.div(me_t, nx)
    core = lax.rem(me_e, 2)
    y = lax.rem(lax.div(me_e, 2), ny)
    zhi = lax.div(me_e, 2 * ny)
    z = zhi * nzlo + zlo
    q = lax.rem(z, nq)
    group = lax.div(z, nq)

    def at(tile, ens):
        return {"tile": tile, "ens": ens}

    def chip(x_at, y_at, z_at):
        return at(
            lax.rem(z_at, nzlo) * nx + x_at, (lax.div(z_at, nzlo) * ny + y_at) * 2 + core
        )

    before = at(lax.rem(me_t + tiles_n - 1, tiles_n), me_e)
    ahead = at(lax.rem(me_t + 1, tiles_n), me_e)
    sibling = at(me_t, me_e + 1 - 2 * core)
    x_steps, y_steps, far_steps = far_first(nx), far_first(ny), far_first(ns)
    xs = [lax.rem(x + d, nx) for d in x_steps]
    ys = [lax.rem(y + d, ny) for d in y_steps]
    x_peers = [chip(v, y, z) for v in xs]
    y_peers = [chip(x, v, z) for v in ys]
    yq_peers, xq_peers, only_q = [], [], []
    for d in range(max(nx, ny)):
        for dq in range(nq):
            if d == 0 and dq == 0:
                continue
            qv = lax.rem(q + dq, nq)
            if d < ny:
                yv = lax.rem(y + d, ny)
                yq_peers.append((chip(x, yv, group * nq + qv), yv * nq + qv, (d, dq, ny)))
            if 0 < d < nx or d == 0:
                xv = lax.rem(x + d, nx)
                xq_peers.append((chip(xv, y, group * nq + qv), xv * nq + qv, (d, dq, nx)))
            if d == 0:
                only_q.append(yq_peers[-1][0])
    far_peers = [chip(x, y, lax.rem(z + d * nq, nz)) for d in far_steps]
    peers = [before, ahead, sibling, *far_peers, *only_q]
    peers += [pair[0] for pair in yq_peers[nq - 1 :] + xq_peers[nq - 1 :]]

    def reach(pair):
        d, dq, n = pair[2]
        return -min(d, n - d) - min(dq, nq - dq)

    yq_peers = [pair[:2] for pair in sorted(yq_peers, key=reach)]
    xq_peers = [pair[:2] for pair in sorted(xq_peers, key=reach)]

    barrier = pltpu.get_barrier_semaphore()
    for peer in peers:
        pl.semaphore_signal(
            barrier, inc=1, device_id=peer, device_id_type=pl.DeviceIdType.MESH
        )
    loads = [
        pltpu.make_async_copy(src, dst, local_sem.at[n])
        for n, (src, dst) in enumerate(
            (
                (x_hbm, tiles.at[pl.ds(OWN, PIX)]),
                (near_hbm, near_ref),
                (code_hbm, code_ref),
                (cot_hbm, cot_ref),
                (w_out_hbm, w_out_ref),
                (taps_hbm, taps_ref),
                (w_in_hbm, w_in_ref),
            )
        )
    ]
    for load in loads:
        load.start()
    loads[0].wait()
    pl.semaphore_wait(barrier, len(peers))

    started = []

    def send(src, dst, peer):
        n = len(started)
        copy = pltpu.make_async_remote_copy(
            src_ref=src,
            dst_ref=dst,
            send_sem=send_sem.at[n],
            recv_sem=recv_sem.at[n],
            device_id=peer,
            device_id_type=pl.DeviceIdType.MESH,
        )
        copy.start()
        started.append(copy)
        return copy

    def rows(start, size):
        return pl.ds(pl.multiple_of(start, size), size)

    halo = [
        send(tiles.at[pl.ds(OWN, PIX)], tiles.at[pl.ds(PIX, PIX)], before),
        send(tiles.at[pl.ds(OWN, PIX)], tiles.at[pl.ds(0, PIX)], ahead),
    ]

    for load in loads[1:]:
        load.wait()
    offset, step_k, step_m = [], [], []
    for s in range(4):
        code = code_ref[0, s]
        slot = lax.rem(2 * lax.rem(near_ref[0, s] - me_t + (tiles_n + 1), tiles_n), 3)
        edge = lax.rem(code, 4)
        flip = lax.div(code, 4)
        along_rows = lax.div(edge, 2)
        far = lax.rem(edge, 2)
        mult_k = TILE - (TILE - 1) * along_rows
        mult_m = 1 + (TILE - 1) * along_rows
        offset.append(slot * PIX + (TILE - 1) * (mult_k * far + mult_m * flip))
        step_k.append(mult_k * (1 - 2 * far))
        step_m.append(mult_m * (1 - 2 * flip))

    def one_hot(mask):
        return jnp.where(mask, 1.0, 0.0).astype(BF16)

    def fill_gather(i, _):
        cells = i * LANES + lax.broadcasted_iota(jnp.int32, (LANES, 1), 0)
        found = source_pixels(cells, offset, step_k, step_m)
        pixel = lax.broadcasted_iota(jnp.int32, (LANES, 3 * PIX), 1)
        gather[rows(i * LANES, LANES), :] = one_hot(found == pixel)
        return 0

    lax.fori_loop(0, GRID // LANES, fill_gather, 0)
    cells_row = lax.broadcasted_iota(jnp.int32, (1, GRID), 1)
    found_row = source_pixels(cells_row, offset, step_k, step_m)

    def fill_spread(i, _):
        pixel = i * 64 + lax.broadcasted_iota(jnp.int32, (64, GRID), 0)
        spread[rows(i * 64, 64), :] = one_hot(pixel == found_row)
        return 0

    lax.fori_loop(0, 3 * PIX // 64, fill_spread, 0)

    order = lax.broadcasted_iota(jnp.int32, (PIX, 1), 0)
    natural = (2 * ((order >> 3) & 7) + (order >> 7)) * TILE + 2 * (order & 7) + (
        (order >> 6) & 1
    )
    reorder = one_hot(natural == lax.broadcasted_iota(jnp.int32, (PIX, PIX), 1))
    cot_p[...] = dot(reorder, cot_ref[...]).astype(BF16)
    for n in range(CHUNKS):
        cols = pl.ds(n * CHUNK, CHUNK)
        d_hidden[:, cols] = dot(cot_p[...], w_out_ref[cols, :], ((1,), (1,)))
    for h in range(HALVES):
        lanes = pl.ds(h * LANES, LANES)
        for tap in range(TAPS * TAPS):
            taps_b[h, pl.ds(tap * 8, 8), :] = jnp.broadcast_to(
                taps_ref[pl.ds(tap, 1), lanes], (8, LANES)
            )
    d_conv[...] = jnp.zeros_like(d_conv)
    d_pad_hi[...] = jnp.zeros_like(d_pad_hi)
    d_pad_lo[...] = jnp.zeros_like(d_pad_lo)
    tap_acc[...] = jnp.zeros_like(tap_acc)
    kb[...] = jnp.zeros_like(kb)

    inner = [
        dot(gather[pl.ds(i * BLOCK, BLOCK), pl.ds(OWN, PIX)], tiles[pl.ds(OWN, PIX), :])
        for i in range(4)
    ]
    for i in range(4):
        for h in range(HALVES):
            padded[h, pl.ds(i * BLOCK, BLOCK), :] = inner[i][:, h * LANES : (h + 1) * LANES]

    for copy in halo:
        copy.wait_recv()
    for i in range(4):
        got = dot(gather[pl.ds(i * BLOCK, BLOCK), pl.ds(0, OWN)], tiles[pl.ds(0, OWN), :])
        for h in range(HALVES):
            padded[h, pl.ds(i * BLOCK, BLOCK), :] += got[:, h * LANES : (h + 1) * LANES]

    def conv_block(i, _):
        h, blk = lax.div(i, 4), lax.rem(i, 4)
        base = pl.multiple_of(blk * BLOCK, BLOCK)
        acc = [jnp.zeros((8, LANES), F32) for _ in range(OUT_ROWS)]
        for b in range(TAPS):
            weight = [taps_b[h, pl.ds((a * TAPS + b) * 8, 8), :] for a in range(TAPS)]
            for rr in range(OUT_ROWS + TAPS - 1):
                cell = padded[h, pl.ds(base + (rr * 16 + b), 8), :]
                for a in range(TAPS):
                    if 0 <= rr - a < OUT_ROWS:
                        acc[rr - a] += cell * weight[a]
        out = pl.multiple_of(blk * 64, 64)
        for ii in range(OUT_ROWS):
            conv[h, pl.ds(out + ii * 8, 8), :] = acc[ii]
        return 0

    lax.fori_loop(0, 4 * HALVES, conv_block, 0)

    c0, c1 = conv[0], conv[1]
    mean = jnp.sum(c0 + c1, axis=-1, keepdims=True) * (1.0 / C)
    c0, c1 = c0 - mean, c1 - mean
    var = jnp.sum(c0 * c0 + c1 * c1, axis=-1, keepdims=True) * (1.0 / C)
    inv_std = lax.rsqrt(var + 1e-06)
    for h, centred in enumerate((c0, c1)):
        scaled = centred * inv_std
        normed_f[h] = scaled
        normed_b[:, pl.ds(h * LANES, LANES)] = scaled.astype(BF16)

    x_rows = HALF_ROWS // 2 // nx
    y_rows = HALF_ROWS // 2 // ny
    last = HALF_ROWS // 2 // (nx * ny * nq)
    r1_y = (nx - 1) * x_rows

    def chip_sum(n):
        first[n].wait_recv()
        place = pl.ds(HALVES * n * CHUNK, HALVES * CHUNK)
        total = part[core, place, :] + r0[place, :].astype(F32)
        s1[place, :] = total.astype(BF16)

    def own_block(start, size):
        place = rows(start, size)
        return part[core, place, :] + r0[place, :].astype(F32)

    root = math.sqrt(2.0 / math.pi)
    first = []
    d_normed = jnp.zeros((PIX, C), F32)
    for n in range(CHUNKS):
        cols = pl.ds(n * CHUNK, CHUNK)
        pre = dot(normed_b[...], w_in_ref[:, cols])
        square = pre * pre
        bent = jnp.tanh(root * pre * (1.0 + 0.044715 * square))
        up = 0.5 * (1.0 + bent)
        hidden = (pre * up).astype(BF16)
        slope = up + 0.5 * pre * (1.0 - bent * bent) * (
            root * (1.0 + 3 * 0.044715 * square)
        )
        d_pre = (d_hidden[:, cols] * slope).astype(BF16)
        got_in = dot(normed_b[...], d_pre, ((0,), (0,)))
        got_out = dot(hidden, cot_p[...], ((0,), (0,)))
        for side, got in enumerate((got_in, got_out)):
            for h in range(HALVES):
                piece = got[:, h * LANES : (h + 1) * LANES]
                place = pl.ds((HALVES * n + h) * CHUNK, CHUNK)
                part[side, place, :] = piece
                part_b[side, place, :] = piece.astype(BF16)
        place = pl.ds(HALVES * n * CHUNK, HALVES * CHUNK)
        first.append(send(part_b.at[1 - core, place], r0.at[place], sibling))
        d_normed = d_normed + dot(d_pre, w_in_ref[:, cols], ((1,), (1,)))
    for m in range(CHUNKS // 2):
        chip_sum(m)
    second_a = [
        send(
            s1.at[rows(xs[d - 1] * x_rows, x_rows)],
            r1.at[pl.ds((d - 1) * x_rows, x_rows)],
            x_peers[d - 1],
        )
        for d in range(1, nx)
    ]

    n0, n1 = normed_f[0], normed_f[1]
    d0, d1 = d_normed[:, :LANES], d_normed[:, LANES:]
    mean_d = jnp.sum(d0 + d1, axis=-1, keepdims=True) * (1.0 / C)
    mean_dn = jnp.sum(d0 * n0 + d1 * n1, axis=-1, keepdims=True) * (1.0 / C)
    for h, (d_half, n_half) in enumerate(((d0, n0), (d1, n1))):
        got = inv_std * (d_half - mean_d - n_half * mean_dn)
        for row in range(PIX // 8):
            d_conv[h, pl.ds(row * DC_PITCH + 8, 8), :] = got[row * 8 : row * 8 + 8]

    for m in range(CHUNKS // 2, CHUNKS):
        chip_sum(m)
    second_b = [
        send(
            s1.at[rows(HALF_ROWS // 2 + ys[d - 1] * y_rows, y_rows)],
            r1.at[pl.ds(r1_y + (d - 1) * y_rows, y_rows)],
            y_peers[d - 1],
        )
        for d in range(1, ny)
    ]

    def tap_block(i, _):
        h, blk = lax.div(i, 4), lax.rem(i, 4)
        base = pl.multiple_of(blk * BLOCK, BLOCK)
        dc_base = pl.multiple_of(blk * (OUT_ROWS * DC_PITCH), 8)
        grads = [
            d_conv[h, pl.ds(dc_base + (ii * DC_PITCH + 8), 8), :] for ii in range(OUT_ROWS)
        ]
        for b in range(TAPS):
            acc = [tap_acc[h, pl.ds((a * TAPS + b) * 8, 8), :] for a in range(TAPS)]
            for rr in range(OUT_ROWS + TAPS - 1):
                cell = padded[h, pl.ds(base + (rr * 16 + b), 8), :]
                for a in range(TAPS):
                    if 0 <= rr - a < OUT_ROWS:
                        acc[a] += cell * grads[rr - a]
            for a in range(TAPS):
                tap_acc[h, pl.ds((a * TAPS + b) * 8, 8), :] = acc[a]
        return 0

    lax.fori_loop(0, 4 * HALVES, tap_block, 0)
    for h in range(HALVES):
        kb[pl.ds(h * 64, TAPS * TAPS), :] = jnp.sum(
            tap_acc[h].reshape(TAPS * TAPS, 8, LANES), axis=1
        )
    k_half = KROWS // 2
    k_rows = k_half // nx
    k1 = send(kb.at[rows((1 - core) * k_half, k_half)], kr, sibling)

    for copy in second_a:
        copy.wait_recv()
    got_a = own_block(x * x_rows, x_rows)
    for d in range(1, nx):
        got_a = got_a + r1[pl.ds((d - 1) * x_rows, x_rows), :].astype(F32)
    t1[pl.ds(0, x_rows), :] = got_a
    s2[pl.ds(0, x_rows), :] = got_a.astype(BF16)
    third = [
        send(s2.at[rows(place * last, last)], r2.at[pl.ds(n * last, last)], peer)
        for n, (peer, place) in enumerate(yq_peers)
    ]
    for copy in second_b:
        copy.wait_recv()
    got_b = own_block(HALF_ROWS // 2 + y * y_rows, y_rows)
    for d in range(1, ny):
        got_b = got_b + r1[pl.ds(r1_y + (d - 1) * y_rows, y_rows), :].astype(F32)
    t1[pl.ds(x_rows, y_rows), :] = got_b
    s2[pl.ds(x_rows, y_rows), :] = got_b.astype(BF16)
    r2_x = len(yq_peers) * last
    third += [
        send(
            s2.at[rows(x_rows + place * last, last)],
            r2.at[pl.ds(r2_x + n * last, last)],
            peer,
        )
        for n, (peer, place) in enumerate(xq_peers)
    ]

    def back_block(i, _):
        h, blk = lax.div(i, 4), lax.rem(i, 4)
        base = pl.multiple_of(blk * (OUT_ROWS * DC_PITCH), 8)
        acc = [
            [jnp.zeros((8, LANES), F32) for _ in range(2)]
            for _ in range(OUT_ROWS + TAPS - 1)
        ]
        for b in range(TAPS):
            weight = [taps_b[h, pl.ds((a * TAPS + b) * 8, 8), :] for a in range(TAPS)]
            for ii in range(OUT_ROWS):
                cells = [
                    d_conv[h, pl.ds(base + (ii * DC_PITCH + 8 * (v + 1) - b), 8), :]
                    for v in range(2)
                ]
                for a in range(TAPS):
                    for v in range(2):
                        acc[ii + a][v] += cells[v] * weight[a]
        lanes = rows(h * LANES, LANES)
        out = pl.multiple_of(blk * BLOCK, BLOCK)
        for rr in range(OUT_ROWS + TAPS - 1):
            row = jnp.concatenate(acc[rr], axis=0)
            high = row.astype(BF16)
            d_pad_hi[pl.ds(out + rr * 16, 16), lanes] = high
            d_pad_lo[pl.ds(out + rr * 16, 16), lanes] = (row - high.astype(F32)).astype(
                BF16
            )
        return 0

    lax.fori_loop(0, 4 * HALVES, back_block, 0)
    rim = []
    for slot, peer in enumerate((before, ahead)):
        rim_send[slot] = dot(spread[pl.ds(slot * PIX, PIX), :], d_pad_hi[...]).astype(
            BF16
        )
        rim.append(send(rim_send.at[slot], rim_recv.at[slot], peer))

    k1.wait_recv()
    kc[...] = kb[rows(core * k_half, k_half), :] + kr[...]
    k2 = [
        send(kc.at[rows(xs[d - 1] * k_rows, k_rows)], kr_x.at[d - 1], x_peers[d - 1])
        for d in range(1, nx)
    ]

    norm = 1.0 / math.sqrt(PIX * tiles_n * nzhi * ny * 2)
    for copy in third:
        copy.wait_recv()
    place_y = y * nq + q
    place_x = x * nq + q
    got_a = t1[rows(place_y * last, last), :]
    for n in range(len(yq_peers)):
        got_a = got_a + r2[pl.ds(n * last, last), :].astype(F32)
    got_b = t1[rows(x_rows + place_x * last, last), :]
    for n in range(len(xq_peers)):
        got_b = got_b + r2[pl.ds(r2_x + n * last, last), :].astype(F32)
    zs[group, pl.ds(0, last), :] = got_a.astype(BF16)
    zs[group, pl.ds(last, last), :] = got_b.astype(BF16)
    fourth = [send(zs.at[group], zs.at[group], peer) for peer in far_peers]

    own = spread[pl.ds(OWN, PIX), :]
    own_grad[...] = dot(own, d_pad_hi[...]) + dot(own, d_pad_lo[...])
    for copy in k2:
        copy.wait_recv()
    k_sum = kc[rows(x * k_rows, k_rows), :]
    for d in range(1, nx):
        k_sum = k_sum + kr_x[d - 1]
    k_q[place_y] = k_sum
    k3 = [send(k_q.at[place_y], k_q.at[place_y], peer) for peer, _ in yq_peers]

    for copy in fourth:
        copy.wait_recv()
    total = zs[0].astype(F32)
    for n in range(1, ns):
        total = total + zs[n].astype(F32)
    total = (total * norm).astype(BF16)
    core_base = core * HALF_ROWS
    b_base = core_base + HALF_ROWS // 2
    place_a = rows(core_base + x * x_rows + place_y * last, last)
    place_b = rows(b_base + y * y_rows + place_x * last, last)
    full[place_a, :] = total[:last]
    full[place_b, :] = total[last:]
    fifth_a = [send(full.at[place_a], full.at[place_a], peer) for peer, _ in yq_peers]
    fifth_b = [send(full.at[place_b], full.at[place_b], peer) for peer, _ in xq_peers]

    for copy in k3:
        copy.wait_recv()
    k_sum = k_q[0]
    for n in range(1, ny * nq):
        k_sum = k_sum + k_q[n]
    k_s[group] = k_sum
    k4 = [send(k_s.at[group], k_s.at[group], peer) for peer in far_peers]

    block_a = rows(core_base + x * x_rows, x_rows)
    block_b = rows(b_base + y * y_rows, y_rows)
    for copy in fifth_a:
        copy.wait_recv()
    seventh_a = [send(full.at[block_a], full.at[block_a], peer) for peer in x_peers]
    for copy in fifth_b:
        copy.wait_recv()
    seventh_b = [send(full.at[block_b], full.at[block_b], peer) for peer in y_peers]
    eighth = [send(full.at[block], full.at[block], sibling) for block in (block_a, block_b)]

    for copy in rim:
        copy.wait_recv()
    gf_ref[...] = (
        cot_ref[...].astype(F32)
        + own_grad[...]
        + rim_recv[0].astype(F32)
        + rim_recv[1].astype(F32)
    ).astype(BF16)

    for copy in k4:
        copy.wait_recv()
    k_sum = k_s[0]
    for n in range(1, ns):
        k_sum = k_sum + k_s[n]
    k_place = rows(core * k_half + x * k_rows, k_rows)
    k_all[k_place, :] = k_sum * norm
    k5 = [send(k_all.at[k_place], k_all.at[k_place], peer) for peer in x_peers]
    for copy in k5:
        copy.wait_recv()
    k_mine = rows(core * k_half, k_half)
    k6 = send(k_all.at[k_mine], k_all.at[k_mine], sibling)

    for d, copy in sorted(zip(x_steps, seventh_a), key=lambda pair: -x_steps.index(pair[0])):
        copy.wait_recv()
        block = rows(core_base + lax.rem(x + nx - d, nx) * x_rows, x_rows)
        eighth.append(send(full.at[block], full.at[block], sibling))
    for d, copy in sorted(zip(y_steps, seventh_b), key=lambda pair: -y_steps.index(pair[0])):
        copy.wait_recv()
        block = rows(b_base + lax.rem(y + ny - d, ny) * y_rows, y_rows)
        eighth.append(send(full.at[block], full.at[block], sibling))

    k6.wait_recv()
    for h in range(HALVES):
        gk_ref[:, pl.ds(h * LANES, LANES)] = k_all[pl.ds(h * 64, TAPS * TAPS), :]
    def widen(side):
        for n in range(CHUNKS):
            for h in range(HALVES):
                j = HALVES * n + h
                piece = full[pl.ds(side * HALF_ROWS + j * C, C), :].astype(F32)
                if side == 0:
                    gwi_ref[:, pl.ds(j * LANES, LANES)] = piece
                else:
                    gwo_ref[pl.ds(n * CHUNK, CHUNK), pl.ds(h * LANES, LANES)] = piece

    for side in range(2):
        pl.when(core == side)(functools.partial(widen, side))
    for copy in eighth:
        copy.wait_recv()
    for side in range(2):
        pl.when(core != side)(functools.partial(widen, side))
    for copy in started:
        copy.wait_send()


def store_body(*refs):
    ins, outs, sem = refs[:4], refs[4:8], refs[8]
    pairs = [(ins[0], outs[0]), (ins[1], outs[1])]
    for src, dst in zip(ins[2:], outs[2:]):
        size = src.shape[0] // 4
        pairs += [
            (src.at[pl.ds(n * size, size)], dst.at[pl.ds(n * size, size)]) for n in range(4)
        ]
    copies = [
        pltpu.make_async_copy(src, dst, sem.at[n]) for n, (src, dst) in enumerate(pairs)
    ]
    for copy in copies:
        copy.start()
    for copy in copies:
        copy.wait()


def body(sizes, features, cotangent, kernel, weight_in, weight_out, near, code):
    nx, nzlo, nzhi, ny, nq = sizes
    ns = nzlo * nzhi // nq
    x_rows = HALF_ROWS // 2 // nx
    y_rows = HALF_ROWS // 2 // ny
    last = HALF_ROWS // 2 // (nx * ny * nq)
    k_half = KROWS // 2
    k_rows = k_half // nx
    in_group = nx * nq - 1 + ny * nq - 1
    copies = 24 + 6 * (nx + ny) + 2 * in_group + ny * nq + 2 * ns
    vmem = pl.BlockSpec(memory_space=pltpu.VMEM)
    hbm = pl.BlockSpec(memory_space=pl.ANY)
    big = pl.BlockSpec(memory_space=pltpu.HBM)
    made = pl.pallas_call(
        functools.partial(kernel_body, sizes),
        out_shape=(
            jax.ShapeDtypeStruct((PIX, C), BF16),
            jax.ShapeDtypeStruct((TAPS * TAPS, C), F32),
            jax.ShapeDtypeStruct((C, HID), F32),
            jax.ShapeDtypeStruct((HID, C), F32),
        ),
        in_specs=[big] * 7,
        out_specs=(vmem, vmem, vmem, vmem),
        scratch_shapes=[
            pltpu.SMEM((1, 4), jnp.int32),
            pltpu.SMEM((1, 4), jnp.int32),
            pltpu.VMEM((PIX, C), BF16),
            pltpu.VMEM((TAPS * TAPS, C), F32),
            pltpu.VMEM((C, HID), BF16),
            pltpu.VMEM((HID, C), BF16),
            pltpu.VMEM((3 * PIX, C), BF16),
            pltpu.VMEM((GRID, 3 * PIX), BF16),
            pltpu.VMEM((3 * PIX, GRID), BF16),
            pltpu.VMEM((HALVES, GRID, LANES), F32),
            pltpu.VMEM((HALVES, TAPS * TAPS * 8, LANES), F32),
            pltpu.VMEM((HALVES, PIX, LANES), F32),
            pltpu.VMEM((HALVES, PIX, LANES), F32),
            pltpu.VMEM((PIX, C), BF16),
            pltpu.VMEM((PIX, C), BF16),
            pltpu.VMEM((PIX, HID), F32),
            pltpu.VMEM((HALVES, PIX // 8 * DC_PITCH, LANES), F32),
            pltpu.VMEM((GRID, C), BF16),
            pltpu.VMEM((GRID, C), BF16),
            pltpu.VMEM((2, PIX, C), BF16),
            pltpu.VMEM((2, PIX, C), BF16),
            pltpu.VMEM((PIX, C), F32),
            pltpu.VMEM((HALVES, TAPS * TAPS * 8, LANES), F32),
            pltpu.VMEM((2, HALF_ROWS, LANES), F32),
            pltpu.VMEM((2, HALF_ROWS, LANES), BF16),
            pltpu.VMEM((HALF_ROWS, LANES), BF16),
            pltpu.VMEM((HALF_ROWS, LANES), BF16),
            pltpu.VMEM((max(1, nx - 1) * x_rows + max(1, ny - 1) * y_rows, LANES), BF16),
            pltpu.VMEM((x_rows + y_rows, LANES), F32),
            pltpu.VMEM((x_rows + y_rows, LANES), BF16),
            pltpu.VMEM((in_group * last, LANES), BF16),
            pltpu.VMEM((ns, 2 * last, LANES), BF16),
            pltpu.VMEM((KROWS, LANES), F32),
            pltpu.VMEM((k_half, LANES), F32),
            pltpu.VMEM((k_half, LANES), F32),
            pltpu.VMEM((max(1, nx - 1), k_rows, LANES), F32),
            pltpu.VMEM((ny * nq, k_rows, LANES), F32),
            pltpu.VMEM((ns, k_rows, LANES), F32),
            pltpu.VMEM((KROWS, LANES), F32),
            pltpu.VMEM((2 * HALF_ROWS, LANES), BF16),
            pltpu.SemaphoreType.DMA((7,)),
            pltpu.SemaphoreType.DMA((copies,)),
            pltpu.SemaphoreType.DMA((copies,)),
        ],
        compiler_params=pltpu.CompilerParams(
            collective_id=0, has_side_effects=True, vmem_limit_bytes=40 << 20
        ),
        name="block_step",
    )(
        *(
            pltpu.with_memory_space_constraint(v, pltpu.HBM)
            for v in (
                near,
                code,
                features.reshape(PIX, C),
                cotangent.reshape(PIX, C),
                kernel,
                weight_in,
                weight_out,
            )
        ),
    )
    gf, gk, gwi, gwo = pl.pallas_call(
        store_body,
        out_shape=tuple(jax.ShapeDtypeStruct(v.shape, v.dtype) for v in made),
        in_specs=[vmem] * 4,
        out_specs=(hbm,) * 4,
        scratch_shapes=[pltpu.SemaphoreType.DMA((10,))],
        compiler_params=pltpu.CompilerParams(vmem_limit_bytes=4 << 20),
        name="store",
    )(*made)
    return gf.reshape(1, 1, TILE, TILE, C), gk, gwi, gwo


def solution(mesh):
    sizes = FACTORS[(mesh.shape["tile"], mesh.shape["ens"])]
    in_specs = (
        P("ens", "tile", None, None, None),
        P("ens", "tile", None, None, None),
        P(),
        P(),
        P(),
        P("tile", None),
        P("tile", None),
    )
    out_specs = (P("ens", "tile", None, None, None), P(), P(), P())
    return jax.shard_map(
        functools.partial(body, sizes),
        mesh=mesh,
        in_specs=in_specs,
        out_specs=out_specs,
        check_vma=False,
    )
```
